256 devices in a mesh: cable: 4 (over y), fx: 32 (over z, x), fz: 2 (over core).
Axes of the slice: x: 4, y: 4, z: 8, core: 2. Of those that a mesh axis runs over, the one named last changes fastest.
Arguments:
- velocity: float32 [3, 256, 64, 256], P(None, 'fx', 'cable', 'fz'), may hold values from -6 to 6
- viscosity: float32 [256, 64, 256], P('fx', 'cable', 'fz'), may hold values from 0.02 to 0.15
- disp_init: float32 [3, 16384], P(None, ('cable', 'fx', 'fz')), may hold values from -3 to 3
- rest_shape: float32 [3, 16384], P(None, ('cable', 'fx', 'fz')), may hold values from -6 to 6
- compliance: float32 [16384], P(('cable', 'fx', 'fz')), may hold values from 0.5 to 2
- stencil_weights: float32 [3, 12, 16384], P(None, None, ('cable', 'fx', 'fz')), may hold values from 0.05 to 0.45
- anchor: int32 [3, 16384], P(None, ('cable', 'fx', 'fz')), may hold values from 0 to 9852, as said below
- owners: int32 [3, 16384], P(None, ('cable', 'fx', 'fz')), may hold values from 0 to 63, as said below
Outputs:
- disp_next: float32 [3, 16384], P(None, ('cable', 'fx', 'fz'))
- velocity_out: float32 [3, 256, 64, 256], P(None, 'fx', 'cable', 'fz')
The draws below stay inside these ranges and needn't reach their ends.
Inputs may be any that keep to these rules, and one draw needn't show every extreme that they name: `owners`: the owner's number is fx * 2 + fz of a fluid block in the segment's own cable group. Among the 64 segments of one device (aligned blocks of 64 segments), at most 4 name the same owner in one iteration; in every iteration one owner is named by exactly 4 segments of every device of each group. `anchor`: the cell is numbered (x * 16 + y) * 128 + z in the owner's block, with x <= 4, y <= 12 and z <= 124, so the 4 x 4 x 4 stencil lies inside that block.
All inputs are finite; a program needn't handle non-finite values.
Results may differ from the reference program's by a relative error of at most 0.0003.
Values sent between devices are 32-bit elements; how exact they have to be, the bound alone decides.
No kernel may reach another device: no remote copies, remote signals or barrier semaphores. Data moves between devices by JAX's collectives and lax.ppermute only.
A program may use at most 64 MiB of HBM per device.

```python
import math
import jax
import jax.numpy as jnp
from jax import lax

CX = 8
CY = 16
CZ = 128
SEG_DEV = 64
ITERS = 3
GROUP = 64
CAP = 4
SEG = 16384
NX = 256
NY = 64
NZ = 256
N_FZ = 2


def draw_owners(key, part):
    blocks = ITERS * SEG // SEG_DEV
    key_hot, key_perm, key_shift = jax.random.split(jax.random.fold_in(key, 11), 3)
    hottest = jax.random.randint(key_hot, (ITERS, 1), 0, GROUP)
    hottest = jnp.repeat(hottest, SEG // SEG_DEV, axis=1).reshape(blocks, 1)
    perm_keys = jax.random.split(key_perm, blocks)
    places = jax.vmap(lambda single: jax.random.permutation(single, SEG_DEV))(perm_keys)
    shifts = jax.random.randint(key_shift, (blocks, 1), 0, GROUP - 1)
    others = (hottest + 1 + (places - CAP + shifts) % (GROUP - 1)) % GROUP
    chosen = jnp.where(places < CAP, hottest, others)
    return chosen.reshape(ITERS, SEG).astype(jnp.int32)


def draw_anchor(key, part):
    key_x, key_y, key_z = jax.random.split(jax.random.fold_in(key, 23), 3)
    first_x = jax.random.randint(key_x, (ITERS, SEG), 0, CX - 3)
    first_y = jax.random.randint(key_y, (ITERS, SEG), 0, CY - 3)
    first_z = jax.random.randint(key_z, (ITERS, SEG), 0, CZ - 3)
    return ((first_x * CY + first_y) * CZ + first_z).astype(jnp.int32)


def steps_of(key, extent, cuts, smallest, largest):
    factor_of = 1.0
    for dim, shards_of in cuts:
        draws = jax.random.uniform(jax.random.fold_in(jax.random.fold_in(key, 6), dim), (shards_of,), jnp.float32, smallest / len(cuts), largest / len(cuts))
        factor_of = factor_of * jnp.repeat(jnp.exp(draws), extent[dim] // shards_of).reshape((-1,) + (1,) * (len(extent) - 1 - dim))
    return factor_of


def normal_values(stream_key, dims, deviation, most, shards=(), kind=jnp.bfloat16):
    gain = steps_of(stream_key, dims, shards, -0.22, 0.18) if shards else 1.0
    result = jax.random.normal(stream_key, dims, jnp.float32) * deviation * gain
    return jnp.minimum(jnp.maximum(result, -most), most).astype(kind)


def setup_inputs(seed: int = 0) -> dict:
    splits = jax.random.split(jax.random.key(seed), 9)
    return {
        "velocity": normal_values(splits[0], (3, NX, NY, NZ), 1.0, 6.0, ((1, 32), (2, 4), (3, 2)), jnp.float32),
        "viscosity": jnp.clip(jnp.exp(math.log(0.15) - 2.014903 * jax.random.uniform(splits[1], (NX, NY, NZ), jnp.float32) ** steps_of(splits[1], (NX, NY, NZ), ((0, 32), (1, 4), (2, 2)), -0.2, 0.2)), 0.02, 0.15),
        "disp_init": normal_values(splits[2], (3, SEG), 0.5, 3.0, ((1, 256),), jnp.float32),
        "rest_shape": normal_values(splits[3], (3, SEG), 1.0, 6.0, ((1, 256),), jnp.float32),
        "compliance": jnp.clip(jnp.exp(math.log(2.0) - 1.3862944 * jax.random.uniform(splits[4], (SEG,), jnp.float32) ** steps_of(splits[4], (SEG,), ((0, 256),), -0.2, 0.2)), 0.5, 2.0),
        "stencil_weights": jnp.clip(0.05 + 0.39999999 * jax.random.uniform(splits[5], (ITERS, 12, SEG), jnp.float32) ** steps_of(splits[5], (ITERS, 12, SEG), ((2, 256),), -0.2, 0.2), 0.05, 0.45),
        "anchor": draw_anchor(jax.random.fold_in(splits[8], 71), 0),
        "owners": draw_owners(jax.random.fold_in(splits[8], 71), 0),
    }


spread_gain = 16.0
drag_coeff = 0.05
relaxation = 0.5
ridge_share = 0.01

def stencil_table(weights):
    table = weights[0:4][:, None, None, :] * weights[4:8][None, :, None, :] * weights[8:12][None, None, :, :]
    return table.reshape(64, weights.shape[1])

def neighbours(field):
    padded = jnp.pad(field, ((0, 0), (1, 1), (1, 1), (1, 1)))
    beside = padded[:, 2:, 1:-1, 1:-1] + padded[:, :-2, 1:-1, 1:-1]
    beside = beside + padded[:, 1:-1, 2:, 1:-1] + padded[:, 1:-1, :-2, 1:-1]
    beside = beside + padded[:, 1:-1, 1:-1, 2:] + padded[:, 1:-1, 1:-1, :-2]
    return beside

def evaluate(velocity, viscosity, disp, weights, anchor_now, owner_now, rest_shape, compliance):
    seg_total = disp.shape[1]
    seg_index = jnp.arange(seg_total, dtype=jnp.int32)
    column = seg_index // (SEG_DEV * GROUP)
    first_x = owner_now // N_FZ * CX + anchor_now // (CY * CZ)
    first_y = column * CY + anchor_now // CZ % CY
    first_z = owner_now % N_FZ * CZ + anchor_now % CZ
    corner = ((first_x * NY + first_y) * NZ + first_z).astype(jnp.int32)
    steps_one = jnp.arange(4, dtype=jnp.int32)
    offsets = ((steps_one[:, None, None] * NY + steps_one[None, :, None]) * NZ + steps_one[None, None, :]).reshape(64)
    cell_index = (corner[None, :] + offsets[:, None]).astype(jnp.int32)
    stencil = stencil_table(weights)
    spread_terms = spread_gain * stencil[None] * disp[:, None, :]
    cells = NX * NY * NZ
    forcing = jnp.zeros((3, cells), jnp.float32).at[:, cell_index.reshape(-1)].add(spread_terms.reshape(3, -1))
    u_star = velocity + forcing.reshape(velocity.shape)
    laplace = neighbours(u_star) - 6.0 * u_star
    speed = jnp.sqrt(1.0 + lax.optimization_barrier(jnp.sum(u_star * u_star, axis=0, keepdims=True)))
    u_new = u_star + viscosity[None] * laplace - drag_coeff * u_star * speed
    picked = u_new.reshape(3, cells)[:, cell_index]
    sampled = lax.optimization_barrier(jnp.sum(stencil[None] * picked, axis=1))
    tension_ramp = 1.0 + 2.0 * seg_index.astype(jnp.float32) / seg_total
    response = rest_shape + compliance[None] * tension_ramp[None] * sampled
    return (response, u_new)

def solve_small(gram, width):
    square = gram[:width, :width]
    target = gram[:width, width]
    shift = ridge_share * jnp.trace(square) / width + 1e-06
    if width == 1:
        return [-target[0] / (square[0, 0] + shift)]
    first = square[0, 0] + shift
    second = square[1, 1] + shift
    cross = square[0, 1]
    determinant = first * second - cross * cross
    return [-(second * target[0] - cross * target[1]) / determinant, -(first * target[1] - cross * target[0]) / determinant]

def reference(velocity, viscosity, disp_init, rest_shape, compliance, stencil_weights, anchor, owners):
    current = disp_init
    residuals = []
    responses = []
    velocity_out = velocity
    for iteration in range(ITERS):
        response, velocity_out = evaluate(velocity, viscosity, current, stencil_weights[iteration], anchor[iteration], owners[iteration], rest_shape, compliance)
        residual = response - current
        if iteration == 0:
            following = current + relaxation * residual
        else:
            columns = [residual - earlier for earlier in residuals]
            changes = [response - earlier for earlier in responses]
            matrix = jnp.stack(columns + [residual]).reshape(iteration + 1, -1)
            gram = jnp.dot(matrix, matrix.T, precision=lax.Precision.HIGHEST)
            coefs = solve_small(gram, iteration)
            following = response
            for column in range(iteration):
                following = following + coefs[column] * changes[column]
        residuals.append(residual)
        responses.append(response)
        current = following
    return (current, velocity_out)
```

```python
import functools

import jax
import jax.numpy as jnp
from jax import lax
from jax.experimental import pallas as pl
from jax.experimental.pallas import tpu as pltpu
from jax.sharding import PartitionSpec as P

F32 = jnp.float32
BF16 = jnp.bfloat16
NT = (((1,), (1,)), ((), ()))
NN = (((1,), (0,)), ((), ()))
EXACT = lax.Precision.HIGHEST

spread_gain = 16.0
drag_coeff = 0.05
relaxation = 0.5
ridge_share = 0.01

SEG_DEV = 64
GROUP = 64
CAP = 4
SLOTS = GROUP * CAP
SX, SY, SZ = 8, 16, 128
XY = SX * SY

R_W, R_A, R_D0, R_REST, R_CR, R_CODE = 0, 12, 15, 18, 21, 22


def split(x):
    hi = x.astype(BF16)
    return hi, (x - hi.astype(F32)).astype(BF16)


def dot3(a, b, dims):
    f = functools.partial(lax.dot_general, dimension_numbers=dims, preferred_element_type=F32)
    return f(a[0], b[0]) + (f(a[0], b[1]) + f(a[1], b[0]))


def iota(shape, dim):
    return lax.broadcasted_iota(jnp.int32, shape, dim)


def pack_kernel(disp, rest, comp, weights, anchor, owner, msg, place, fields):
    fz_n, fx_n, cable_n = lax.axis_size("fz"), lax.axis_size("fx"), lax.axis_size("cable")
    device = (lax.axis_index("cable") * fx_n + lax.axis_index("fx")) * fz_n + lax.axis_index("fz")
    position = (device * SEG_DEV + iota((1, SEG_DEV), 1)).astype(F32)
    ramp = 1.0 + 2.0 * position / (SEG_DEV * fz_n * fx_n * cable_n)
    dest = iota((GROUP, SEG_DEV), 0)
    earlier = (iota((SEG_DEV, SEG_DEV), 0) < iota((SEG_DEV, SEG_DEV), 1)).astype(F32)
    hots, ranks, codes = [], [], []
    for t in range(3):
        own = owner[t : t + 1, :]
        hot = (dest == own).astype(F32)
        before = lax.dot_general(hot, earlier, NN, preferred_element_type=F32)
        rank = jnp.sum(hot * before, axis=0, keepdims=True)
        hots.append(hot)
        ranks.append(rank)
        codes.append(own.astype(F32) * CAP + rank)
    fields[...] = jnp.zeros_like(fields)
    fields[R_D0 : R_D0 + 3, :] = disp[...]
    fields[R_REST : R_REST + 3, :] = rest[...]
    fields[R_CR : R_CR + 1, :] = comp[...] * ramp
    fields[R_CODE : R_CODE + 1, :] = codes[0]
    fields[R_CODE + 1 : R_CODE + 2, :] = codes[1]
    for t in range(3):
        cell = anchor[t : t + 1, :]
        fields[R_W : R_W + 12, :] = weights[t]
        fields[R_A : R_A + 1, :] = (cell >> 11).astype(F32)
        fields[R_A + 1 : R_A + 2, :] = ((cell >> 7) & (SY - 1)).astype(F32)
        fields[R_A + 2 : R_A + 3, :] = (cell & (SZ - 1)).astype(F32)
        now = fields[...]
        placed = jnp.concatenate([jnp.where(ranks[t] == k, now, 0.0) for k in range(CAP)], axis=0)
        msg[:, 128 * t : 128 * t + 128] = lax.dot_general(
            hots[t], placed, NT, precision=EXACT, preferred_element_type=F32
        )
    place[...] = jnp.zeros_like(place)
    place[0:1, :] = owner[2:3, :].astype(F32)
    place[1:2, :] = ranks[2]


def slot_rows(block):
    wide = jnp.concatenate([block, jnp.zeros((128 - GROUP, 128), F32)], axis=0)
    turned = jnp.transpose(wide)
    low = turned[0:32] + pltpu.roll(turned[32:64], 64, 1)
    high = turned[64:96] + pltpu.roll(turned[96:128], 64, 1)
    return jnp.concatenate([low, high], axis=1)


def along(rows, first, start, extent):
    at = iota((extent, SLOTS), 0).astype(F32) - rows[start : start + 1]
    total = jnp.zeros((extent, SLOTS), F32)
    for i in range(4):
        total = jnp.where(at == i, rows[first + i : first + i + 1], total)
    return total


def tables(rows):
    wx = along(rows, R_W, R_A, SX)
    wy = along(rows, R_W + 4, R_A + 1, SY)
    wz = along(rows, R_W + 8, R_A + 2, SZ)
    wxy = jnp.concatenate([wx[x : x + 1] * wy for x in range(SX)], axis=0)
    return wxy, wz


def spread(wxy2, wz, disp):
    return dot3(wxy2, split(wz * (spread_gain * disp)), NT)


def look_up(sent, code):
    low_half = iota((1, 128), 1) < 64
    label = (iota((GROUP, SLOTS), 0) * CAP + iota((GROUP, SLOTS), 1) // 64).astype(F32)
    halves = [[None] * 2 for _ in range(3)]
    for half in range(2):
        piece = code[:, 128 * half : 128 * half + 128]
        turned = pltpu.roll(piece, 64, 1)
        found = []
        for odd in range(2):
            both = jnp.where(low_half, turned, piece) if odd else jnp.where(low_half, piece, turned)
            match = label == jnp.concatenate([both, both], axis=1)
            per = []
            for comp in range(3):
                hit = jnp.where(match, sent[:, comp * SLOTS : (comp + 1) * SLOTS], 0.0)
                hit = jnp.sum(hit, axis=0, keepdims=True)
                hit = hit[:, :128] + hit[:, 128:]
                per.append(hit + pltpu.roll(hit, 64, 1))
            found.append(per)
        for comp in range(3):
            halves[comp][half] = jnp.where(low_half, found[0][comp], found[1][comp])
    return [jnp.concatenate(halves[comp], axis=1) for comp in range(3)]


def responses(rows, sampled):
    cr = rows[R_CR : R_CR + 1]
    return [rows[R_REST + c : R_REST + c + 1] + cr * sampled[c] for c in range(3)]


def put_faces(field, first, xlo, xhi, ylo, yhi):
    for c in range(3):
        xlo[first + c] = field[first + c, 0:SY, :]
        xhi[first + c] = field[first + c, XY - SY : XY, :]
        ylo[first + c] = field[first + c, pl.ds(0, SX, stride=SY), :]
        yhi[first + c] = field[first + c, pl.ds(SY - 1, SX, stride=SY), :]


def spread_kernel(t, *refs):
    static, velocity = refs[0:2]
    sent = refs[2 : 2 + t]
    field, xlo, xhi, ylo, yhi, wxy_out, wz_out, aux = refs[2 + t : 10 + t]
    rows = slot_rows(static[:, 128 * t : 128 * t + 128])
    wxy, wz = tables(rows)
    wxy_out[...] = wxy
    wz_out[...] = wz
    wxy2 = split(wxy)
    first = [rows[R_D0 + c : R_D0 + c + 1] for c in range(3)]
    aux[...] = jnp.zeros_like(aux)
    if t == 0:
        bases = [first]
    else:
        before = responses(rows, look_up(sent[0], rows[R_CODE : R_CODE + 1]))
        gap = [before[c] - first[c] for c in range(3)]
        second = [first[c] + relaxation * gap[c] for c in range(3)]
        bases = [second]
        kept = [second, gap]
        if t == 2:
            latest = responses(rows, look_up(sent[1], rows[R_CODE + 1 : R_CODE + 2]))
            change = [latest[c] - before[c] for c in range(3)]
            bases = [latest, change]
            kept = [latest, change, gap, [latest[c] - second[c] for c in range(3)], before]
        for n, group in enumerate(kept):
            for c in range(3):
                aux[3 * n + c : 3 * n + c + 1, :] = group[c]
        aux[16:20, :] = rows[R_REST : R_REST + 4]
    for n, base in enumerate(bases):
        for c in range(3):
            forced = spread(wxy2, wz, base[c])
            field[3 * n + c] = velocity[c] + forced if n == 0 else forced
        put_faces(field, 3 * n, xlo, xhi, ylo, yhi)
    if t == 2:
        gram = refs[10 + t]
        total = jnp.sum(sent[1][:, 3 * SLOTS : 3 * SLOTS + 128], axis=0, keepdims=True)
        total = jnp.broadcast_to(total, (8, 128))
        gram[...] = total
        ylo[6] = total
        yhi[6] = total


def wake(u, beside_z, xl, xu, yl, yu, viscosity):
    lane = iota((XY, SZ), 1)
    y = iota((XY, SZ), 0) % SY
    upper_core = lax.axis_index("fz") > 0
    speed = jnp.sqrt(1.0 + (u[0] * u[0] + u[1] * u[1] + u[2] * u[2]))
    new = []
    for c in range(3):
        here = u[c]
        near = jnp.concatenate([xl[c], here[: XY - SY]], axis=0)
        near = near + jnp.concatenate([here[SY:], xu[c]], axis=0)
        wide_l = jnp.concatenate([jnp.broadcast_to(yl[c][x : x + 1], (SY, SZ)) for x in range(SX)], axis=0)
        wide_u = jnp.concatenate([jnp.broadcast_to(yu[c][x : x + 1], (SY, SZ)) for x in range(SX)], axis=0)
        near = near + jnp.where(y == 0, wide_l, pltpu.roll(here, 1, 0))
        near = near + jnp.where(y == SY - 1, wide_u, pltpu.roll(here, XY - 1, 0))
        left = jnp.where(upper_core, beside_z[c], 0.0)
        right = jnp.where(upper_core, 0.0, beside_z[c])
        near = near + pltpu.roll(jnp.where(lane == SZ - 1, left, here), 1, 1)
        near = near + pltpu.roll(jnp.where(lane == 0, right, here), SZ - 1, 1)
        new.append(here + viscosity * (near - 6.0 * here) - drag_coeff * here * speed)
    return new


def sample(new, wxy, wz):
    wz2 = split(wz)
    return [
        jnp.sum(wxy * dot3(split(new[c]), wz2, NN), axis=0, keepdims=True) for c in range(3)
    ]


def total_of(a, b):
    rows = a[0] * b[0] + a[1] * b[1] + a[2] * b[2]
    return jnp.sum(rows, axis=1, keepdims=True)


def in_lanes(values):
    lane = iota((1, 128), 1)
    row = jnp.zeros((1, 128), F32)
    for n, value in enumerate(values):
        row = jnp.where(lane == n, value, row)
    return row


def lane_of(row, n):
    return jnp.sum(jnp.where(iota(row.shape, 1) == n, row, 0.0), axis=1, keepdims=True)


def sample_kernel(t, *refs):
    viscosity, field, beside_z, xl, xu, yl, yu, wxy, wz, aux = refs[0:10]
    inside = (
        lax.axis_index("fx") > 0,
        lax.axis_index("fx") < lax.axis_size("fx") - 1,
        lax.axis_index("cable") > 0,
        lax.axis_index("cable") < lax.axis_size("cable") - 1,
    )

    def whole(ref):
        if t < 2:
            return [ref[c] for c in range(3)]
        return [ref[c] + coef * ref[3 + c] for c in range(3)]

    if t == 2:
        own, across = refs[10:12]
        gram = own[0:1] + yl[6][0:1] + yu[6][0:1] + across[0:1]
        square, target = lane_of(gram, 0), lane_of(gram, 1)
        coef = -target / (square + (ridge_share * square + 1e-06))
    u = whole(field)
    faces = [
        [jnp.where(ok, face, 0.0) for face in whole(ref)]
        for ok, ref in zip(inside, (xl, xu, yl, yu))
    ]
    new = wake(u, whole(beside_z), *faces, viscosity[...])
    sampled = sample(new, wxy[...], wz[...])
    if t == 0:
        msg = refs[10]
        for c in range(3):
            msg[:, SLOTS * c : SLOTS * (c + 1)] = jnp.broadcast_to(sampled[c], (GROUP, SLOTS))
        return

    def kept(n):
        return [aux[3 * n + c : 3 * n + c + 1, :] for c in range(3)]

    cr = aux[19:20, :]
    response = [aux[16 + c : 17 + c, :] + cr * sampled[c] for c in range(3)]
    if t == 1:
        msg = refs[10]
        disp, gap0 = kept(0), kept(1)
        gap = [response[c] - disp[c] for c in range(3)]
        v0 = [gap[c] - gap0[c] for c in range(3)]
        for c in range(3):
            msg[:, SLOTS * c : SLOTS * (c + 1)] = jnp.broadcast_to(sampled[c], (GROUP, SLOTS))
        row = in_lanes([total_of(v0, v0), total_of(v0, gap)])
        msg[:, 3 * SLOTS : 3 * SLOTS + 128] = jnp.broadcast_to(row, (GROUP, 128))
        return
    out, msg, turn = refs[12:15]
    for c in range(3):
        out[c] = new[c]
    latest, change, gap0, gap1, before = (kept(n) for n in range(5))
    disp = [latest[c] + coef * change[c] for c in range(3)]
    gap = [response[c] - disp[c] for c in range(3)]
    v0 = [gap[c] - gap0[c] for c in range(3)]
    v1 = [gap[c] - gap1[c] for c in range(3)]
    row = in_lanes(
        [total_of(v0, v0), total_of(v0, v1), total_of(v1, v1), total_of(v0, gap), total_of(v1, gap)]
    )
    turn[...] = jnp.zeros_like(turn)
    for n, group in enumerate((response, before, latest)):
        for c in range(3):
            turn[3 * n + c : 3 * n + c + 1, :] = group[c][:, :128]
            turn[32 + 3 * n + c : 33 + 3 * n + c, :] = group[c][:, 128:]
    turned = jnp.transpose(turn[...])
    block = turned[0:64] + pltpu.roll(turned[64:128], 16, 1)
    block = block + pltpu.roll(jnp.broadcast_to(row, (8, 128)), 64, 1)[0:1]
    for c in range(4):
        msg[GROUP * c : GROUP * (c + 1), :] = block


def finish_kernel(sent, place, out):
    row = jnp.sum(sent[...], axis=0, keepdims=True)
    g00, g01, g11, b0, b1 = (lane_of(row, 64 + n) for n in range(5))
    shift = ridge_share * (g00 + g11) / 2 + 1e-06
    first, second = g00 + shift, g11 + shift
    determinant = first * second - g01 * g01
    c0 = -(second * b0 - g01 * b1) / determinant
    c1 = -(first * b1 - g01 * b0) / determinant
    start = pl.multiple_of(lax.axis_index("cable") * GROUP, GROUP)
    mine = sent[pl.ds(start, GROUP), :]
    turned = jnp.transpose(jnp.concatenate([mine, jnp.zeros((128 - GROUP, 128), F32)], axis=0))
    hot = (iota((128, SEG_DEV), 0).astype(F32) == place[0:1, :]).astype(F32)
    got = lax.dot_general(turned[0:64], hot, NN, precision=EXACT, preferred_element_type=F32)
    rank = place[1:2, :]
    rows = jnp.zeros((16, SEG_DEV), F32)
    for k in range(CAP):
        rows = jnp.where(rank == k, got[16 * k : 16 * k + 16], rows)
    response, before, latest = rows[0:3], rows[3:6], rows[6:9]
    out[...] = response + c0 * (response - before) + c1 * (response - latest)


def call(kernel, name, ins, outs, scratch=(), flops=0):
    vmem = pl.BlockSpec(memory_space=pltpu.VMEM)
    size = sum(a.size * 4 for a in ins) + sum(4 * o[0] * o[1] * (o[2] if len(o) > 2 else 1) for o in outs)
    got = pl.pallas_call(
        kernel,
        name=name,
        out_shape=[jax.ShapeDtypeStruct(o, F32) for o in outs],
        in_specs=[vmem] * len(ins),
        out_specs=[vmem] * len(outs),
        scratch_shapes=list(scratch),
        compiler_params=pltpu.CompilerParams(vmem_limit_bytes=16 * 1024 * 1024),
        cost_estimate=pl.CostEstimate(flops=flops, bytes_accessed=size, transcendentals=0),
    )(*ins)
    return got


def shifted(array, axis, by):
    count = lax.axis_size(axis)
    return lax.ppermute(array, axis, [(i, (i + by) % count) for i in range(count)])


def exchange(array, axes):
    return lax.all_to_all(array, axes, 0, 0, tiled=True)


def body(velocity, viscosity, disp_init, rest_shape, compliance, stencil_weights, anchor, owners):
    group = ("fx", "fz")
    flow = velocity.reshape(3, XY, SZ)
    thick = viscosity.reshape(XY, SZ)
    msg, place = call(
        pack_kernel,
        "pack",
        (disp_init, rest_shape, compliance.reshape(1, SEG_DEV), stencil_weights, anchor, owners),
        [(GROUP, 384), (8, SEG_DEV)],
        [pltpu.VMEM((32, SEG_DEV), F32)],
    )
    static = exchange(msg, group)
    sent = []
    for t in range(3):
        n = 6 if t == 2 else 3
        ny = 7 if t == 2 else 3
        outs = [(n, XY, SZ), (n, SY, SZ), (n, SY, SZ), (ny, SX, SZ), (ny, SX, SZ)]
        outs += [(XY, SLOTS), (SZ, SLOTS), (24, SLOTS)]
        if t == 2:
            outs.append((8, 128))
        field, xlo, xhi, ylo, yhi, wxy, wz, aux, *gram = call(
            functools.partial(spread_kernel, t), f"spread{t}", (static, flow, *sent), outs
        )
        beside_z = shifted(field, "fz", 1)
        yl, yu = shifted(yhi, "cable", 1), shifted(ylo, "cable", -1)
        xl, xu = shifted(xhi, "fx", 1), shifted(xlo, "fx", -1)
        ins = [thick, field, beside_z, xl, xu, yl, yu, wxy, wz, aux]
        kernel, name = functools.partial(sample_kernel, t), f"sample{t}"
        if t < 2:
            width = 3 * SLOTS + (128 if t else 0)
            (msg,) = call(kernel, name, ins, [(GROUP, width)])
            sent.append(exchange(msg, group))
        else:
            ins += [gram[0], shifted(gram[0], "cable", 2)]
            out, msg = call(
                kernel, name, ins, [(3, XY, SZ), (4 * GROUP, 128)], [pltpu.VMEM((128, 128), F32)]
            )
    last = exchange(msg, ("cable", "fx", "fz"))
    (disp_next,) = call(finish_kernel, "finish", (last, place), [(3, SEG_DEV)])
    return disp_next, out.reshape(velocity.shape)


def solution(mesh):
    segments = ("cable", "fx", "fz")
    placed = (
        P(None, "fx", "cable", "fz"),
        P("fx", "cable", "fz"),
        P(None, segments),
        P(None, segments),
        P(segments),
        P(None, None, segments),
        P(None, segments),
        P(None, segments),
    )
    return jax.shard_map(
        body,
        mesh=mesh,
        in_specs=placed,
        out_specs=(P(None, segments), P(None, "fx", "cable", "fz")),
        check_vma=False,
    )
```

```python
import functools
import math

import jax
import jax.numpy as jnp
from jax import lax
from jax.experimental import pallas as pl
from jax.experimental.pallas import tpu as pltpu
from jax.sharding import PartitionSpec as P

F32 = jnp.float32
BF16 = jnp.bfloat16
NT = (((1,), (1,)), ((), ()))
NN = (((1,), (0,)), ((), ()))
EXACT = lax.Precision.HIGHEST

spread_gain = 16.0
drag_coeff = 0.05
relaxation = 0.5
ridge_share = 0.01

SEG_DEV = 64
GROUP = 64
CAP = 4
SLOTS = GROUP * CAP
SX, SY, SZ = 8, 16, 128
XY = SX * SY

R_W, R_CELL, R_D0, R_REST, R_CR, R_CODE = 0, 12, 13, 16, 19, 20
HEIGHT = (16, 24, 24)
SETS = 3
BASE = (0, 192, 480)
FIELDS = 768


def split(x):
    hi = x.astype(BF16)
    return hi, (x - hi.astype(F32)).astype(BF16)


def dot3(a, b, dims):
    f = functools.partial(lax.dot_general, dimension_numbers=dims, preferred_element_type=F32)
    return f(a[0], b[0]) + (f(a[0], b[1]) + f(a[1], b[0]))


def iota(shape, dim):
    return lax.broadcasted_iota(jnp.int32, shape, dim)


def pack_kernel(*refs):
    far, (msg, place, xlo, xhi), near, fields, turn, sems = refs[0:7], refs[7:11], refs[11:17], refs[17], refs[18], refs[19]
    copies = [pltpu.make_async_copy(far[n], near[n], sems.at[n]) for n in (5, 4, 3, 0, 1, 2)]
    copies.append(pltpu.make_async_copy(far[6].at[:, 0:SY, :], xlo, sems.at[6]))
    copies.append(pltpu.make_async_copy(far[6].at[:, XY - SY : XY, :], xhi, sems.at[7]))
    for copy in copies:
        copy.start()
    disp, rest, comp, weights, anchor, owner = near
    fz_n, fx_n, cable_n = lax.axis_size("fz"), lax.axis_size("fx"), lax.axis_size("cable")
    device = (lax.axis_index("cable") * fx_n + lax.axis_index("fx")) * fz_n + lax.axis_index("fz")
    position = (device * SEG_DEV + iota((1, SEG_DEV), 1)).astype(F32)
    ramp = 1.0 + 2.0 * position / (SEG_DEV * fz_n * fx_n * cable_n)
    dest = iota((GROUP, SEG_DEV), 0)
    earlier = (iota((SEG_DEV, SEG_DEV), 0) < iota((SEG_DEV, SEG_DEV), 1)).astype(F32)
    fields[...] = jnp.zeros_like(fields)
    turn[...] = jnp.zeros_like(turn)
    place[...] = jnp.zeros_like(place)
    for copy in copies:
        copy.wait()
    ranks, codes = [], []
    for t in range(3):
        own = owner[t : t + 1, :]
        hot = (dest == own).astype(F32)
        before = lax.dot_general(hot, earlier, NN, preferred_element_type=F32)
        rank = jnp.sum(hot * before, axis=0, keepdims=True)
        ranks.append(rank)
        codes.append(own.astype(F32) * CAP + rank)
    fields[R_D0 : R_D0 + 3, :] = disp[...]
    fields[R_REST : R_REST + 3, :] = rest[...]
    fields[R_CR : R_CR + 1, :] = comp[...] * ramp
    fields[R_CODE : R_CODE + 1, :] = codes[0] + SLOTS * codes[1]
    for t in range(3):
        own = owner[t : t + 1, :]
        fields[R_W : R_W + 12, :] = weights[t]
        fields[R_CELL : R_CELL + 1, :] = anchor[t : t + 1, :].astype(F32)
        now = fields[0 : HEIGHT[t], :]
        placed = jnp.concatenate([jnp.where(ranks[t] == k, now, 0.0) for k in range(CAP)], axis=0)
        for j, step in enumerate((0, fz_n, -fz_n)):
            start = BASE[t] + CAP * HEIGHT[t] * j
            turn[start : start + CAP * HEIGHT[t], 0:GROUP] = lax.dot_general(
                placed, (dest == own + step).astype(F32), NT, precision=EXACT, preferred_element_type=F32
            )
    for n in range(FIELDS // 128):
        msg[:, 128 * n : 128 * n + 128] = jnp.transpose(turn[128 * n : 128 * n + 128, :])[0:GROUP]
    place[0:1, :] = owner[2:3, :].astype(F32)
    place[1:2, :] = ranks[2]


def turn_static(static, turned, t):
    first = BASE[t] // 128
    last = (BASE[t] + SETS * CAP * HEIGHT[t] + 127) // 128
    for n in range(first, last):
        block = static[:, 128 * n : 128 * n + 128]
        wide = jnp.concatenate([block, jnp.zeros((128 - GROUP, 128), F32)], axis=0)
        turned[128 * n : 128 * n + 128, :] = jnp.transpose(wide)


def slot_rows(turned, t, j):
    height = HEIGHT[t]
    start = BASE[t] + CAP * height * j
    part = [turned[start + height * k : start + height * (k + 1), :] for k in range(CAP)]
    halves = [part[2 * n] + pltpu.roll(part[2 * n + 1], 64, 1) for n in range(2)]
    return jnp.concatenate(halves, axis=1)


def along(rows, first, at):
    total = jnp.zeros(at.shape, F32)
    for i in range(4):
        total = jnp.where(at == i, rows[first + i : first + i + 1], total)
    return total


def tables(rows, plane=None):
    cell = rows[R_CELL : R_CELL + 1].astype(jnp.int32)
    wy = along(rows, R_W + 4, iota((SY, SLOTS), 0) - ((cell >> 7) & (SY - 1)))
    wz = along(rows, R_W + 8, iota((SZ, SLOTS), 0) - (cell & (SZ - 1)))
    if plane is not None:
        return along(rows, R_W, plane - (cell >> 11)) * wy, wz
    wx = along(rows, R_W, iota((SX, SLOTS), 0) - (cell >> 11))
    return jnp.concatenate([wx[x : x + 1] * wy for x in range(SX)], axis=0), wz


def spread(wxy2, wz, disp):
    return dot3(wxy2, split(wz * (spread_gain * disp)), NT)


def look_up(sent, code):
    low_half = iota((1, 128), 1) < 64
    label = iota((GROUP, SLOTS), 0) * CAP + iota((GROUP, SLOTS), 1) // 64
    halves = [[None] * 2 for _ in range(3)]
    for half in range(2):
        piece = code[:, 128 * half : 128 * half + 128]
        turned = pltpu.roll(piece, 64, 1)
        found = []
        for odd in range(2):
            both = jnp.where(low_half, turned, piece) if odd else jnp.where(low_half, piece, turned)
            match = label == jnp.concatenate([both, both], axis=1)
            per = []
            for comp in range(3):
                hit = jnp.where(match, sent[:, comp * SLOTS : (comp + 1) * SLOTS], 0.0)
                hit = jnp.sum(hit, axis=0, keepdims=True)
                hit = hit[:, :128] + hit[:, 128:]
                per.append(hit + pltpu.roll(hit, 64, 1))
            found.append(per)
        for comp in range(3):
            halves[comp][half] = jnp.where(low_half, found[0][comp], found[1][comp])
    return [jnp.concatenate(halves[comp], axis=1) for comp in range(3)]


def responses(rows, sampled):
    cr = rows[R_CR : R_CR + 1]
    return [rows[R_REST + c : R_REST + c + 1] + cr * sampled[c] for c in range(3)]


def displacements(t, rows, sent):
    first = [rows[R_D0 + c : R_D0 + c + 1] for c in range(3)]
    if t == 0:
        return [first], []
    code = rows[R_CODE : R_CODE + 1].astype(jnp.int32)
    before = responses(rows, look_up(sent[0], code & (SLOTS - 1)))
    gap = [before[c] - first[c] for c in range(3)]
    second = [first[c] + relaxation * gap[c] for c in range(3)]
    if t == 1:
        return [second], [second, gap]
    latest = responses(rows, look_up(sent[1], code >> 8))
    change = [latest[c] - before[c] for c in range(3)]
    return [latest, change], [latest, change, gap, [latest[c] - second[c] for c in range(3)], before]


def spread_kernel(t, *refs):
    static, velocity, far_l, far_u = refs[0:4]
    sent = refs[4 : 4 + t]
    field, xl, xu, wxy_out, wz_out, aux = refs[4 + t : 10 + t]
    faces, turned = refs[10 + t : -1], refs[-1]
    turn_static(static, turned, t)
    rows = slot_rows(turned, t, 0)
    wxy, wz = tables(rows)
    wxy_out[...] = wxy
    wz_out[...] = wz
    wxy2 = split(wxy)
    bases, kept = displacements(t, rows, sent)
    for n, base in enumerate(bases):
        for c in range(3):
            forced = spread(wxy2, wz, base[c])
            field[3 * n + c] = velocity[c] + forced if n == 0 else forced
    if t > 0:
        aux[...] = jnp.zeros_like(aux)
        for n, group in enumerate(kept):
            for c in range(3):
                aux[3 * n + c : 3 * n + c + 1, :] = group[c]
        aux[16:20, :] = rows[R_REST : R_REST + 4]
    fx = lax.axis_index("fx")
    beside = ((xl, far_l, SX - 1, fx > 0), (xu, far_u, 0, fx < lax.axis_size("fx") - 1))
    for j, (out, far, plane, inside) in enumerate(beside):
        rows = slot_rows(turned, t, 1 + j)
        wxy, wz = tables(rows, plane)
        wxy2 = split(wxy)
        bases, _ = displacements(t, rows, sent)
        for n, base in enumerate(bases):
            for c in range(3):
                forced = spread(wxy2, wz, base[c])
                out[3 * n + c] = jnp.where(inside, far[c], 0.0) + forced if n == 0 else forced
    low = [field[n, pl.ds(0, SX, stride=SY), :] for n in range(3 * len(bases))]
    high = [field[n, pl.ds(SY - 1, SX, stride=SY), :] for n in range(3 * len(bases))]
    if t < 2:
        for c in range(3):
            faces[0][c] = low[c]
            faces[1][c] = high[c]
        return
    total = jnp.sum(sent[1][:, 3 * SLOTS : 3 * SLOTS + 128], axis=0, keepdims=True)
    total = jnp.broadcast_to(total, (8, 128))
    me = lax.axis_index("cable")
    for e in range(4):
        for n in range(6):
            faces[0][e, n] = jnp.where(me < e, high[n], low[n])
        faces[0][e, 6] = total


def wake(u, beside_z, xl, xu, yl, yu, viscosity):
    lane = iota((XY, SZ), 1)
    y = iota((XY, SZ), 0) % SY
    upper_core = lax.axis_index("fz") > 0
    speed = jnp.sqrt(1.0 + (u[0] * u[0] + u[1] * u[1] + u[2] * u[2]))
    new = []
    for c in range(3):
        here = u[c]
        near = jnp.concatenate([xl[c], here[: XY - SY]], axis=0)
        near = near + jnp.concatenate([here[SY:], xu[c]], axis=0)
        wide_l = jnp.concatenate([jnp.broadcast_to(yl[c][x : x + 1], (SY, SZ)) for x in range(SX)], axis=0)
        wide_u = jnp.concatenate([jnp.broadcast_to(yu[c][x : x + 1], (SY, SZ)) for x in range(SX)], axis=0)
        near = near + jnp.where(y == 0, wide_l, pltpu.roll(here, 1, 0))
        near = near + jnp.where(y == SY - 1, wide_u, pltpu.roll(here, XY - 1, 0))
        left = jnp.where(upper_core, beside_z[c], 0.0)
        right = jnp.where(upper_core, 0.0, beside_z[c])
        near = near + pltpu.roll(jnp.where(lane == SZ - 1, left, here), 1, 1)
        near = near + pltpu.roll(jnp.where(lane == 0, right, here), SZ - 1, 1)
        new.append(here + viscosity * (near - 6.0 * here) - drag_coeff * here * speed)
    return new


def sample(new, wxy, wz):
    wz2 = split(wz)
    return [
        jnp.sum(wxy * dot3(split(new[c]), wz2, NN), axis=0, keepdims=True) for c in range(3)
    ]


def total_of(a, b):
    rows = a[0] * b[0] + a[1] * b[1] + a[2] * b[2]
    return jnp.sum(rows, axis=1, keepdims=True)


def in_lanes(values):
    lane = iota((1, 128), 1)
    row = jnp.zeros((1, 128), F32)
    for n, value in enumerate(values):
        row = jnp.where(lane == n, value, row)
    return row


def lane_of(row, n):
    return jnp.sum(jnp.where(iota(row.shape, 1) == n, row, 0.0), axis=1, keepdims=True)


def sample_kernel(t, *refs):
    viscosity, field, beside_z, xl, xu, wxy, wz, aux = refs[0:8]
    me = lax.axis_index("cable")
    last = lax.axis_size("cable") - 1

    def whole(ref):
        if t < 2:
            return [ref[c] for c in range(3)]
        return [ref[c] + coef * ref[3 + c] for c in range(3)]

    if t < 2:
        yl = [jnp.where(me > 0, refs[8][c], 0.0) for c in range(3)]
        yu = [jnp.where(me < last, refs[9][c], 0.0) for c in range(3)]
    else:
        got = refs[8]
        gram = got[0, 6] + got[1, 6] + got[2, 6] + got[3, 6]
        square, target = lane_of(gram[0:1], 0), lane_of(gram[0:1], 1)
        coef = -target / (square + (ridge_share * square + 1e-06))
        yl, yu = [], []
        for c in range(3):
            below, above = jnp.zeros((SX, SZ), F32), jnp.zeros((SX, SZ), F32)
            for e in range(4):
                face = got[e, c] + coef * got[e, 3 + c]
                below = jnp.where(me == e + 1, face, below)
                above = jnp.where(me == e - 1, face, above)
            yl.append(below)
            yu.append(above)
    u = whole(field)
    faces = [whole(xl), whole(xu), yl, yu]
    new = wake(u, whole(beside_z), *faces, viscosity[...])
    sampled = sample(new, wxy[...], wz[...])
    if t == 0:
        for c in range(3):
            refs[10][:, SLOTS * c : SLOTS * (c + 1)] = jnp.broadcast_to(sampled[c], (GROUP, SLOTS))
        return

    def kept(n):
        return [aux[3 * n + c : 3 * n + c + 1, :] for c in range(3)]

    cr = aux[19:20, :]
    response = [aux[16 + c : 17 + c, :] + cr * sampled[c] for c in range(3)]
    if t == 1:
        msg = refs[10]
        disp, gap0 = kept(0), kept(1)
        gap = [response[c] - disp[c] for c in range(3)]
        v0 = [gap[c] - gap0[c] for c in range(3)]
        for c in range(3):
            msg[:, SLOTS * c : SLOTS * (c + 1)] = jnp.broadcast_to(sampled[c], (GROUP, SLOTS))
        row = in_lanes([total_of(v0, v0), total_of(v0, gap)])
        msg[:, 3 * SLOTS : 3 * SLOTS + 128] = jnp.broadcast_to(row, (GROUP, 128))
        return
    out, msg, turn = refs[9:12]
    for c in range(3):
        out[c] = new[c]
    latest, change, gap0, gap1, before = (kept(n) for n in range(5))
    disp = [latest[c] + coef * change[c] for c in range(3)]
    gap = [response[c] - disp[c] for c in range(3)]
    v0 = [gap[c] - gap0[c] for c in range(3)]
    v1 = [gap[c] - gap1[c] for c in range(3)]
    row = in_lanes(
        [total_of(v0, v0), total_of(v0, v1), total_of(v1, v1), total_of(v0, gap), total_of(v1, gap)]
    )
    turn[...] = jnp.zeros_like(turn)
    for n, group in enumerate((response, before, latest)):
        for c in range(3):
            turn[3 * n + c : 3 * n + c + 1, :] = group[c][:, :128]
            turn[32 + 3 * n + c : 33 + 3 * n + c, :] = group[c][:, 128:]
    turned = jnp.transpose(turn[...])
    block = turned[0:64] + pltpu.roll(turned[64:128], 16, 1)
    block = block + pltpu.roll(jnp.broadcast_to(row, (8, 128)), 64, 1)[0:1]
    for c in range(4):
        msg[GROUP * c : GROUP * (c + 1), :] = block


def finish_kernel(sent, place, out):
    row = jnp.sum(sent[...], axis=0, keepdims=True)
    g00, g01, g11, b0, b1 = (lane_of(row, 64 + n) for n in range(5))
    shift = ridge_share * (g00 + g11) / 2 + 1e-06
    first, second = g00 + shift, g11 + shift
    determinant = first * second - g01 * g01
    c0 = -(second * b0 - g01 * b1) / determinant
    c1 = -(first * b1 - g01 * b0) / determinant
    start = pl.multiple_of(lax.axis_index("cable") * GROUP, GROUP)
    mine = sent[pl.ds(start, GROUP), :]
    turned = jnp.transpose(jnp.concatenate([mine, jnp.zeros((128 - GROUP, 128), F32)], axis=0))
    hot = (iota((128, SEG_DEV), 0).astype(F32) == place[0:1, :]).astype(F32)
    got = lax.dot_general(turned[0:64], hot, NN, precision=EXACT, preferred_element_type=F32)
    rank = place[1:2, :]
    rows = jnp.zeros((16, SEG_DEV), F32)
    for k in range(CAP):
        rows = jnp.where(rank == k, got[16 * k : 16 * k + 16], rows)
    response, before, latest = rows[0:3], rows[3:6], rows[6:9]
    out[...] = response + c0 * (response - before) + c1 * (response - latest)


def call(kernel, name, ins, outs, scratch=(), space=pltpu.VMEM):
    size = sum(a.size * 4 for a in ins) + sum(4 * math.prod(o) for o in outs)
    return pl.pallas_call(
        kernel,
        name=name,
        out_shape=[jax.ShapeDtypeStruct(o, F32) for o in outs],
        in_specs=[pl.BlockSpec(memory_space=space)] * len(ins),
        out_specs=[pl.BlockSpec(memory_space=pltpu.VMEM)] * len(outs),
        scratch_shapes=list(scratch),
        compiler_params=pltpu.CompilerParams(vmem_limit_bytes=16 * 1024 * 1024),
        cost_estimate=pl.CostEstimate(flops=0, bytes_accessed=size, transcendentals=0),
    )(*ins)


def shifted(array, axis, by):
    count = lax.axis_size(axis)
    return lax.ppermute(array, axis, [(i, (i + by) % count) for i in range(count)])


def exchange(array, axes):
    return lax.all_to_all(array, axes, 0, 0, tiled=True)


def body(velocity, viscosity, disp_init, rest_shape, compliance, stencil_weights, anchor, owners):
    group = ("fx", "fz")
    flow = velocity.reshape(3, XY, SZ)
    thick = viscosity.reshape(XY, SZ)
    ins = (disp_init, rest_shape, compliance.reshape(1, SEG_DEV), stencil_weights, anchor, owners)
    msg, place, xlo, xhi = call(
        pack_kernel,
        "pack",
        (*ins, flow),
        [(GROUP, FIELDS), (8, SEG_DEV), (3, SY, SZ), (3, SY, SZ)],
        [pltpu.VMEM(a.shape, a.dtype) for a in ins]
        + [pltpu.VMEM((24, SEG_DEV), F32), pltpu.VMEM((FIELDS, 128), F32), pltpu.SemaphoreType.DMA((8,))],
        pltpu.HBM,
    )
    static = exchange(msg, group)
    far_l, far_u = shifted(xhi, "fx", 1), shifted(xlo, "fx", -1)
    sent = []
    for t in range(3):
        n = 6 if t == 2 else 3
        outs = [(n, XY, SZ), (n, SY, SZ), (n, SY, SZ), (XY, SLOTS), (SZ, SLOTS), (24, SLOTS)]
        outs += [(4, 7, SX, SZ)] if t == 2 else [(3, SX, SZ)] * 2
        field, xl, xu, wxy, wz, aux, *faces = call(
            functools.partial(spread_kernel, t),
            f"spread{t}",
            (static, flow, far_l, far_u, *sent),
            outs,
            [pltpu.VMEM((FIELDS, 128), F32)],
        )
        ins = [thick, field, shifted(field, "fz", 1), xl, xu, wxy, wz, aux]
        kernel, name = functools.partial(sample_kernel, t), f"sample{t}"
        if t < 2:
            ins += [shifted(faces[1], "cable", 1), shifted(faces[0], "cable", -1)]
            (msg,) = call(kernel, name, ins, [(GROUP, 3 * SLOTS + (128 if t else 0))])
            sent.append(exchange(msg, group))
        else:
            ins.append(exchange(faces[0], "cable"))
            out, msg = call(
                kernel, name, ins, [(3, XY, SZ), (4 * GROUP, 128)], [pltpu.VMEM((128, 128), F32)]
            )
    last = exchange(msg, ("cable", "fx", "fz"))
    (disp_next,) = call(finish_kernel, "finish", (last, place), [(3, SEG_DEV)])
    return disp_next, out.reshape(velocity.shape)


def solution(mesh):
    segments = ("cable", "fx", "fz")
    placed = (
        P(None, "fx", "cable", "fz"),
        P("fx", "cable", "fz"),
        P(None, segments),
        P(None, segments),
        P(segments),
        P(None, None, segments),
        P(None, segments),
        P(None, segments),
    )
    return jax.shard_map(
        body,
        mesh=mesh,
        in_specs=placed,
        out_specs=(P(None, segments), P(None, "fx", "cable", "fz")),
        check_vma=False,
    )
```

```python
import functools
import math

import jax
import jax.numpy as jnp
from jax import lax
from jax.experimental import pallas as pl
from jax.experimental.pallas import tpu as pltpu
from jax.sharding import PartitionSpec as P

F32 = jnp.float32
BF16 = jnp.bfloat16
NT = (((1,), (1,)), ((), ()))
NN = (((1,), (0,)), ((), ()))
EXACT = lax.Precision.HIGHEST

spread_gain = 16.0
drag_coeff = 0.05
relaxation = 0.5
ridge_share = 0.01

SEG_DEV = 64
GROUP = 64
CAP = 4
SLOTS = GROUP * CAP
SX, SY, SZ = 8, 16, 128
XY = SX * SY

R_W, R_CELL, R_D0, R_REST, R_CR, R_CODE = 0, 12, 13, 16, 19, 20
HEIGHT = (16, 24, 24)
SETS = 3
BASE = (0, 192, 480)
FIELDS = 768


def split(x):
    hi = x.astype(BF16)
    return hi, (x - hi.astype(F32)).astype(BF16)


def dot3(a, b, dims):
    f = functools.partial(lax.dot_general, dimension_numbers=dims, preferred_element_type=F32)
    return f(a[0], b[0]) + (f(a[0], b[1]) + f(a[1], b[0]))


def iota(shape, dim):
    return lax.broadcasted_iota(jnp.int32, shape, dim)


def pack_kernel(*refs):
    far, (msg, place, xlo, xhi), near, fields, turn, sems = refs[0:7], refs[7:11], refs[11:17], refs[17], refs[18], refs[19]
    copies = [pltpu.make_async_copy(far[n], near[n], sems.at[n]) for n in (5, 4, 3, 0, 1, 2)]
    copies.append(pltpu.make_async_copy(far[6].at[:, 0:SY, :], xlo, sems.at[6]))
    copies.append(pltpu.make_async_copy(far[6].at[:, XY - SY : XY, :], xhi, sems.at[7]))
    for copy in copies:
        copy.start()
    disp, rest, comp, weights, anchor, owner = near
    fz_n, fx_n, cable_n = lax.axis_size("fz"), lax.axis_size("fx"), lax.axis_size("cable")
    device = (lax.axis_index("cable") * fx_n + lax.axis_index("fx")) * fz_n + lax.axis_index("fz")
    position = (device * SEG_DEV + iota((1, SEG_DEV), 1)).astype(F32)
    ramp = 1.0 + 2.0 * position / (SEG_DEV * fz_n * fx_n * cable_n)
    dest = iota((GROUP, SEG_DEV), 0)
    earlier = (iota((SEG_DEV, SEG_DEV), 0) < iota((SEG_DEV, SEG_DEV), 1)).astype(F32)
    fields[...] = jnp.zeros_like(fields)
    turn[...] = jnp.zeros_like(turn)
    place[...] = jnp.zeros_like(place)
    for copy in copies:
        copy.wait()
    ranks, codes = [], []
    for t in range(3):
        own = owner[t : t + 1, :]
        hot = (dest == own).astype(F32)
        before = lax.dot_general(hot, earlier, NN, preferred_element_type=F32)
        rank = jnp.sum(hot * before, axis=0, keepdims=True)
        ranks.append(rank)
        codes.append(own.astype(F32) * CAP + rank)
    fields[R_D0 : R_D0 + 3, :] = disp[...]
    fields[R_REST : R_REST + 3, :] = rest[...]
    fields[R_CR : R_CR + 1, :] = comp[...] * ramp
    fields[R_CODE : R_CODE + 1, :] = codes[0] + SLOTS * codes[1]
    for t in range(3):
        own = owner[t : t + 1, :]
        fields[R_W : R_W + 12, :] = weights[t]
        fields[R_CELL : R_CELL + 1, :] = anchor[t : t + 1, :].astype(F32)
        now = fields[0 : HEIGHT[t], :]
        placed = jnp.concatenate([jnp.where(ranks[t] == k, now, 0.0) for k in range(CAP)], axis=0)
        for j, step in enumerate((0, fz_n, -fz_n)):
            start = BASE[t] + CAP * HEIGHT[t] * j
            turn[start : start + CAP * HEIGHT[t], 0:GROUP] = lax.dot_general(
                placed, (dest == own + step).astype(F32), NT, precision=EXACT, preferred_element_type=F32
            )
    for n in range(FIELDS // 128):
        msg[:, 128 * n : 128 * n + 128] = jnp.transpose(turn[128 * n : 128 * n + 128, :])[0:GROUP]
    place[0:1, :] = owner[2:3, :].astype(F32)
    place[1:2, :] = ranks[2]


def turn_static(static, turned, t):
    first = BASE[t] // 128
    last = (BASE[t] + SETS * CAP * HEIGHT[t] + 127) // 128
    for n in range(first, last):
        block = static[:, 128 * n : 128 * n + 128]
        wide = jnp.concatenate([block, jnp.zeros((128 - GROUP, 128), F32)], axis=0)
        turned[128 * n : 128 * n + 128, :] = jnp.transpose(wide)


def slot_rows(turned, t, j):
    height = HEIGHT[t]
    start = BASE[t] + CAP * height * j
    part = [turned[start + height * k : start + height * (k + 1), :] for k in range(CAP)]
    halves = [part[2 * n] + pltpu.roll(part[2 * n + 1], 64, 1) for n in range(2)]
    return jnp.concatenate(halves, axis=1)


def along(rows, first, at):
    total = jnp.zeros(at.shape, F32)
    for i in range(4):
        total = jnp.where(at == i, rows[first + i : first + i + 1], total)
    return total


def tables(rows, plane=None):
    cell = rows[R_CELL : R_CELL + 1].astype(jnp.int32)
    wy = along(rows, R_W + 4, iota((SY, SLOTS), 0) - ((cell >> 7) & (SY - 1)))
    wz = along(rows, R_W + 8, iota((SZ, SLOTS), 0) - (cell & (SZ - 1)))
    if plane is not None:
        return along(rows, R_W, plane - (cell >> 11)) * wy, wz
    wx = along(rows, R_W, iota((SX, SLOTS), 0) - (cell >> 11))
    return jnp.concatenate([wx[x : x + 1] * wy for x in range(SX)], axis=0), wz


def spread(wxy2, wz, disp):
    return dot3(wxy2, split(wz * (spread_gain * disp)), NT)


def look_up(sent, code):
    low_half = iota((1, 128), 1) < 64
    label = iota((GROUP, SLOTS), 0) * CAP + iota((GROUP, SLOTS), 1) // 64
    halves = [[None] * 2 for _ in range(3)]
    for half in range(2):
        piece = code[:, 128 * half : 128 * half + 128]
        turned = pltpu.roll(piece, 64, 1)
        found = []
        for odd in range(2):
            both = jnp.where(low_half, turned, piece) if odd else jnp.where(low_half, piece, turned)
            match = label == jnp.concatenate([both, both], axis=1)
            per = []
            for comp in range(3):
                hit = jnp.where(match, sent[:, comp * SLOTS : (comp + 1) * SLOTS], 0.0)
                hit = jnp.sum(hit, axis=0, keepdims=True)
                hit = hit[:, :128] + hit[:, 128:]
                per.append(hit + pltpu.roll(hit, 64, 1))
            found.append(per)
        for comp in range(3):
            halves[comp][half] = jnp.where(low_half, found[0][comp], found[1][comp])
    return [jnp.concatenate(halves[comp], axis=1) for comp in range(3)]


def responses(rows, sampled):
    cr = rows[R_CR : R_CR + 1]
    return [rows[R_REST + c : R_REST + c + 1] + cr * sampled[c] for c in range(3)]


def displacements(t, rows, sent):
    first = [rows[R_D0 + c : R_D0 + c + 1] for c in range(3)]
    if t == 0:
        return [first], []
    code = rows[R_CODE : R_CODE + 1].astype(jnp.int32)
    before = responses(rows, look_up(sent[0], code & (SLOTS - 1)))
    gap = [before[c] - first[c] for c in range(3)]
    second = [first[c] + relaxation * gap[c] for c in range(3)]
    if t == 1:
        return [second], [second, gap]
    latest = responses(rows, look_up(sent[1], code >> 8))
    change = [latest[c] - before[c] for c in range(3)]
    return [latest, change], [latest, change, gap, [latest[c] - second[c] for c in range(3)], before]


def spread_kernel(t, *refs):
    static, velocity, far_l, far_u = refs[0:4]
    sent = refs[4 : 4 + t]
    field, xl, xu, wxy_out, wz_out, aux = refs[4 + t : 10 + t]
    faces, turned = refs[10 + t : -1], refs[-1]
    turn_static(static, turned, t)
    rows = slot_rows(turned, t, 0)
    wxy, wz = tables(rows)
    wxy_out[...] = wxy
    wz_out[...] = wz
    wxy2 = split(wxy)
    bases, kept = displacements(t, rows, sent)
    for n, base in enumerate(bases):
        for c in range(3):
            forced = spread(wxy2, wz, base[c])
            field[3 * n + c] = velocity[c] + forced if n == 0 else forced
    if t > 0:
        aux[...] = jnp.zeros_like(aux)
        for n, group in enumerate(kept):
            for c in range(3):
                aux[3 * n + c : 3 * n + c + 1, :] = group[c]
        aux[16:20, :] = rows[R_REST : R_REST + 4]
    fx = lax.axis_index("fx")
    beside = ((xl, far_l, SX - 1, fx > 0), (xu, far_u, 0, fx < lax.axis_size("fx") - 1))
    for j, (out, far, plane, inside) in enumerate(beside):
        rows = slot_rows(turned, t, 1 + j)
        wxy, wz = tables(rows, plane)
        wxy2 = split(wxy)
        bases, _ = displacements(t, rows, sent)
        for n, base in enumerate(bases):
            for c in range(3):
                forced = spread(wxy2, wz, base[c])
                out[3 * n + c] = jnp.where(inside, far[c], 0.0) + forced if n == 0 else forced
    low = [field[n, pl.ds(0, SX, stride=SY), :] for n in range(3 * len(bases))]
    high = [field[n, pl.ds(SY - 1, SX, stride=SY), :] for n in range(3 * len(bases))]
    if t < 2:
        for c in range(3):
            faces[0][c] = low[c]
            faces[1][c] = high[c]
        return
    total = jnp.sum(sent[1][:, 3 * SLOTS : 3 * SLOTS + 128], axis=0, keepdims=True)
    total = jnp.broadcast_to(total, (8, 128))
    me = lax.axis_index("cable")
    for e in range(4):
        for n in range(6):
            faces[0][e, n] = jnp.where(me < e, high[n], low[n])
        faces[0][e, 6] = total


def wake(u, beside_z, xl, xu, yl, yu, viscosity):
    lane = iota((XY, SZ), 1)
    y = iota((XY, SZ), 0) % SY
    upper_core = lax.axis_index("fz") > 0
    speed = jnp.sqrt(1.0 + (u[0] * u[0] + u[1] * u[1] + u[2] * u[2]))
    new = []
    for c in range(3):
        here = u[c]
        near = jnp.concatenate([xl[c], here[: XY - SY]], axis=0)
        near = near + jnp.concatenate([here[SY:], xu[c]], axis=0)
        wide_l = jnp.concatenate([jnp.broadcast_to(yl[c][x : x + 1], (SY, SZ)) for x in range(SX)], axis=0)
        wide_u = jnp.concatenate([jnp.broadcast_to(yu[c][x : x + 1], (SY, SZ)) for x in range(SX)], axis=0)
        near = near + jnp.where(y == 0, wide_l, pltpu.roll(here, 1, 0))
        near = near + jnp.where(y == SY - 1, wide_u, pltpu.roll(here, XY - 1, 0))
        left = jnp.where(upper_core, beside_z[c], 0.0)
        right = jnp.where(upper_core, 0.0, beside_z[c])
        near = near + pltpu.roll(jnp.where(lane == SZ - 1, left, here), 1, 1)
        near = near + pltpu.roll(jnp.where(lane == 0, right, here), SZ - 1, 1)
        new.append(here + viscosity * (near - 6.0 * here) - drag_coeff * here * speed)
    return new


def sample(new, wxy, wz):
    wz2 = split(wz)
    return [
        jnp.sum(wxy * dot3(split(new[c]), wz2, NN), axis=0, keepdims=True) for c in range(3)
    ]


def total_of(a, b):
    rows = a[0] * b[0] + a[1] * b[1] + a[2] * b[2]
    return jnp.sum(rows, axis=1, keepdims=True)


def in_lanes(values):
    lane = iota((1, 128), 1)
    row = jnp.zeros((1, 128), F32)
    for n, value in enumerate(values):
        row = jnp.where(lane == n, value, row)
    return row


def lane_of(row, n):
    return jnp.sum(jnp.where(iota(row.shape, 1) == n, row, 0.0), axis=1, keepdims=True)


def sample_kernel(t, *refs):
    viscosity, field, beside_z, xl, xu, wxy, wz, aux = refs[0:8]
    me = lax.axis_index("cable")
    last = lax.axis_size("cable") - 1

    def whole(ref):
        if t < 2:
            return [ref[c] for c in range(3)]
        return [ref[c] + coef * ref[3 + c] for c in range(3)]

    if t < 2:
        yl = [jnp.where(me > 0, refs[8][c], 0.0) for c in range(3)]
        yu = [jnp.where(me < last, refs[9][c], 0.0) for c in range(3)]
    else:
        got = refs[8]
        gram = got[0, 6] + got[1, 6] + got[2, 6] + got[3, 6]
        square, target = lane_of(gram[0:1], 0), lane_of(gram[0:1], 1)
        coef = -target / (square + (ridge_share * square + 1e-06))
        yl, yu = [], []
        for c in range(3):
            below, above = jnp.zeros((SX, SZ), F32), jnp.zeros((SX, SZ), F32)
            for e in range(4):
                face = got[e, c] + coef * got[e, 3 + c]
                below = jnp.where(me == e + 1, face, below)
                above = jnp.where(me == e - 1, face, above)
            yl.append(below)
            yu.append(above)
    u = whole(field)
    faces = [whole(xl), whole(xu), yl, yu]
    new = wake(u, whole(beside_z), *faces, viscosity[...])
    sampled = sample(new, wxy[...], wz[...])
    if t == 0:
        for c in range(3):
            refs[10][:, SLOTS * c : SLOTS * (c + 1)] = jnp.broadcast_to(sampled[c], (GROUP, SLOTS))
        return

    def kept(n):
        return [aux[3 * n + c : 3 * n + c + 1, :] for c in range(3)]

    cr = aux[19:20, :]
    response = [aux[16 + c : 17 + c, :] + cr * sampled[c] for c in range(3)]
    if t == 1:
        msg = refs[10]
        disp, gap0 = kept(0), kept(1)
        gap = [response[c] - disp[c] for c in range(3)]
        v0 = [gap[c] - gap0[c] for c in range(3)]
        for c in range(3):
            msg[:, SLOTS * c : SLOTS * (c + 1)] = jnp.broadcast_to(sampled[c], (GROUP, SLOTS))
        row = in_lanes([total_of(v0, v0), total_of(v0, gap)])
        msg[:, 3 * SLOTS : 3 * SLOTS + 128] = jnp.broadcast_to(row, (GROUP, 128))
        return
    out, msg, turn = refs[9:12]
    for c in range(3):
        out[c] = new[c]
    latest, change, gap0, gap1, before = (kept(n) for n in range(5))
    disp = [latest[c] + coef * change[c] for c in range(3)]
    gap = [response[c] - disp[c] for c in range(3)]
    v0 = [gap[c] - gap0[c] for c in range(3)]
    v1 = [gap[c] - gap1[c] for c in range(3)]
    row = in_lanes(
        [total_of(v0, v0), total_of(v0, v1), total_of(v1, v1), total_of(v0, gap), total_of(v1, gap)]
    )
    turn[...] = jnp.zeros_like(turn)
    for n, group in enumerate((response, before, latest)):
        for c in range(3):
            turn[3 * n + c : 3 * n + c + 1, :] = group[c][:, :128]
            turn[32 + 3 * n + c : 33 + 3 * n + c, :] = group[c][:, 128:]
    turned = jnp.transpose(turn[...])
    block = turned[0:64] + pltpu.roll(turned[64:128], 16, 1)
    block = block + pltpu.roll(jnp.broadcast_to(row, (8, 128)), 64, 1)[0:1]
    for c in range(4):
        msg[GROUP * c : GROUP * (c + 1), :] = block


def finish_kernel(sent, place, out):
    row = jnp.sum(sent[...], axis=0, keepdims=True)
    g00, g01, g11, b0, b1 = (lane_of(row, 64 + n) for n in range(5))
    shift = ridge_share * (g00 + g11) / 2 + 1e-06
    first, second = g00 + shift, g11 + shift
    determinant = first * second - g01 * g01
    c0 = -(second * b0 - g01 * b1) / determinant
    c1 = -(first * b1 - g01 * b0) / determinant
    start = pl.multiple_of(lax.axis_index("cable") * GROUP, GROUP)
    mine = sent[pl.ds(start, GROUP), :]
    turned = jnp.transpose(jnp.concatenate([mine, jnp.zeros((128 - GROUP, 128), F32)], axis=0))
    hot = (iota((128, SEG_DEV), 0).astype(F32) == place[0:1, :]).astype(F32)
    got = lax.dot_general(turned[0:64], hot, NN, precision=EXACT, preferred_element_type=F32)
    rank = place[1:2, :]
    rows = jnp.zeros((16, SEG_DEV), F32)
    for k in range(CAP):
        rows = jnp.where(rank == k, got[16 * k : 16 * k + 16], rows)
    response, before, latest = rows[0:3], rows[3:6], rows[6:9]
    out[...] = response + c0 * (response - before) + c1 * (response - latest)


def call(kernel, name, ins, outs, scratch=(), space=pltpu.VMEM):
    size = sum(a.size * 4 for a in ins) + sum(4 * math.prod(o) for o in outs)
    return pl.pallas_call(
        kernel,
        name=name,
        out_shape=[jax.ShapeDtypeStruct(o, F32) for o in outs],
        in_specs=[pl.BlockSpec(memory_space=space)] * len(ins),
        out_specs=[pl.BlockSpec(memory_space=pltpu.VMEM)] * len(outs),
        scratch_shapes=list(scratch),
        compiler_params=pltpu.CompilerParams(vmem_limit_bytes=16 * 1024 * 1024),
        cost_estimate=pl.CostEstimate(flops=0, bytes_accessed=size, transcendentals=0),
    )(*ins)


def shifted(array, axis, by):
    count = lax.axis_size(axis)
    return lax.ppermute(array, axis, [(i, (i + by) % count) for i in range(count)])


def exchange(array, axes):
    return lax.all_to_all(array, axes, 0, 0, tiled=True)


def body(velocity, viscosity, disp_init, rest_shape, compliance, stencil_weights, anchor, owners):
    group = ("fx", "fz")
    flow = velocity.reshape(3, XY, SZ)
    thick = viscosity.reshape(XY, SZ)
    ins = (disp_init, rest_shape, compliance.reshape(1, SEG_DEV), stencil_weights, anchor, owners)
    msg, place, xlo, xhi = call(
        pack_kernel,
        "pack",
        tuple(pltpu.with_memory_space_constraint(a, pltpu.HBM) for a in (*ins, flow)),
        [(GROUP, FIELDS), (8, SEG_DEV), (3, SY, SZ), (3, SY, SZ)],
        [pltpu.VMEM(a.shape, a.dtype) for a in ins]
        + [pltpu.VMEM((24, SEG_DEV), F32), pltpu.VMEM((FIELDS, 128), F32), pltpu.SemaphoreType.DMA((8,))],
        pltpu.HBM,
    )
    static = exchange(msg, group)
    far_l, far_u = shifted(xhi, "fx", 1), shifted(xlo, "fx", -1)
    sent = []
    for t in range(3):
        n = 6 if t == 2 else 3
        outs = [(n, XY, SZ), (n, SY, SZ), (n, SY, SZ), (XY, SLOTS), (SZ, SLOTS), (24, SLOTS)]
        outs += [(4, 7, SX, SZ)] if t == 2 else [(3, SX, SZ)] * 2
        field, xl, xu, wxy, wz, aux, *faces = call(
            functools.partial(spread_kernel, t),
            f"spread{t}",
            (static, flow, far_l, far_u, *sent),
            outs,
            [pltpu.VMEM((FIELDS, 128), F32)],
        )
        ins = [thick, field, shifted(field, "fz", 1), xl, xu, wxy, wz, aux]
        kernel, name = functools.partial(sample_kernel, t), f"sample{t}"
        if t < 2:
            ins += [shifted(faces[1], "cable", 1), shifted(faces[0], "cable", -1)]
            (msg,) = call(kernel, name, ins, [(GROUP, 3 * SLOTS + (128 if t else 0))])
            sent.append(exchange(msg, group))
        else:
            ins.append(exchange(faces[0], "cable"))
            out, msg = call(
                kernel, name, ins, [(3, XY, SZ), (4 * GROUP, 128)], [pltpu.VMEM((128, 128), F32)]
            )
    last = exchange(msg, ("cable", "fx", "fz"))
    (disp_next,) = call(finish_kernel, "finish", (last, place), [(3, SEG_DEV)])
    return disp_next, out.reshape(velocity.shape)


def solution(mesh):
    segments = ("cable", "fx", "fz")
    placed = (
        P(None, "fx", "cable", "fz"),
        P("fx", "cable", "fz"),
        P(None, segments),
        P(None, segments),
        P(segments),
        P(None, None, segments),
        P(None, segments),
        P(None, segments),
    )
    return jax.shard_map(
        body,
        mesh=mesh,
        in_specs=placed,
        out_specs=(P(None, segments), P(None, "fx", "cable", "fz")),
        check_vma=False,
    )
```

```python
import functools
import math

import jax
import jax.numpy as jnp
from jax import lax
from jax.experimental import pallas as pl
from jax.experimental.pallas import tpu as pltpu
from jax.sharding import PartitionSpec as P


F32 = jnp.float32
BF16 = jnp.bfloat16
NT = (((1,), (1,)), ((), ()))
NN = (((1,), (0,)), ((), ()))
EXACT = lax.Precision.HIGHEST

spread_gain = 16.0
drag_coeff = 0.05
relaxation = 0.5
ridge_share = 0.01

SEG_DEV = 64
GROUP = 64
CAP = 4
SLOTS = GROUP * CAP
SX, SY, SZ = 8, 16, 128
XY = SX * SY

R_W, R_CELL, R_D0, R_REST, R_CR, R_CODE = 0, 12, 13, 16, 19, 20
HEIGHT = (16, 24, 24)
SETS = 3
BASE = (0, 192, 480)
FIELDS = 768


def split(x):
    hi = x.astype(BF16)
    return hi, (x - hi.astype(F32)).astype(BF16)


def dot(a, b, dims):
    return lax.dot_general(a, b, dims, preferred_element_type=F32)


def iota(shape, dim):
    return lax.broadcasted_iota(jnp.int32, shape, dim)


def pack_kernel(*refs):
    far, (msg, place, xlo, xhi), near, fields, turn, sems = refs[0:7], refs[7:11], refs[11:17], refs[17], refs[18], refs[19]
    copies = [pltpu.make_async_copy(far[n], near[n], sems.at[n]) for n in (5, 4, 3, 0, 1, 2)]
    copies.append(pltpu.make_async_copy(far[6].at[:, 0:SY, :], xlo, sems.at[6]))
    copies.append(pltpu.make_async_copy(far[6].at[:, XY - SY : XY, :], xhi, sems.at[7]))
    for copy in copies:
        copy.start()
    disp, rest, comp, weights, anchor, owner = near
    fz_n, fx_n, cable_n = lax.axis_size("fz"), lax.axis_size("fx"), lax.axis_size("cable")
    device = (lax.axis_index("cable") * fx_n + lax.axis_index("fx")) * fz_n + lax.axis_index("fz")
    position = (device * SEG_DEV + iota((1, SEG_DEV), 1)).astype(F32)
    ramp = 1.0 + 2.0 * position / (SEG_DEV * fz_n * fx_n * cable_n)
    dest = iota((GROUP, SEG_DEV), 0)
    earlier = (iota((SEG_DEV, SEG_DEV), 0) < iota((SEG_DEV, SEG_DEV), 1)).astype(F32)
    fields[...] = jnp.zeros_like(fields)
    turn[...] = jnp.zeros_like(turn)
    place[...] = jnp.zeros_like(place)
    for copy in copies:
        copy.wait()
    ranks, codes = [], []
    for t in range(3):
        own = owner[t : t + 1, :]
        hot = (dest == own).astype(F32)
        before = dot(hot, earlier, NN)
        rank = jnp.sum(hot * before, axis=0, keepdims=True)
        ranks.append(rank)
        codes.append(own.astype(F32) * CAP + rank)
    fields[R_D0 : R_D0 + 3, :] = disp[...]
    fields[R_REST : R_REST + 3, :] = rest[...]
    fields[R_CR : R_CR + 1, :] = comp[...] * ramp
    fields[R_CODE : R_CODE + 1, :] = codes[0] + SLOTS * codes[1]
    for t in range(3):
        own = owner[t : t + 1, :]
        fields[R_W : R_W + 12, :] = weights[t]
        fields[R_CELL : R_CELL + 1, :] = anchor[t : t + 1, :].astype(F32)
        now = fields[0 : HEIGHT[t], :]
        placed = jnp.concatenate([jnp.where(ranks[t] == k, now, 0.0) for k in range(CAP)], axis=0)
        hi, rest_of = split(placed)
        low = (placed - hi.astype(F32) - rest_of.astype(F32)).astype(BF16)
        hots = [(dest == own + step).astype(F32).astype(BF16) for step in (0, fz_n, -fz_n)]
        hots = jnp.concatenate(hots, axis=0)
        got = dot(hi, hots, NT) + (dot(rest_of, hots, NT) + dot(low, hots, NT))
        for j in range(SETS):
            start = BASE[t] + CAP * HEIGHT[t] * j
            turn[start : start + CAP * HEIGHT[t], 0:GROUP] = got[:, GROUP * j : GROUP * (j + 1)]
    for n in range(FIELDS // 128):
        msg[:, 128 * n : 128 * n + 128] = jnp.transpose(turn[128 * n : 128 * n + 128, :])[0:GROUP]
    place[0:1, :] = owner[2:3, :].astype(F32)
    place[1:2, :] = ranks[2]


def turn_static(static, turned, t):
    first = BASE[t] // 128
    last = (BASE[t] + SETS * CAP * HEIGHT[t] + 127) // 128
    for n in range(first, last):
        block = static[:, 128 * n : 128 * n + 128]
        wide = jnp.concatenate([block, jnp.zeros((128 - GROUP, 128), F32)], axis=0)
        turned[128 * n : 128 * n + 128, :] = jnp.transpose(wide)


def slot_rows(turned, t, j):
    height = HEIGHT[t]
    start = BASE[t] + CAP * height * j
    part = [turned[start + height * k : start + height * (k + 1), :] for k in range(CAP)]
    halves = [part[2 * n] + pltpu.roll(part[2 * n + 1], 64, 1) for n in range(2)]
    return jnp.concatenate(halves, axis=1)


def along(rows, first, at):
    total = jnp.zeros(at.shape, F32)
    for i in range(4):
        total = jnp.where(at == i, rows[first + i : first + i + 1], total)
    return total


def tables(rows, plane=None):
    cell = rows[R_CELL : R_CELL + 1].astype(jnp.int32)
    wy = along(rows, R_W + 4, iota((SY, SLOTS), 0) - ((cell >> 7) & (SY - 1)))
    wz = along(rows, R_W + 8, iota((SZ, SLOTS), 0) - (cell & (SZ - 1)))
    if plane is not None:
        return along(rows, R_W, plane - (cell >> 11)) * wy, wz
    wx = along(rows, R_W, iota((SX, SLOTS), 0) - (cell >> 11))
    return jnp.concatenate([wx[x : x + 1] * wy for x in range(SX)], axis=0), wz


def spread(wxy, wz2, base):
    hi, low = split(jnp.concatenate([wxy * (spread_gain * base[c]) for c in range(3)], axis=0))
    both = dot(hi, wz2, NT)
    return both[:, :SZ] + (both[:, SZ:] + dot(low, wz2[0:SZ], NT))


def look_up(halves, code):
    low_half = iota((1, 128), 1) < 64
    mine = lax.axis_index("fz")
    height = GROUP // 2
    label = (iota((height, SLOTS), 0) * 2 + mine) * CAP + iota((height, SLOTS), 1) // 64
    labels = (label, label + CAP * (1 - 2 * mine))
    found = [[None] * 2 for _ in range(3)]
    for part in range(2):
        piece = code[:, 128 * part : 128 * part + 128]
        turned = pltpu.roll(piece, 64, 1)
        pair = []
        for odd in range(2):
            both = jnp.where(low_half, turned, piece) if odd else jnp.where(low_half, piece, turned)
            wanted = jnp.concatenate([both, both], axis=1)
            per = []
            for comp in range(3):
                lanes = slice(comp * SLOTS, (comp + 1) * SLOTS)
                hit = jnp.where(labels[0] == wanted, halves[0][:, lanes], 0.0)
                hit = hit + jnp.where(labels[1] == wanted, halves[1][:, lanes], 0.0)
                hit = jnp.sum(hit, axis=0, keepdims=True)
                hit = hit[:, :128] + hit[:, 128:]
                per.append(hit + pltpu.roll(hit, 64, 1))
            pair.append(per)
        for comp in range(3):
            found[comp][part] = jnp.where(low_half, pair[0][comp], pair[1][comp])
    return [jnp.concatenate(found[comp], axis=1) for comp in range(3)]


def responses(rows, sampled):
    cr = rows[R_CR : R_CR + 1]
    return [rows[R_REST + c : R_REST + c + 1] + cr * sampled[c] for c in range(3)]


def prepare_kernel(t, *refs):
    static, sent, (wxy_out, wz_out, plane_out, slots, turned) = refs[0], refs[1:-5], refs[-5:]
    turn_static(static, turned, t)
    for j in range(SETS):
        rows = slot_rows(turned, t, j)
        wxy, wz = tables(rows, (None, SX - 1, 0)[j])
        hi, low = split(wz)
        wz_out[j, 0:SZ, :] = hi
        wz_out[j, SZ:, :] = low
        if j == 0:
            wxy_out[...] = wxy
        else:
            plane_out[j - 1] = wxy
        slots[32 * j : 32 * j + HEIGHT[t], :] = rows
        if t == 2:
            code = rows[R_CODE : R_CODE + 1].astype(jnp.int32)
            before = responses(rows, look_up(sent, code & (SLOTS - 1)))
            for c in range(3):
                slots[32 * j + 24 + c : 32 * j + 25 + c, :] = before[c]


def displacements(t, rows, sent):
    first = [rows[R_D0 + c : R_D0 + c + 1] for c in range(3)]
    if t == 0:
        return [first], []
    code = rows[R_CODE : R_CODE + 1].astype(jnp.int32)
    if t == 1:
        before = responses(rows, look_up(sent, code & (SLOTS - 1)))
    else:
        before = [rows[24 + c : 25 + c] for c in range(3)]
    gap = [before[c] - first[c] for c in range(3)]
    second = [first[c] + relaxation * gap[c] for c in range(3)]
    if t == 1:
        return [second], [second, gap]
    latest = responses(rows, look_up(sent, code >> 8))
    change = [latest[c] - before[c] for c in range(3)]
    return [latest, change], [latest, change, gap, [latest[c] - second[c] for c in range(3)], before]


def spread_kernel(t, *refs):
    if t == 0:
        static, velocity, far_l, far_u = refs[0:4]
        sent = ()
        field, xl, xu, ylo, yhi, *tabled, turned = refs[4:]
        prepare_kernel(0, static, *tabled, turned)
    else:
        velocity, far_l, far_u = refs[0:3]
        sent, tabled = refs[3:5], refs[5:9]
        field, xl, xu, ylo, yhi, aux = refs[9:15]
        aux[...] = jnp.zeros_like(aux)
    wxy, wz, plane, slots = tabled
    fx = lax.axis_index("fx")
    inside = (None, fx > 0, fx < lax.axis_size("fx") - 1)
    for j, out in enumerate((field, xl, xu)):
        rows = slots[32 * j : 32 * j + 32, :]
        bases, kept = displacements(t, rows, sent)
        height = SY if j else XY
        for n, base in enumerate(bases):
            forced = spread(plane[j - 1] if j else wxy[...], wz[j], base)
            for c in range(3):
                part = forced[height * c : height * (c + 1)]
                if n == 0 and j == 0:
                    part = part + velocity[c]
                elif n == 0:
                    part = part + jnp.where(inside[j], (far_l, far_u)[j - 1][c], 0.0)
                out[3 * n + c] = part
        if j == 0 and t > 0:
            for n, group in enumerate(kept):
                for c in range(3):
                    aux[3 * n + c : 3 * n + c + 1, :] = group[c]
            aux[16:20, :] = rows[R_REST : R_REST + 4]
    for n in range(3 * len(bases)):
        ylo[n] = field[n, pl.ds(0, SX, stride=SY), :]
        yhi[n] = field[n, pl.ds(SY - 1, SX, stride=SY), :]
    if t == 2:
        lanes = slice(3 * SLOTS, 3 * SLOTS + 128)
        total = jnp.sum(sent[0][:, lanes] + sent[1][:, lanes], axis=0, keepdims=True)
        total = jnp.broadcast_to(total, (8, 128))
        ylo[6] = total
        yhi[6] = total
        refs[15][...] = total


def wake(u, beside_z, xl, xu, yl, yu, viscosity):
    lane = iota((XY, SZ), 1)
    y = iota((XY, SZ), 0) % SY
    upper_core = lax.axis_index("fz") > 0
    speed = jnp.sqrt(1.0 + (u[0] * u[0] + u[1] * u[1] + u[2] * u[2]))
    new = []
    for c in range(3):
        here = u[c]
        near = jnp.concatenate([xl[c], here[: XY - SY]], axis=0)
        near = near + jnp.concatenate([here[SY:], xu[c]], axis=0)
        wide_l = jnp.concatenate([jnp.broadcast_to(yl[c][x : x + 1], (SY, SZ)) for x in range(SX)], axis=0)
        wide_u = jnp.concatenate([jnp.broadcast_to(yu[c][x : x + 1], (SY, SZ)) for x in range(SX)], axis=0)
        near = near + jnp.where(y == 0, wide_l, pltpu.roll(here, 1, 0))
        near = near + jnp.where(y == SY - 1, wide_u, pltpu.roll(here, XY - 1, 0))
        left = jnp.where(upper_core, beside_z[c], 0.0)
        right = jnp.where(upper_core, 0.0, beside_z[c])
        near = near + pltpu.roll(jnp.where(lane == SZ - 1, left, here), 1, 1)
        near = near + pltpu.roll(jnp.where(lane == 0, right, here), SZ - 1, 1)
        new.append(here + viscosity * (near - 6.0 * here) - drag_coeff * here * speed)
    return new


def sample(new, wxy, wz2):
    wz_hi, wz_low = wz2[0:SZ], wz2[SZ:]
    both = jnp.concatenate([wz_hi, wz_hi], axis=0)
    sampled = []
    for c in range(3):
        hi, low = split(new[c])
        along_z = dot(jnp.concatenate([hi, low], axis=1), both, NN) + dot(hi, wz_low, NN)
        sampled.append(jnp.sum(wxy * along_z, axis=0, keepdims=True))
    return sampled


def total_of(a, b):
    rows = a[0] * b[0] + a[1] * b[1] + a[2] * b[2]
    return jnp.sum(rows, axis=1, keepdims=True)


def in_lanes(values):
    lane = iota((1, 128), 1)
    row = jnp.zeros((1, 128), F32)
    for n, value in enumerate(values):
        row = jnp.where(lane == n, value, row)
    return row


def lane_of(row, n):
    return jnp.sum(jnp.where(iota(row.shape, 1) == n, row, 0.0), axis=1, keepdims=True)


def sample_kernel(t, *refs):
    viscosity, field, beside_z, xl, xu, yl, yu, wxy, wz = refs[0:9]
    me = lax.axis_index("cable")
    last = lax.axis_size("cable") - 1

    def whole(ref):
        if t < 2:
            return [ref[c] for c in range(3)]
        return [ref[c] + coef * ref[3 + c] for c in range(3)]

    if t == 2:
        gram = yl[6] + yu[6] + (refs[10][...] + refs[11][...])
        square, target = lane_of(gram[0:1], 0), lane_of(gram[0:1], 1)
        coef = -target / (square + (ridge_share * square + 1e-06))
    u = whole(field)
    below = [jnp.where(me > 0, face, 0.0) for face in whole(yl)]
    above = [jnp.where(me < last, face, 0.0) for face in whole(yu)]
    faces = [whole(xl), whole(xu), below, above]
    new = wake(u, whole(beside_z), *faces, viscosity[...])
    sampled = sample(new, wxy[...], wz[0])
    if t == 0:
        for c in range(3):
            refs[9][:, SLOTS * c : SLOTS * (c + 1)] = jnp.broadcast_to(sampled[c], (GROUP // 2, SLOTS))
        return
    aux = refs[9]

    def kept(n):
        return [aux[3 * n + c : 3 * n + c + 1, :] for c in range(3)]

    cr = aux[19:20, :]
    response = [aux[16 + c : 17 + c, :] + cr * sampled[c] for c in range(3)]
    if t == 1:
        msg = refs[10]
        disp, gap0 = kept(0), kept(1)
        gap = [response[c] - disp[c] for c in range(3)]
        v0 = [gap[c] - gap0[c] for c in range(3)]
        for c in range(3):
            msg[:, SLOTS * c : SLOTS * (c + 1)] = jnp.broadcast_to(sampled[c], (GROUP // 2, SLOTS))
        row = in_lanes([total_of(v0, v0), total_of(v0, gap)])
        msg[:, 3 * SLOTS : 3 * SLOTS + 128] = jnp.broadcast_to(row, (GROUP // 2, 128))
        return
    out, msg, turn = refs[12:15]
    for c in range(3):
        out[c] = new[c]
    latest, change, gap0, gap1, before = (kept(n) for n in range(5))
    disp = [latest[c] + coef * change[c] for c in range(3)]
    gap = [response[c] - disp[c] for c in range(3)]
    v0 = [gap[c] - gap0[c] for c in range(3)]
    v1 = [gap[c] - gap1[c] for c in range(3)]
    row = in_lanes(
        [total_of(v0, v0), total_of(v0, v1), total_of(v1, v1), total_of(v0, gap), total_of(v1, gap)]
    )
    turn[...] = jnp.zeros_like(turn)
    for n, group in enumerate((response, before, latest)):
        for c in range(3):
            turn[3 * n + c : 3 * n + c + 1, :] = group[c][:, :128]
            turn[32 + 3 * n + c : 33 + 3 * n + c, :] = group[c][:, 128:]
    turned = jnp.transpose(turn[...])
    block = turned[0:64] + pltpu.roll(turned[64:128], 16, 1)
    block = block + pltpu.roll(jnp.broadcast_to(row, (8, 128)), 64, 1)[0:1]
    for c in range(4):
        msg[GROUP * c : GROUP * (c + 1), :] = block


def finish_kernel(sent, place, out):
    row = jnp.sum(sent[...], axis=0, keepdims=True)
    g00, g01, g11, b0, b1 = (lane_of(row, 64 + n) for n in range(5))
    shift = ridge_share * (g00 + g11) / 2 + 1e-06
    first, second = g00 + shift, g11 + shift
    determinant = first * second - g01 * g01
    c0 = -(second * b0 - g01 * b1) / determinant
    c1 = -(first * b1 - g01 * b0) / determinant
    start = pl.multiple_of(lax.axis_index("cable") * GROUP, GROUP)
    mine = sent[pl.ds(start, GROUP), :]
    turned = jnp.transpose(jnp.concatenate([mine, jnp.zeros((128 - GROUP, 128), F32)], axis=0))
    hot = (iota((128, SEG_DEV), 0).astype(F32) == place[0:1, :]).astype(F32)
    got = lax.dot_general(turned[0:64], hot, NN, precision=EXACT, preferred_element_type=F32)
    rank = place[1:2, :]
    rows = jnp.zeros((16, SEG_DEV), F32)
    for k in range(CAP):
        rows = jnp.where(rank == k, got[16 * k : 16 * k + 16], rows)
    response, before, latest = rows[0:3], rows[3:6], rows[6:9]
    out[...] = response + c0 * (response - before) + c1 * (response - latest)


def shape(*dims, kind=F32):
    return jax.ShapeDtypeStruct(dims, kind)


def call(kernel, name, ins, outs, scratch=(), space=pltpu.VMEM):
    size = sum(a.size * a.dtype.itemsize for a in (*ins, *outs))
    return pl.pallas_call(
        kernel,
        name=name,
        out_shape=outs,
        in_specs=[pl.BlockSpec(memory_space=space)] * len(ins),
        out_specs=[pl.BlockSpec(memory_space=pltpu.VMEM)] * len(outs),
        scratch_shapes=list(scratch),
        compiler_params=pltpu.CompilerParams(vmem_limit_bytes=16 * 1024 * 1024),
        cost_estimate=pl.CostEstimate(flops=0, bytes_accessed=size, transcendentals=0),
    )(*ins)


def shifted(array, axis, by):
    count = lax.axis_size(axis)
    return lax.ppermute(array, axis, [(i, (i + by) % count) for i in range(count)])


def exchange(array, axes):
    return lax.all_to_all(array, axes, 0, 0, tiled=True)


def body(velocity, viscosity, disp_init, rest_shape, compliance, stencil_weights, anchor, owners):
    flow = velocity.reshape(3, XY, SZ)
    thick = viscosity.reshape(XY, SZ)
    ins = (disp_init, rest_shape, compliance.reshape(1, SEG_DEV), stencil_weights, anchor, owners)
    msg, place, xlo, xhi = call(
        pack_kernel,
        "pack",
        tuple(pltpu.with_memory_space_constraint(a, pltpu.HBM) for a in (*ins, flow)),
        [shape(GROUP, FIELDS), shape(8, SEG_DEV), shape(3, SY, SZ), shape(3, SY, SZ)],
        [pltpu.VMEM(a.shape, a.dtype) for a in ins]
        + [pltpu.VMEM((24, SEG_DEV), F32), pltpu.VMEM((FIELDS, 128), F32), pltpu.SemaphoreType.DMA((8,))],
        pltpu.HBM,
    )
    static = exchange(msg, ("fx", "fz"))
    far_l, far_u = shifted(xhi, "fx", 1), shifted(xlo, "fx", -1)
    table_outs = [
        shape(XY, SLOTS),
        shape(SETS, 2 * SZ, SLOTS, kind=BF16),
        shape(2, SY, SLOTS),
        shape(32 * SETS, SLOTS),
    ]
    turned = [pltpu.VMEM((FIELDS, 128), F32)]
    sent, tabled = (), ()
    for t in range(3):
        n = 6 if t == 2 else 3
        faced = 7 if t == 2 else 3
        outs = [shape(n, XY, SZ), shape(n, SY, SZ), shape(n, SY, SZ)] + [shape(faced, SX, SZ)] * 2
        kernel, name = functools.partial(spread_kernel, t), f"spread{t}"
        if t == 0:
            field, xl, xu, ylo, yhi, *tabled = call(
                kernel, name, (static, flow, far_l, far_u), outs + table_outs, turned
            )
            extra = []
        else:
            outs.append(shape(24, SLOTS))
            if t == 2:
                outs.append(shape(8, 128))
            field, xl, xu, ylo, yhi, *extra = call(
                kernel, name, (flow, far_l, far_u, *sent, *tabled), outs
            )
        ins = [thick, field, shifted(field, "fz", 1), xl, xu]
        ins += [shifted(yhi, "cable", 1), shifted(ylo, "cable", -1), *tabled[0:2], *extra]
        if t < 2:
            tabled = call(
                functools.partial(prepare_kernel, t + 1),
                f"prepare{t + 1}",
                (static, *sent),
                table_outs,
                turned,
            )
        kernel, name = functools.partial(sample_kernel, t), f"sample{t}"
        if t < 2:
            (msg,) = call(kernel, name, ins, [shape(GROUP // 2, 3 * SLOTS + (128 if t else 0))])
            half = exchange(msg, "fx")
            sent = (half, shifted(half, "fz", 1))
        else:
            ins.append(shifted(extra[1], "cable", 2))
            out, msg = call(
                kernel, name, ins, [shape(3, XY, SZ), shape(4 * GROUP, 128)], [pltpu.VMEM((128, 128), F32)]
            )
    last = exchange(msg, ("cable", "fx", "fz"))
    (disp_next,) = call(finish_kernel, "finish", (last, place), [shape(3, SEG_DEV)])
    return disp_next, out.reshape(velocity.shape)


def solution(mesh):
    segments = ("cable", "fx", "fz")
    placed = (
        P(None, "fx", "cable", "fz"),
        P("fx", "cable", "fz"),
        P(None, segments),
        P(None, segments),
        P(segments),
        P(None, None, segments),
        P(None, segments),
        P(None, segments),
    )
    return jax.shard_map(
        body,
        mesh=mesh,
        in_specs=placed,
        out_specs=(P(None, segments), P(None, "fx", "cable", "fz")),
        check_vma=False,
    )
```

```python
import functools
import math

import jax
import jax.numpy as jnp
from jax import lax
from jax.experimental import pallas as pl
from jax.experimental.pallas import tpu as pltpu
from jax.sharding import PartitionSpec as P


F32 = jnp.float32
BF16 = jnp.bfloat16
NT = (((1,), (1,)), ((), ()))
NN = (((1,), (0,)), ((), ()))

spread_gain = 16.0
drag_coeff = 0.05
relaxation = 0.5
ridge_share = 0.01

SEG_DEV = 64
GROUP = 64
HALF = GROUP // 2
CAP = 4
SLOTS = GROUP * CAP
SX, SY, SZ = 8, 16, 128
XY = SX * SY

R_W, R_CELL, R_D0, R_REST, R_CR, R_CODE = 0, 12, 13, 16, 19, 20
HEIGHT = (16, 24, 24)
SETS = 3
BASE = (0, 192, 480)
FIELDS = 768


def split(x):
    hi = x.astype(BF16)
    return hi, (x - hi.astype(F32)).astype(BF16)


def dot(a, b, dims):
    return lax.dot_general(a, b, dims, preferred_element_type=F32)


def iota(shape, dim):
    return lax.broadcasted_iota(jnp.int32, shape, dim)


def pack_kernel(*refs):
    far, (keep, give, place, xlo, xhi), near, (fields, turn, sems) = refs[0:7], refs[7:12], refs[12:18], refs[18:21]
    copies = [pltpu.make_async_copy(far[n], near[n], sems.at[n]) for n in (5, 4, 3, 0, 1, 2)]
    copies.append(pltpu.make_async_copy(far[6].at[:, 0:SY, :], xlo, sems.at[6]))
    copies.append(pltpu.make_async_copy(far[6].at[:, XY - SY : XY, :], xhi, sems.at[7]))
    for copy in copies:
        copy.start()
    disp, rest, comp, weights, anchor, owner = near
    fz_n, fx_n, cable_n = lax.axis_size("fz"), lax.axis_size("fx"), lax.axis_size("cable")
    device = (lax.axis_index("cable") * fx_n + lax.axis_index("fx")) * fz_n + lax.axis_index("fz")
    position = (device * SEG_DEV + iota((1, SEG_DEV), 1)).astype(F32)
    ramp = 1.0 + 2.0 * position / (SEG_DEV * fz_n * fx_n * cable_n)
    dest = iota((GROUP, SEG_DEV), 0)
    earlier = (iota((SEG_DEV, SEG_DEV), 0) < iota((SEG_DEV, SEG_DEV), 1)).astype(F32)
    fields[...] = jnp.zeros_like(fields)
    turn[...] = jnp.zeros_like(turn)
    place[...] = jnp.zeros_like(place)
    for copy in copies:
        copy.wait()
    mine = lax.axis_index("fz")
    ranks, codes, places = [], [], []
    for t in range(3):
        own = owner[t : t + 1, :]
        at = ((own & 1) ^ mine) * HALF + (own >> 1)
        hot = (dest == at).astype(F32)
        before = dot(hot, earlier, NN)
        rank = jnp.sum(hot * before, axis=0, keepdims=True)
        ranks.append(rank)
        codes.append(own.astype(F32) * CAP + rank)
        after = jnp.where((own >> 1) < HALF - 1, at + 1, -1)
        ahead = jnp.where((own >> 1) > 0, at - 1, -1)
        places.append((at, after, ahead))
    fields[R_D0 : R_D0 + 3, :] = disp[...]
    fields[R_REST : R_REST + 3, :] = rest[...]
    fields[R_CR : R_CR + 1, :] = comp[...] * ramp
    fields[R_CODE : R_CODE + 1, :] = codes[0] + SLOTS * codes[1]
    for t in range(3):
        fields[R_W : R_W + 12, :] = weights[t]
        fields[R_CELL : R_CELL + 1, :] = anchor[t : t + 1, :].astype(F32)
        now = fields[0 : HEIGHT[t], :]
        placed = jnp.concatenate([jnp.where(ranks[t] == k, now, 0.0) for k in range(CAP)], axis=0)
        hi, rest_of = split(placed)
        low = (placed - hi.astype(F32) - rest_of.astype(F32)).astype(BF16)
        hots = [(dest == at).astype(F32).astype(BF16) for at in places[t]]
        hots = jnp.concatenate(hots, axis=0)
        got = dot(hi, hots, NT) + (dot(rest_of, hots, NT) + dot(low, hots, NT))
        for j in range(SETS):
            start = BASE[t] + CAP * HEIGHT[t] * j
            turn[start : start + CAP * HEIGHT[t], 0:GROUP] = got[:, GROUP * j : GROUP * (j + 1)]
    for n in range(FIELDS // 128):
        lanes = slice(128 * n, 128 * n + 128)
        block = jnp.transpose(turn[lanes, :])
        keep[:, lanes] = block[0:HALF]
        give[:, lanes] = block[HALF:GROUP]
    place[0:1, :] = (owner[2:3, :] >> 1).astype(F32)
    place[1:2, :] = ranks[2] + CAP * ((owner[2:3, :] & 1) ^ mine).astype(F32)


def turn_static(static, turned, t):
    first = BASE[t] // 128
    last = (BASE[t] + SETS * CAP * HEIGHT[t] + 127) // 128
    low = lax.axis_index("fz") == 0
    for n in range(first, last):
        same = static[:, 128 * n : 128 * n + 128]
        other = static[:, FIELDS + 128 * n : FIELDS + 128 * n + 128]
        wide = jnp.concatenate(
            [jnp.where(low, same, other), jnp.where(low, other, same), jnp.zeros((128 - GROUP, 128), F32)],
            axis=0,
        )
        turned[128 * n : 128 * n + 128, :] = jnp.transpose(wide)


def slot_rows(turned, t, j):
    height = HEIGHT[t]
    start = BASE[t] + CAP * height * j
    part = [turned[start + height * k : start + height * (k + 1), :] for k in range(CAP)]
    halves = [part[2 * n] + pltpu.roll(part[2 * n + 1], 64, 1) for n in range(2)]
    return jnp.concatenate(halves, axis=1)


def along(rows, first, at):
    total = jnp.zeros(at.shape, F32)
    for i in range(4):
        total = jnp.where(at == i, rows[first + i : first + i + 1], total)
    return total


def tables(rows, plane=None):
    cell = rows[R_CELL : R_CELL + 1].astype(jnp.int32)
    wy = along(rows, R_W + 4, iota((SY, SLOTS), 0) - ((cell >> 7) & (SY - 1)))
    wz = along(rows, R_W + 8, iota((SZ, SLOTS), 0) - (cell & (SZ - 1)))
    if plane is not None:
        return along(rows, R_W, plane - (cell >> 11)) * wy, wz
    wx = along(rows, R_W, iota((SX, SLOTS), 0) - (cell >> 11))
    return jnp.concatenate([wx[x : x + 1] * wy for x in range(SX)], axis=0), wz


def spread(wxy, wz2, base):
    hi, low = split(jnp.concatenate([wxy * (spread_gain * base[c]) for c in range(3)], axis=0))
    both = dot(hi, wz2, NT)
    return both[:, :SZ] + (both[:, SZ:] + dot(low, wz2[0:SZ], NT))


def look_up(halves, code):
    low_half = iota((1, 128), 1) < 64
    mine = lax.axis_index("fz")
    height = HALF
    label = (iota((height, SLOTS), 0) * 2 + mine) * CAP + iota((height, SLOTS), 1) // 64
    labels = (label, label + CAP * (1 - 2 * mine))
    found = [[None] * 2 for _ in range(3)]
    for part in range(2):
        piece = code[:, 128 * part : 128 * part + 128]
        turned = pltpu.roll(piece, 64, 1)
        pair = []
        for odd in range(2):
            both = jnp.where(low_half, turned, piece) if odd else jnp.where(low_half, piece, turned)
            wanted = jnp.concatenate([both, both], axis=1)
            per = []
            for comp in range(3):
                lanes = slice(comp * SLOTS, (comp + 1) * SLOTS)
                hit = jnp.where(labels[0] == wanted, halves[0][:, lanes], 0.0)
                hit = hit + jnp.where(labels[1] == wanted, halves[1][:, lanes], 0.0)
                hit = jnp.sum(hit, axis=0, keepdims=True)
                hit = hit[:, :128] + hit[:, 128:]
                per.append(hit + pltpu.roll(hit, 64, 1))
            pair.append(per)
        for comp in range(3):
            found[comp][part] = jnp.where(low_half, pair[0][comp], pair[1][comp])
    return [jnp.concatenate(found[comp], axis=1) for comp in range(3)]


def responses(rows, sampled):
    cr = rows[R_CR : R_CR + 1]
    return [rows[R_REST + c : R_REST + c + 1] + cr * sampled[c] for c in range(3)]


def prepare_kernel(t, *refs):
    static, sent, (wxy_out, wz_out, plane_out, slots, turned) = refs[0], refs[1:-5], refs[-5:]
    turn_static(static, turned, t)
    for j in range(SETS):
        rows = slot_rows(turned, t, j)
        wxy, wz = tables(rows, (None, SX - 1, 0)[j])
        hi, low = split(wz)
        wz_out[j, 0:SZ, :] = hi
        wz_out[j, SZ:, :] = low
        if j == 0:
            wxy_out[...] = wxy
        else:
            plane_out[j - 1] = wxy
        slots[32 * j : 32 * j + HEIGHT[t], :] = rows
        if t == 2:
            code = rows[R_CODE : R_CODE + 1].astype(jnp.int32)
            before = responses(rows, look_up(sent, code & (SLOTS - 1)))
            for c in range(3):
                slots[32 * j + 24 + c : 32 * j + 25 + c, :] = before[c]


def displacements(t, rows, sent):
    first = [rows[R_D0 + c : R_D0 + c + 1] for c in range(3)]
    if t == 0:
        return [first], []
    code = rows[R_CODE : R_CODE + 1].astype(jnp.int32)
    if t == 1:
        before = responses(rows, look_up(sent, code & (SLOTS - 1)))
    else:
        before = [rows[24 + c : 25 + c] for c in range(3)]
    gap = [before[c] - first[c] for c in range(3)]
    second = [first[c] + relaxation * gap[c] for c in range(3)]
    if t == 1:
        return [second], [second, gap]
    latest = responses(rows, look_up(sent, code >> 8))
    change = [latest[c] - before[c] for c in range(3)]
    return [latest, change], [latest, change, gap, [latest[c] - second[c] for c in range(3)], before]


def spread_kernel(t, *refs):
    if t == 0:
        static, velocity, far_l, far_u = refs[0:4]
        sent = ()
        field, xl, xu, ylo, yhi, *tabled, turned = refs[4:]
        prepare_kernel(0, static, *tabled, turned)
    else:
        velocity, far_l, far_u = refs[0:3]
        sent, tabled = refs[3:5], refs[5:9]
        across, refs = (refs[9:10], refs[10:]) if t == 2 else ((), refs[9:])
        field, xl, xu, ylo, yhi, aux = refs[0:6]
        aux[...] = jnp.zeros_like(aux)
    wxy, wz, plane, slots = tabled
    fx = lax.axis_index("fx")
    inside = (None, fx > 0, fx < lax.axis_size("fx") - 1)
    for j, out in enumerate((field, xl, xu)):
        rows = slots[32 * j : 32 * j + 32, :]
        bases, kept = displacements(t, rows, sent)
        height = SY if j else XY
        for n, base in enumerate(bases):
            forced = spread(plane[j - 1] if j else wxy[...], wz[j], base)
            for c in range(3):
                part = forced[height * c : height * (c + 1)]
                if n == 0 and j == 0:
                    part = part + velocity[c]
                elif n == 0:
                    part = part + jnp.where(inside[j], (far_l, far_u)[j - 1][c], 0.0)
                out[3 * n + c] = part
        if j == 0 and t > 0:
            for n, group in enumerate(kept):
                for c in range(3):
                    aux[3 * n + c : 3 * n + c + 1, :] = group[c]
            aux[16:20, :] = rows[R_REST : R_REST + 4]
    for n in range(3 * len(bases)):
        ylo[n] = field[n, pl.ds(0, SX, stride=SY), :]
        yhi[n] = field[n, pl.ds(SY - 1, SX, stride=SY), :]
    if t == 2:
        lanes = slice(3 * SLOTS, 3 * SLOTS + 128)
        total = jnp.sum(sent[0][:, lanes] + sent[1][:, lanes], axis=0, keepdims=True)
        total = jnp.broadcast_to(total, (8, 128))
        ylo[6] = total
        yhi[6] = total
        field[6] = jnp.zeros((XY, SZ), F32)
        field[6, 0:8, :] = across[0][...]
        refs[6][...] = total + across[0][...]


def part_gram_kernel(half, out):
    total = jnp.sum(half[:, 3 * SLOTS : 3 * SLOTS + 128], axis=0, keepdims=True)
    out[...] = jnp.broadcast_to(total, (8, 128))


def wake(u, beside_z, xl, xu, yl, yu, viscosity):
    lane = iota((XY, SZ), 1)
    y = iota((XY, SZ), 0) % SY
    upper_core = lax.axis_index("fz") > 0
    speed = jnp.sqrt(1.0 + (u[0] * u[0] + u[1] * u[1] + u[2] * u[2]))
    new = []
    for c in range(3):
        here = u[c]
        near = jnp.concatenate([xl[c], here[: XY - SY]], axis=0)
        near = near + jnp.concatenate([here[SY:], xu[c]], axis=0)
        wide_l = jnp.concatenate([jnp.broadcast_to(yl[c][x : x + 1], (SY, SZ)) for x in range(SX)], axis=0)
        wide_u = jnp.concatenate([jnp.broadcast_to(yu[c][x : x + 1], (SY, SZ)) for x in range(SX)], axis=0)
        near = near + jnp.where(y == 0, wide_l, pltpu.roll(here, 1, 0))
        near = near + jnp.where(y == SY - 1, wide_u, pltpu.roll(here, XY - 1, 0))
        left = jnp.where(upper_core, beside_z[c], 0.0)
        right = jnp.where(upper_core, 0.0, beside_z[c])
        near = near + pltpu.roll(jnp.where(lane == SZ - 1, left, here), 1, 1)
        near = near + pltpu.roll(jnp.where(lane == 0, right, here), SZ - 1, 1)
        new.append(here + viscosity * (near - 6.0 * here) - drag_coeff * here * speed)
    return new


def sample(new, wxy, wz2):
    wz_hi, wz_low = wz2[0:SZ], wz2[SZ:]
    both = jnp.concatenate([wz_hi, wz_hi], axis=0)
    sampled = []
    for c in range(3):
        hi, low = split(new[c])
        along_z = dot(jnp.concatenate([hi, low], axis=1), both, NN) + dot(hi, wz_low, NN)
        sampled.append(jnp.sum(wxy * along_z, axis=0, keepdims=True))
    return sampled


def total_of(a, b):
    rows = a[0] * b[0] + a[1] * b[1] + a[2] * b[2]
    return jnp.sum(rows, axis=1, keepdims=True)


def in_lanes(values):
    lane = iota((1, 128), 1)
    row = jnp.zeros((1, 128), F32)
    for n, value in enumerate(values):
        row = jnp.where(lane == n, value, row)
    return row


def lane_of(row, n):
    return jnp.sum(jnp.where(iota(row.shape, 1) == n, row, 0.0), axis=1, keepdims=True)


def sample_kernel(t, *refs):
    viscosity, field, beside_z, xl, xu, yl, yu, wxy, wz = refs[0:9]
    me = lax.axis_index("cable")
    last = lax.axis_size("cable") - 1

    def whole(ref):
        if t < 2:
            return [ref[c] for c in range(3)]
        return [ref[c] + coef * ref[3 + c] for c in range(3)]

    if t == 2:
        gram = yl[6] + yu[6] + (refs[10][...] + beside_z[6, 0:8, :])
        square, target = lane_of(gram[0:1], 0), lane_of(gram[0:1], 1)
        coef = -target / (square + (ridge_share * square + 1e-06))
    u = whole(field)
    below = [jnp.where(me > 0, face, 0.0) for face in whole(yl)]
    above = [jnp.where(me < last, face, 0.0) for face in whole(yu)]
    faces = [whole(xl), whole(xu), below, above]
    new = wake(u, whole(beside_z), *faces, viscosity[...])
    if t == 2:
        for c in range(3):
            refs[14][c] = new[c]
        leave = pltpu.make_async_copy(refs[14], refs[11], refs[16])
        leave.start()
    sampled = sample(new, wxy[...], wz[0])
    if t == 0:
        for c in range(3):
            refs[9][:, SLOTS * c : SLOTS * (c + 1)] = jnp.broadcast_to(sampled[c], (HALF, SLOTS))
        return
    aux = refs[9]

    def kept(n):
        return [aux[3 * n + c : 3 * n + c + 1, :] for c in range(3)]

    cr = aux[19:20, :]
    response = [aux[16 + c : 17 + c, :] + cr * sampled[c] for c in range(3)]
    if t == 1:
        msg = refs[10]
        disp, gap0 = kept(0), kept(1)
        gap = [response[c] - disp[c] for c in range(3)]
        v0 = [gap[c] - gap0[c] for c in range(3)]
        for c in range(3):
            msg[:, SLOTS * c : SLOTS * (c + 1)] = jnp.broadcast_to(sampled[c], (HALF, SLOTS))
        row = in_lanes([total_of(v0, v0), total_of(v0, gap)])
        msg[:, 3 * SLOTS : 3 * SLOTS + 128] = jnp.broadcast_to(row, (HALF, 128))
        return
    turn = refs[15]
    latest, change, gap0, gap1, before = (kept(n) for n in range(5))
    disp = [latest[c] + coef * change[c] for c in range(3)]
    gap = [response[c] - disp[c] for c in range(3)]
    v0 = [gap[c] - gap0[c] for c in range(3)]
    v1 = [gap[c] - gap1[c] for c in range(3)]
    row = in_lanes(
        [total_of(v0, v0), total_of(v0, v1), total_of(v1, v1), total_of(v0, gap), total_of(v1, gap)]
    )
    turn[...] = jnp.zeros_like(turn)
    for n, group in enumerate((response, before, latest)):
        for c in range(3):
            turn[3 * n + c : 3 * n + c + 1, :] = group[c][:, :128]
            turn[32 + 3 * n + c : 33 + 3 * n + c, :] = group[c][:, 128:]
    turned = jnp.transpose(turn[...])
    block = turned[0:64] + pltpu.roll(turned[64:128], 16, 1)
    block = block + pltpu.roll(jnp.broadcast_to(row, (8, 128)), 9, 1)[0:1]
    low = lax.axis_index("fz") == 0
    refs[12][...] = jnp.where(low, block[0:HALF], block[HALF:GROUP])
    refs[13][...] = jnp.where(low, block[HALF:GROUP], block[0:HALF])
    leave.wait()


def join_kernel(keep, got, out):
    row = keep[...] + pltpu.roll(got[...], 64, 1)
    for c in range(out.shape[0] // HALF):
        out[HALF * c : HALF * (c + 1), :] = row


def finish_kernel(sent, place, out):
    row = jnp.sum(sent[...], axis=0, keepdims=True)
    row = row + pltpu.roll(jnp.broadcast_to(row, (8, 128)), 64, 1)[0:1]
    g00, g01, g11, b0, b1 = (lane_of(row, 9 + n) for n in range(5))
    shift = ridge_share * (g00 + g11) / 2 + 1e-06
    first, second = g00 + shift, g11 + shift
    determinant = first * second - g01 * g01
    c0 = -(second * b0 - g01 * b1) / determinant
    c1 = -(first * b1 - g01 * b0) / determinant
    start = pl.multiple_of(lax.axis_index("cable") * HALF, HALF)
    mine = sent[pl.ds(start, HALF), :]
    turned = jnp.transpose(jnp.concatenate([mine, jnp.zeros((128 - HALF, 128), F32)], axis=0))
    hot = (iota((128, SEG_DEV), 0).astype(F32) == place[0:1, :]).astype(F32).astype(BF16)
    hi, rest_of = split(turned)
    low = (turned - hi.astype(F32) - rest_of.astype(F32)).astype(BF16)
    got = dot(hi, hot, NN) + (dot(rest_of, hot, NN) + dot(low, hot, NN))
    slot = place[1:2, :]
    rows = jnp.zeros((16, SEG_DEV), F32)
    for k in range(2 * CAP):
        rows = jnp.where(slot == k, got[16 * k : 16 * k + 16], rows)
    response, before, latest = rows[0:3], rows[3:6], rows[6:9]
    out[...] = response + c0 * (response - before) + c1 * (response - latest)


def shape(*dims, kind=F32):
    return jax.ShapeDtypeStruct(dims, kind)


def call(kernel, name, ins, outs, scratch=(), space=pltpu.VMEM, out_space=pltpu.VMEM):
    size = sum(a.size * a.dtype.itemsize for a in (*ins, *outs))
    return pl.pallas_call(
        kernel,
        name=name,
        out_shape=outs,
        in_specs=[pl.BlockSpec(memory_space=space)] * len(ins),
        out_specs=[pl.BlockSpec(memory_space=out_space if n == 0 else pltpu.VMEM) for n in range(len(outs))],
        scratch_shapes=list(scratch),
        compiler_params=pltpu.CompilerParams(vmem_limit_bytes=16 * 1024 * 1024),
        cost_estimate=pl.CostEstimate(flops=0, bytes_accessed=size, transcendentals=0),
    )(*ins)


def shifted(array, axis, by):
    count = lax.axis_size(axis)
    return lax.ppermute(array, axis, [(i, (i + by) % count) for i in range(count)])


def exchange(array, axes):
    return lax.all_to_all(array, axes, 0, 0, tiled=True)


def body(velocity, viscosity, disp_init, rest_shape, compliance, stencil_weights, anchor, owners):
    flow = velocity.reshape(3, XY, SZ)
    thick = viscosity.reshape(XY, SZ)
    ins = (disp_init, rest_shape, compliance.reshape(1, SEG_DEV), stencil_weights, anchor, owners)
    keep, give, place, xlo, xhi = call(
        pack_kernel,
        "pack",
        tuple(pltpu.with_memory_space_constraint(a, pltpu.HBM) for a in (*ins, flow)),
        [shape(HALF, FIELDS), shape(HALF, FIELDS), shape(8, SEG_DEV), shape(3, SY, SZ), shape(3, SY, SZ)],
        [pltpu.VMEM(a.shape, a.dtype) for a in ins]
        + [pltpu.VMEM((24, SEG_DEV), F32), pltpu.VMEM((FIELDS, 128), F32), pltpu.SemaphoreType.DMA((8,))],
        pltpu.HBM,
    )
    static = exchange(jnp.concatenate([keep, shifted(give, "fz", 1)], axis=1), "fx")
    far_l, far_u = shifted(xhi, "fx", 1), shifted(xlo, "fx", -1)
    table_outs = [
        shape(XY, SLOTS),
        shape(SETS, 2 * SZ, SLOTS, kind=BF16),
        shape(2, SY, SLOTS),
        shape(32 * SETS, SLOTS),
    ]
    turned = [pltpu.VMEM((FIELDS, 128), F32)]
    sent, tabled = (), ()
    for t in range(3):
        n = 6 if t == 2 else 3
        planes = 7 if t == 2 else 3
        faced = 7 if t == 2 else 3
        outs = [shape(planes, XY, SZ), shape(n, SY, SZ), shape(n, SY, SZ)] + [shape(faced, SX, SZ)] * 2
        kernel, name = functools.partial(spread_kernel, t), f"spread{t}"
        if t == 0:
            field, xl, xu, ylo, yhi, *tabled = call(
                kernel, name, (static, flow, far_l, far_u), outs + table_outs, turned
            )
            extra = []
        else:
            outs.append(shape(24, SLOTS))
            if t == 2:
                outs.append(shape(8, 128))
            field, xl, xu, ylo, yhi, *extra = call(
                kernel, name, (flow, far_l, far_u, *sent, *tabled, *across), outs
            )
        ins = [thick, field, shifted(field, "fz", 1), xl, xu]
        ins += [shifted(yhi, "cable", 1), shifted(ylo, "cable", -1), *tabled[0:2], *extra]
        if t < 2:
            tabled = call(
                functools.partial(prepare_kernel, t + 1),
                f"prepare{t + 1}",
                (static, *sent),
                table_outs,
                turned,
            )
        kernel, name = functools.partial(sample_kernel, t), f"sample{t}"
        if t < 2:
            (msg,) = call(kernel, name, ins, [shape(HALF, 3 * SLOTS + (128 if t else 0))])
            half = exchange(msg, "fx")
            sent, across = (half, shifted(half, "fz", 1)), ()
            if t == 1:
                (gram,) = call(part_gram_kernel, "gram", (half,), [shape(8, 128)])
                across = (shifted(gram, "cable", 2),)
        else:
            out, keep, give = call(
                kernel,
                name,
                ins,
                [shape(3, XY, SZ), shape(HALF, 128), shape(HALF, 128)],
                [pltpu.VMEM((3, XY, SZ), F32), pltpu.VMEM((128, 128), F32), pltpu.SemaphoreType.DMA(())],
                out_space=pltpu.HBM,
            )
    cables = lax.axis_size("cable")
    (msg,) = call(join_kernel, "join", (keep, shifted(give, "fz", 1)), [shape(cables * HALF, 128)])
    last = exchange(msg, ("cable", "fx"))
    (disp_next,) = call(finish_kernel, "finish", (last, place), [shape(3, SEG_DEV)])
    return disp_next, out.reshape(velocity.shape)


def solution(mesh):
    segments = ("cable", "fx", "fz")
    placed = (
        P(None, "fx", "cable", "fz"),
        P("fx", "cable", "fz"),
        P(None, segments),
        P(None, segments),
        P(segments),
        P(None, None, segments),
        P(None, segments),
        P(None, segments),
    )
    return jax.shard_map(
        body,
        mesh=mesh,
        in_specs=placed,
        out_specs=(P(None, segments), P(None, "fx", "cable", "fz")),
        check_vma=False,
    )
```

```python
import functools
import math

import jax
import jax.numpy as jnp
from jax import lax
from jax.experimental import pallas as pl
from jax.experimental.pallas import tpu as pltpu
from jax.sharding import PartitionSpec as P


F32 = jnp.float32
BF16 = jnp.bfloat16
NT = (((1,), (1,)), ((), ()))
NN = (((1,), (0,)), ((), ()))

spread_gain = 16.0
drag_coeff = 0.05
relaxation = 0.5
ridge_share = 0.01

SEG_DEV = 64
GROUP = 64
CAP = 4
HALF = GROUP // 2
SLOTS = GROUP * CAP
SX, SY, SZ = 8, 16, 128
XY = SX * SY

R_W, R_CELL, R_D0, R_REST, R_CR, R_CODE = 0, 12, 13, 16, 19, 20
HEIGHT = (16, 24, 24)
SETS = 3
BASE = (0, 0, 288)
EARLY, LATE = 256, 640


def split(x):
    hi = x.astype(BF16)
    return hi, (x - hi.astype(F32)).astype(BF16)


def dot(a, b, dims):
    return lax.dot_general(a, b, dims, preferred_element_type=F32)


def iota(shape, dim):
    return lax.broadcasted_iota(jnp.int32, shape, dim)


def split3(x):
    hi, low = split(x)
    return hi, low, (x - hi.astype(F32) - low.astype(F32)).astype(BF16)


def rank_of(own):
    hot = (iota((GROUP, SEG_DEV), 0) == own).astype(F32)
    earlier = (iota((SEG_DEV, SEG_DEV), 0) < iota((SEG_DEV, SEG_DEV), 1)).astype(F32)
    return jnp.sum(hot * dot(hot, earlier, NN), axis=0, keepdims=True)


def put_slots(fields, rank, rows, turn, base):
    height = fields.shape[0]
    parts = split3(jnp.concatenate([jnp.where(rank == k, fields, 0.0) for k in range(CAP)], axis=0))
    dest = iota((GROUP, SEG_DEV), 0)
    hots = jnp.concatenate([(dest == row).astype(F32).astype(BF16) for row in rows], axis=0)
    got = dot(parts[0], hots, NT) + (dot(parts[1], hots, NT) + dot(parts[2], hots, NT))
    for j in range(SETS):
        start = base + CAP * height * j
        turn[start : start + CAP * height, 0:GROUP] = got[:, GROUP * j : GROUP * (j + 1)]


def pack_kernel(*refs):
    far, (msg, later, firsts, xlo, xhi), near, (turn, sems) = refs[0:7], refs[7:12], refs[12:18], refs[18:20]
    copies = [pltpu.make_async_copy(far[n], near[n], sems.at[n]) for n in (5, 4, 3, 0, 1, 2)]
    copies.append(pltpu.make_async_copy(far[6].at[:, 0:SY, :], xlo, sems.at[6]))
    copies.append(pltpu.make_async_copy(far[6].at[:, XY - SY : XY, :], xhi, sems.at[7]))
    for copy in copies:
        copy.start()
    disp, rest, comp, weights, anchor, owner = near
    fz_n, fx_n, cable_n = lax.axis_size("fz"), lax.axis_size("fx"), lax.axis_size("cable")
    device = (lax.axis_index("cable") * fx_n + lax.axis_index("fx")) * fz_n + lax.axis_index("fz")
    position = (device * SEG_DEV + iota((1, SEG_DEV), 1)).astype(F32)
    ramp = 1.0 + 2.0 * position / (SEG_DEV * fz_n * fx_n * cable_n)
    later[...] = jnp.zeros_like(later)
    firsts[...] = jnp.zeros_like(firsts)
    turn[...] = jnp.zeros_like(turn)
    for copy in copies:
        copy.wait()
    own = owner[0:1, :]
    rank = rank_of(own)
    firsts[0:12, :] = weights[0]
    firsts[R_CELL : R_CELL + 1, :] = anchor[0:1, :].astype(F32)
    firsts[R_D0 : R_D0 + 3, :] = disp[...]
    put_slots(firsts[0 : HEIGHT[0], :], rank, (own, own + fz_n, own - fz_n), turn, BASE[0])
    for n in range(EARLY // 128):
        msg[:, 128 * n : 128 * n + 128] = jnp.transpose(turn[128 * n : 128 * n + 128, :])[0:GROUP]
    for t in (1, 2):
        at = 24 * (t - 1)
        later[at : at + 12, :] = weights[t]
        later[at + R_CELL : at + R_CELL + 1, :] = anchor[t : t + 1, :].astype(F32)
        later[at + R_D0 : at + R_D0 + 3, :] = disp[...]
        later[at + R_REST : at + R_REST + 3, :] = rest[...]
        later[at + R_CR : at + R_CR + 1, :] = comp[...] * ramp
    later[48:51, :] = owner[...].astype(F32)
    later[51:52, :] = rank


def pack_later_kernel(later, keep, give, place, turn):
    mine = lax.axis_index("fz")
    turn[...] = jnp.zeros_like(turn)
    owners = [later[48 + t : 49 + t, :].astype(jnp.int32) for t in range(3)]
    ranks = [later[51:52, :], rank_of(owners[1]), rank_of(owners[2])]
    codes = [owners[t].astype(F32) * CAP + ranks[t] for t in range(2)]
    code = codes[0] + SLOTS * codes[1]
    for t in (1, 2):
        side, fx = (owners[t] & 1) ^ mine, owners[t] >> 1
        at = side * HALF + fx
        rows = (at, jnp.where(fx < HALF - 1, at + 1, -1), jnp.where(fx > 0, at - 1, -1))
        fields = later[24 * (t - 1) : 24 * t, :]
        fields = jnp.where(iota((24, SEG_DEV), 0) == R_CODE, code, fields)
        put_slots(fields, ranks[t], rows, turn, BASE[t])
    for n in range(LATE // 128):
        lanes = slice(128 * n, 128 * n + 128)
        block = jnp.transpose(turn[lanes, :])
        keep[:, lanes] = block[0:HALF]
        give[:, lanes] = block[HALF:GROUP]
    place[...] = jnp.zeros_like(place)
    place[0:1, :] = later[50:51, :]
    place[1:2, :] = ranks[2]


def turn_static(static, turned, t):
    first = BASE[t] // 128
    last = (BASE[t] + SETS * CAP * HEIGHT[t] + 127) // 128
    low = lax.axis_index("fz") == 0
    for n in range(first, last):
        if t == 0:
            spare = LATE - GROUP
            turned[spare:LATE, :] = static[:, 128 * n : 128 * n + 128]
            homes = [turned[pl.ds(spare + f, HALF, stride=2), :] for f in range(2)]
        else:
            at = 3 * SLOTS + 128 * n
            same, other = static[:, at : at + 128], static[:, at + LATE : at + LATE + 128]
            homes = [jnp.where(low, same, other), jnp.where(low, other, same)]
        wide = jnp.concatenate([*homes, jnp.zeros((128 - GROUP, 128), F32)], axis=0)
        turned[128 * n : 128 * n + 128, :] = jnp.transpose(wide)


def slot_rows(turned, t, j):
    height = HEIGHT[t]
    start = BASE[t] + CAP * height * j
    part = [turned[start + height * k : start + height * (k + 1), :] for k in range(CAP)]
    halves = [part[2 * n] + pltpu.roll(part[2 * n + 1], 64, 1) for n in range(2)]
    return jnp.concatenate(halves, axis=1)


def along(rows, first, at):
    total = jnp.zeros(at.shape, F32)
    for i in range(4):
        total = jnp.where(at == i, rows[first + i : first + i + 1], total)
    return total


def tables(rows, plane=None):
    cell = rows[R_CELL : R_CELL + 1].astype(jnp.int32)
    wy = along(rows, R_W + 4, iota((SY, SLOTS), 0) - ((cell >> 7) & (SY - 1)))
    wz = along(rows, R_W + 8, iota((SZ, SLOTS), 0) - (cell & (SZ - 1)))
    if plane is not None:
        return along(rows, R_W, plane - (cell >> 11)) * wy, wz
    wx = along(rows, R_W, iota((SX, SLOTS), 0) - (cell >> 11))
    return jnp.concatenate([wx[x : x + 1] * wy for x in range(SX)], axis=0), wz


def spread(wxy, wz2, base):
    hi, low = split(jnp.concatenate([wxy * (spread_gain * base[c]) for c in range(3)], axis=0))
    both = dot(hi, wz2, NT)
    return both[:, :SZ] + (both[:, SZ:] + dot(low, wz2[0:SZ], NT))


def look_up(halves, code):
    low_half = iota((1, 128), 1) < 64
    mine = lax.axis_index("fz")
    height = HALF
    label = (iota((height, SLOTS), 0) * 2 + mine) * CAP + iota((height, SLOTS), 1) // 64
    labels = (label, label + CAP * (1 - 2 * mine))
    found = [[None] * 2 for _ in range(3)]
    for part in range(2):
        piece = code[:, 128 * part : 128 * part + 128]
        turned = pltpu.roll(piece, 64, 1)
        pair = []
        for odd in range(2):
            both = jnp.where(low_half, turned, piece) if odd else jnp.where(low_half, piece, turned)
            wanted = jnp.concatenate([both, both], axis=1)
            per = []
            for comp in range(3):
                lanes = slice(comp * SLOTS, (comp + 1) * SLOTS)
                hit = jnp.where(labels[0] == wanted, halves[0][:, lanes], 0.0)
                hit = hit + jnp.where(labels[1] == wanted, halves[1][:, lanes], 0.0)
                hit = jnp.sum(hit, axis=0, keepdims=True)
                hit = hit[:, :128] + hit[:, 128:]
                per.append(hit + pltpu.roll(hit, 64, 1))
            pair.append(per)
        for comp in range(3):
            found[comp][part] = jnp.where(low_half, pair[0][comp], pair[1][comp])
    return [jnp.concatenate(found[comp], axis=1) for comp in range(3)]


def responses(rows, sampled):
    cr = rows[R_CR : R_CR + 1]
    return [rows[R_REST + c : R_REST + c + 1] + cr * sampled[c] for c in range(3)]


def prepare_kernel(t, *refs):
    static, sent, (wxy_out, wz_out, plane_out, slots, turned) = refs[0], refs[1:-5], refs[-5:]
    turn_static(static, turned, t)
    for j in range(SETS):
        rows = slot_rows(turned, t, j)
        wxy, wz = tables(rows, (None, SX - 1, 0)[j])
        hi, low = split(wz)
        wz_out[j, 0:SZ, :] = hi
        wz_out[j, SZ:, :] = low
        if j == 0:
            wxy_out[...] = wxy
        else:
            plane_out[j - 1] = wxy
        slots[32 * j : 32 * j + HEIGHT[t], :] = rows
        if t == 2:
            code = rows[R_CODE : R_CODE + 1].astype(jnp.int32)
            before = responses(rows, look_up(sent, code & (SLOTS - 1)))
            for c in range(3):
                slots[32 * j + 24 + c : 32 * j + 25 + c, :] = before[c]


def displacements(t, rows, sent):
    first = [rows[R_D0 + c : R_D0 + c + 1] for c in range(3)]
    if t == 0:
        return [first], []
    code = rows[R_CODE : R_CODE + 1].astype(jnp.int32)
    if t == 1:
        before = responses(rows, look_up(sent, code & (SLOTS - 1)))
    else:
        before = [rows[24 + c : 25 + c] for c in range(3)]
    gap = [before[c] - first[c] for c in range(3)]
    second = [first[c] + relaxation * gap[c] for c in range(3)]
    if t == 1:
        return [second], [second, gap]
    latest = responses(rows, look_up(sent, code >> 8))
    change = [latest[c] - before[c] for c in range(3)]
    return [latest, change], [latest, change, gap, [latest[c] - second[c] for c in range(3)], before]


def spread_kernel(t, *refs):
    if t == 0:
        static, velocity, far_l, far_u = refs[0:4]
        sent = ()
        field, xl, xu, ylo, yhi, *tabled, turned = refs[4:]
        prepare_kernel(0, static, *tabled, turned)
    else:
        velocity, far_l, far_u = refs[0:3]
        sent, tabled = refs[3:5], refs[5:9]
        field, xl, xu, ylo, yhi, aux = refs[9:15]
        aux[...] = jnp.zeros_like(aux)
    wxy, wz, plane, slots = tabled
    fx = lax.axis_index("fx")
    inside = (None, fx > 0, fx < lax.axis_size("fx") - 1)
    for j, out in enumerate((field, xl, xu)):
        rows = slots[32 * j : 32 * j + 32, :]
        bases, kept = displacements(t, rows, sent)
        height = SY if j else XY
        for n, base in enumerate(bases):
            forced = spread(plane[j - 1] if j else wxy[...], wz[j], base)
            for c in range(3):
                part = forced[height * c : height * (c + 1)]
                if n == 0 and j == 0:
                    part = part + velocity[c]
                elif n == 0:
                    part = part + jnp.where(inside[j], (far_l, far_u)[j - 1][c], 0.0)
                out[3 * n + c] = part
        if j == 0 and t > 0:
            for n, group in enumerate(kept):
                for c in range(3):
                    aux[3 * n + c : 3 * n + c + 1, :] = group[c]
            aux[16:20, :] = rows[R_REST : R_REST + 4]
    for n in range(3 * len(bases)):
        ylo[n] = field[n, pl.ds(0, SX, stride=SY), :]
        yhi[n] = field[n, pl.ds(SY - 1, SX, stride=SY), :]
    if t == 2:
        lanes = slice(3 * SLOTS, 3 * SLOTS + 128)
        total = jnp.sum(sent[0][:, lanes] + sent[1][:, lanes], axis=0, keepdims=True)
        total = jnp.broadcast_to(total, (8, 128))
        ylo[6] = total
        yhi[6] = total
        refs[15][...] = total


def wake(u, beside_z, xl, xu, yl, yu, viscosity):
    lane = iota((XY, SZ), 1)
    y = iota((XY, SZ), 0) % SY
    upper_core = lax.axis_index("fz") > 0
    speed = jnp.sqrt(1.0 + (u[0] * u[0] + u[1] * u[1] + u[2] * u[2]))
    new = []
    for c in range(3):
        here = u[c]
        near = jnp.concatenate([xl[c], here[: XY - SY]], axis=0)
        near = near + jnp.concatenate([here[SY:], xu[c]], axis=0)
        wide_l = jnp.concatenate([jnp.broadcast_to(yl[c][x : x + 1], (SY, SZ)) for x in range(SX)], axis=0)
        wide_u = jnp.concatenate([jnp.broadcast_to(yu[c][x : x + 1], (SY, SZ)) for x in range(SX)], axis=0)
        near = near + jnp.where(y == 0, wide_l, pltpu.roll(here, 1, 0))
        near = near + jnp.where(y == SY - 1, wide_u, pltpu.roll(here, XY - 1, 0))
        left = jnp.where(upper_core, beside_z[c], 0.0)
        right = jnp.where(upper_core, 0.0, beside_z[c])
        near = near + pltpu.roll(jnp.where(lane == SZ - 1, left, here), 1, 1)
        near = near + pltpu.roll(jnp.where(lane == 0, right, here), SZ - 1, 1)
        new.append(here + viscosity * (near - 6.0 * here) - drag_coeff * here * speed)
    return new


def sample(new, wxy, wz2):
    wz_hi, wz_low = wz2[0:SZ], wz2[SZ:]
    both = jnp.concatenate([wz_hi, wz_hi], axis=0)
    sampled = []
    for c in range(3):
        hi, low = split(new[c])
        along_z = dot(jnp.concatenate([hi, low], axis=1), both, NN) + dot(hi, wz_low, NN)
        sampled.append(jnp.sum(wxy * along_z, axis=0, keepdims=True))
    return sampled


def total_of(a, b):
    rows = a[0] * b[0] + a[1] * b[1] + a[2] * b[2]
    return jnp.sum(rows, axis=1, keepdims=True)


def in_lanes(values):
    lane = iota((1, 128), 1)
    row = jnp.zeros((1, 128), F32)
    for n, value in enumerate(values):
        row = jnp.where(lane == n, value, row)
    return row


def lane_of(row, n):
    return jnp.sum(jnp.where(iota(row.shape, 1) == n, row, 0.0), axis=1, keepdims=True)


def sample_kernel(t, *refs):
    viscosity, field, beside_z, xl, xu, yl, yu, wxy, wz = refs[0:9]
    me = lax.axis_index("cable")
    last = lax.axis_size("cable") - 1

    def whole(ref):
        if t < 2:
            return [ref[c] for c in range(3)]
        return [ref[c] + coef * ref[3 + c] for c in range(3)]

    if t == 2:
        gram = yl[6] + yu[6] + (refs[10][...] + refs[11][...])
        square, target = lane_of(gram[0:1], 0), lane_of(gram[0:1], 1)
        coef = -target / (square + (ridge_share * square + 1e-06))
    u = whole(field)
    below = [jnp.where(me > 0, face, 0.0) for face in whole(yl)]
    above = [jnp.where(me < last, face, 0.0) for face in whole(yu)]
    faces = [whole(xl), whole(xu), below, above]
    new = wake(u, whole(beside_z), *faces, viscosity[...])
    sampled = sample(new, wxy[...], wz[0])
    if t == 0:
        keep, got, msg = refs[9:12]
        for c in range(3):
            msg[:, SLOTS * c : SLOTS * (c + 1)] = jnp.broadcast_to(sampled[c], (HALF, SLOTS))
        msg[:, 3 * SLOTS : 3 * SLOTS + LATE] = keep[...]
        msg[:, 3 * SLOTS + LATE :] = got[...]
        return
    aux = refs[9]

    def kept(n):
        return [aux[3 * n + c : 3 * n + c + 1, :] for c in range(3)]

    cr = aux[19:20, :]
    response = [aux[16 + c : 17 + c, :] + cr * sampled[c] for c in range(3)]
    if t == 1:
        msg = refs[10]
        disp, gap0 = kept(0), kept(1)
        gap = [response[c] - disp[c] for c in range(3)]
        v0 = [gap[c] - gap0[c] for c in range(3)]
        for c in range(3):
            msg[:, SLOTS * c : SLOTS * (c + 1)] = jnp.broadcast_to(sampled[c], (HALF, SLOTS))
        row = in_lanes([total_of(v0, v0), total_of(v0, gap)])
        msg[:, 3 * SLOTS : 3 * SLOTS + 128] = jnp.broadcast_to(row, (HALF, 128))
        return
    out, msg, turn = refs[12:15]
    for c in range(3):
        out[c] = new[c]
    latest, change, gap0, gap1, before = (kept(n) for n in range(5))
    disp = [latest[c] + coef * change[c] for c in range(3)]
    gap = [response[c] - disp[c] for c in range(3)]
    v0 = [gap[c] - gap0[c] for c in range(3)]
    v1 = [gap[c] - gap1[c] for c in range(3)]
    row = in_lanes(
        [total_of(v0, v0), total_of(v0, v1), total_of(v1, v1), total_of(v0, gap), total_of(v1, gap)]
    )
    turn[...] = jnp.zeros_like(turn)
    for n, group in enumerate((response, before, latest)):
        for c in range(3):
            turn[3 * n + c : 3 * n + c + 1, :] = group[c][:, :128]
            turn[32 + 3 * n + c : 33 + 3 * n + c, :] = group[c][:, 128:]
    turned = jnp.transpose(turn[...])
    block = turned[0:64] + pltpu.roll(turned[64:128], 16, 1)
    block = block + pltpu.roll(jnp.broadcast_to(row, (8, 128)), 64, 1)[0:1]
    for c in range(4):
        for f in range(2):
            msg[pl.ds(GROUP * c + f, HALF, stride=2), :] = block[HALF * f : HALF * (f + 1)]


def finish_kernel(sent, place, out):
    row = jnp.sum(sent[...], axis=0, keepdims=True)
    g00, g01, g11, b0, b1 = (lane_of(row, 64 + n) for n in range(5))
    shift = ridge_share * (g00 + g11) / 2 + 1e-06
    first, second = g00 + shift, g11 + shift
    determinant = first * second - g01 * g01
    c0 = -(second * b0 - g01 * b1) / determinant
    c1 = -(first * b1 - g01 * b0) / determinant
    start = pl.multiple_of(lax.axis_index("cable") * GROUP, GROUP)
    mine = sent[pl.ds(start, GROUP), :]
    turned = jnp.transpose(jnp.concatenate([mine, jnp.zeros((128 - GROUP, 128), F32)], axis=0))
    hot = (iota((128, SEG_DEV), 0).astype(F32) == place[0:1, :]).astype(F32).astype(BF16)
    parts = split3(turned[0:64])
    got = dot(parts[0], hot, NN) + (dot(parts[1], hot, NN) + dot(parts[2], hot, NN))
    rank = place[1:2, :]
    rows = jnp.zeros((16, SEG_DEV), F32)
    for k in range(CAP):
        rows = jnp.where(rank == k, got[16 * k : 16 * k + 16], rows)
    response, before, latest = rows[0:3], rows[3:6], rows[6:9]
    out[...] = response + c0 * (response - before) + c1 * (response - latest)


def shape(*dims, kind=F32):
    return jax.ShapeDtypeStruct(dims, kind)


def call(kernel, name, ins, outs, scratch=(), space=pltpu.VMEM):
    size = sum(a.size * a.dtype.itemsize for a in (*ins, *outs))
    return pl.pallas_call(
        kernel,
        name=name,
        out_shape=outs,
        in_specs=[pl.BlockSpec(memory_space=space)] * len(ins),
        out_specs=[pl.BlockSpec(memory_space=pltpu.VMEM)] * len(outs),
        scratch_shapes=list(scratch),
        compiler_params=pltpu.CompilerParams(vmem_limit_bytes=16 * 1024 * 1024),
        cost_estimate=pl.CostEstimate(flops=0, bytes_accessed=size, transcendentals=0),
    )(*ins)


def shifted(array, axis, by):
    count = lax.axis_size(axis)
    return lax.ppermute(array, axis, [(i, (i + by) % count) for i in range(count)])


def exchange(array, axes):
    return lax.all_to_all(array, axes, 0, 0, tiled=True)


def body(velocity, viscosity, disp_init, rest_shape, compliance, stencil_weights, anchor, owners):
    flow = velocity.reshape(3, XY, SZ)
    thick = viscosity.reshape(XY, SZ)
    ins = (disp_init, rest_shape, compliance.reshape(1, SEG_DEV), stencil_weights, anchor, owners)
    msg, later, _, xlo, xhi = call(
        pack_kernel,
        "pack",
        tuple(pltpu.with_memory_space_constraint(a, pltpu.HBM) for a in (*ins, flow)),
        [shape(GROUP, EARLY), shape(56, SEG_DEV), shape(24, SEG_DEV), shape(3, SY, SZ), shape(3, SY, SZ)],
        [pltpu.VMEM(a.shape, a.dtype) for a in ins]
        + [pltpu.VMEM((EARLY, 128), F32), pltpu.SemaphoreType.DMA((8,))],
        pltpu.HBM,
    )
    static = exchange(msg, ("fx", "fz"))
    keep, give, place = call(
        pack_later_kernel,
        "pack_later",
        (later,),
        [shape(HALF, LATE), shape(HALF, LATE), shape(8, SEG_DEV)],
        [pltpu.VMEM((LATE, 128), F32)],
    )
    static, *carried = lax.optimization_barrier((static, keep, shifted(give, "fz", 1)))
    far_l, far_u = shifted(xhi, "fx", 1), shifted(xlo, "fx", -1)
    table_outs = [
        shape(XY, SLOTS),
        shape(SETS, 2 * SZ, SLOTS, kind=BF16),
        shape(2, SY, SLOTS),
        shape(32 * SETS, SLOTS),
    ]
    turned = [pltpu.VMEM((LATE, 128), F32)]
    sent, tabled = (), ()
    for t in range(3):
        n = 6 if t == 2 else 3
        faced = 7 if t == 2 else 3
        outs = [shape(n, XY, SZ), shape(n, SY, SZ), shape(n, SY, SZ)] + [shape(faced, SX, SZ)] * 2
        kernel, name = functools.partial(spread_kernel, t), f"spread{t}"
        if t == 0:
            field, xl, xu, ylo, yhi, *tabled = call(
                kernel, name, (static, flow, far_l, far_u), outs + table_outs, turned
            )
            extra = []
        else:
            outs.append(shape(24, SLOTS))
            if t == 2:
                outs.append(shape(8, 128))
            field, xl, xu, ylo, yhi, *extra = call(
                kernel, name, (flow, far_l, far_u, *sent, *tabled), outs
            )
        ins = [thick, field, shifted(field, "fz", 1), xl, xu]
        ins += [shifted(yhi, "cable", 1), shifted(ylo, "cable", -1), *tabled[0:2], *extra]
        kernel, name = functools.partial(sample_kernel, t), f"sample{t}"
        if t < 2:
            if t == 0:
                ins += carried
            (msg,) = call(kernel, name, ins, [shape(HALF, 3 * SLOTS + (128 if t else 2 * LATE))])
            half = exchange(msg, "fx")
            if t == 0:
                static, before = half, ()
            sent = (half, shifted(half if t else half[:, : 3 * SLOTS], "fz", 1))
            tabled = call(
                functools.partial(prepare_kernel, t + 1), f"prepare{t + 1}", (static, *before), table_outs, turned
            )
            before = sent
        else:
            ins.append(shifted(extra[1], "cable", 2))
            out, msg = call(
                kernel, name, ins, [shape(3, XY, SZ), shape(4 * GROUP, 128)], [pltpu.VMEM((128, 128), F32)]
            )
    last = exchange(msg, ("cable", "fx", "fz"))
    (disp_next,) = call(finish_kernel, "finish", (last, place), [shape(3, SEG_DEV)])
    return disp_next, out.reshape(velocity.shape)


def solution(mesh):
    segments = ("cable", "fx", "fz")
    placed = (
        P(None, "fx", "cable", "fz"),
        P("fx", "cable", "fz"),
        P(None, segments),
        P(None, segments),
        P(segments),
        P(None, None, segments),
        P(None, segments),
        P(None, segments),
    )
    return jax.shard_map(
        body,
        mesh=mesh,
        in_specs=placed,
        out_specs=(P(None, segments), P(None, "fx", "cable", "fz")),
        check_vma=False,
    )
```

```python
import functools

import jax
import jax.numpy as jnp
from jax import lax
from jax.experimental import pallas as pl
from jax.experimental.pallas import tpu as pltpu
from jax.sharding import PartitionSpec as P


F32 = jnp.float32
BF16 = jnp.bfloat16
NT = (((1,), (1,)), ((), ()))
NN = (((1,), (0,)), ((), ()))

spread_gain = 16.0
drag_coeff = 0.05
relaxation = 0.5
ridge_share = 0.01

SEG_DEV = 64
GROUP = 64
CAP = 4
HALF = GROUP // 2
SLOTS = GROUP * CAP
SX, SY, SZ = 8, 16, 128
XY = SX * SY

R_W, R_CELL, R_D0, R_REST, R_CR, R_CODE = 0, 12, 13, 16, 19, 20
HEIGHT = (16, 24, 24)
SETS = 3
BASE = (0, 0, 288)
EARLY, LATE = 256, 640


def split(x):
    hi = x.astype(BF16)
    return hi, (x - hi.astype(F32)).astype(BF16)


def dot(a, b, dims):
    return lax.dot_general(a, b, dims, preferred_element_type=F32)


def iota(shape, dim):
    return lax.broadcasted_iota(jnp.int32, shape, dim)


def split3(x):
    hi, low = split(x)
    return hi, low, (x - hi.astype(F32) - low.astype(F32)).astype(BF16)


def rank_of(own):
    hot = (iota((GROUP, SEG_DEV), 0) == own).astype(F32)
    earlier = (iota((SEG_DEV, SEG_DEV), 0) < iota((SEG_DEV, SEG_DEV), 1)).astype(F32)
    return jnp.sum(hot * dot(hot, earlier, NN), axis=0, keepdims=True)


def put_slots(fields, rank, rows, turn, base):
    height = fields.shape[0]
    parts = split3(jnp.concatenate([jnp.where(rank == k, fields, 0.0) for k in range(CAP)], axis=0))
    dest = iota((GROUP, SEG_DEV), 0)
    hots = jnp.concatenate([(dest == row).astype(F32).astype(BF16) for row in rows], axis=0)
    got = dot(parts[0], hots, NT) + (dot(parts[1], hots, NT) + dot(parts[2], hots, NT))
    for j in range(SETS):
        start = base + CAP * height * j
        turn[start : start + CAP * height, 0:GROUP] = got[:, GROUP * j : GROUP * (j + 1)]


def pack_kernel(*refs):
    far, (msg, later, firsts, xlo, xhi), near, (turn, sems) = refs[0:7], refs[7:12], refs[12:18], refs[18:20]
    copies = [pltpu.make_async_copy(far[n], near[n], sems.at[n]) for n in (5, 4, 3, 0, 1, 2)]
    copies.append(pltpu.make_async_copy(far[6].at[:, 0:SY, :], xlo, sems.at[6]))
    copies.append(pltpu.make_async_copy(far[6].at[:, XY - SY : XY, :], xhi, sems.at[7]))
    for copy in copies:
        copy.start()
    disp, rest, comp, weights, anchor, owner = near
    fz_n, fx_n, cable_n = lax.axis_size("fz"), lax.axis_size("fx"), lax.axis_size("cable")
    device = (lax.axis_index("cable") * fx_n + lax.axis_index("fx")) * fz_n + lax.axis_index("fz")
    position = (device * SEG_DEV + iota((1, SEG_DEV), 1)).astype(F32)
    ramp = 1.0 + 2.0 * position / (SEG_DEV * fz_n * fx_n * cable_n)
    later[...] = jnp.zeros_like(later)
    firsts[...] = jnp.zeros_like(firsts)
    turn[...] = jnp.zeros_like(turn)
    for copy in copies:
        copy.wait()
    own = owner[0:1, :]
    rank = rank_of(own)
    firsts[0:12, :] = weights[0]
    firsts[R_CELL : R_CELL + 1, :] = anchor[0:1, :].astype(F32)
    firsts[R_D0 : R_D0 + 3, :] = disp[...]
    put_slots(firsts[0 : HEIGHT[0], :], rank, (own, own + fz_n, own - fz_n), turn, BASE[0])
    for n in range(EARLY // 128):
        msg[:, 128 * n : 128 * n + 128] = jnp.transpose(turn[128 * n : 128 * n + 128, :])[0:GROUP]
    for t in (1, 2):
        at = 24 * (t - 1)
        later[at : at + 12, :] = weights[t]
        later[at + R_CELL : at + R_CELL + 1, :] = anchor[t : t + 1, :].astype(F32)
        later[at + R_D0 : at + R_D0 + 3, :] = disp[...]
        later[at + R_REST : at + R_REST + 3, :] = rest[...]
        later[at + R_CR : at + R_CR + 1, :] = comp[...] * ramp
    later[48:51, :] = owner[...].astype(F32)
    later[51:52, :] = rank


def pack_later_kernel(later, keep, give, place, turn):
    mine = lax.axis_index("fz")
    turn[...] = jnp.zeros_like(turn)
    owners = [later[48 + t : 49 + t, :].astype(jnp.int32) for t in range(3)]
    ranks = [later[51:52, :], rank_of(owners[1]), rank_of(owners[2])]
    codes = [owners[t].astype(F32) * CAP + ranks[t] for t in range(2)]
    code = codes[0] + SLOTS * codes[1]
    for t in (1, 2):
        side, fx = (owners[t] & 1) ^ mine, owners[t] >> 1
        at = side * HALF + fx
        rows = (at, jnp.where(fx < HALF - 1, at + 1, -1), jnp.where(fx > 0, at - 1, -1))
        fields = later[24 * (t - 1) : 24 * t, :]
        fields = jnp.where(iota((24, SEG_DEV), 0) == R_CODE, code, fields)
        put_slots(fields, ranks[t], rows, turn, BASE[t])
    for n in range(LATE // 128):
        lanes = slice(128 * n, 128 * n + 128)
        block = jnp.transpose(turn[lanes, :])
        keep[:, lanes] = block[0:HALF]
        give[:, lanes] = block[HALF:GROUP]
    place[...] = jnp.zeros_like(place)
    place[0:1, :] = later[50:51, :]
    place[1:2, :] = ranks[2]


def turn_static(static, turned, t):
    first = BASE[t] // 128
    last = (BASE[t] + SETS * CAP * HEIGHT[t] + 127) // 128
    low = lax.axis_index("fz") == 0
    for n in range(first, last):
        if t == 0:
            spare = LATE - GROUP
            turned[spare:LATE, :] = static[:, 128 * n : 128 * n + 128]
            homes = [turned[pl.ds(spare + f, HALF, stride=2), :] for f in range(2)]
        else:
            at = 3 * SLOTS + 128 * n
            same, other = static[:, at : at + 128], static[:, at + LATE : at + LATE + 128]
            homes = [jnp.where(low, same, other), jnp.where(low, other, same)]
        wide = jnp.concatenate([*homes, jnp.zeros((128 - GROUP, 128), F32)], axis=0)
        turned[128 * n : 128 * n + 128, :] = jnp.transpose(wide)


def slot_rows(turned, t, j):
    height = HEIGHT[t]
    start = BASE[t] + CAP * height * j
    part = [turned[start + height * k : start + height * (k + 1), :] for k in range(CAP)]
    halves = [part[2 * n] + pltpu.roll(part[2 * n + 1], 64, 1) for n in range(2)]
    return jnp.concatenate(halves, axis=1)


def along(rows, first, at):
    total = jnp.zeros(at.shape, F32)
    for i in range(4):
        total = jnp.where(at == i, rows[first + i : first + i + 1], total)
    return total


def tables(rows, plane=None):
    cell = rows[R_CELL : R_CELL + 1].astype(jnp.int32)
    wy = along(rows, R_W + 4, iota((SY, SLOTS), 0) - ((cell >> 7) & (SY - 1)))
    wz = along(rows, R_W + 8, iota((SZ, SLOTS), 0) - (cell & (SZ - 1)))
    if plane is not None:
        return along(rows, R_W, plane - (cell >> 11)) * wy, wz
    wx = along(rows, R_W, iota((SX, SLOTS), 0) - (cell >> 11))
    return jnp.concatenate([wx[x : x + 1] * wy for x in range(SX)], axis=0), wz


def spread(wxy, wz2, base):
    hi, low = split(jnp.concatenate([wxy * (spread_gain * base[c]) for c in range(3)], axis=0))
    both = dot(hi, wz2, NT)
    return both[:, :SZ] + (both[:, SZ:] + dot(low, wz2[0:SZ], NT))


def look_up(halves, code):
    low_half = iota((1, 128), 1) < 64
    mine = lax.axis_index("fz")
    height = HALF
    label = (iota((height, SLOTS), 0) * 2 + mine) * CAP + iota((height, SLOTS), 1) // 64
    labels = (label, label + CAP * (1 - 2 * mine))
    found = [[None] * 2 for _ in range(3)]
    for part in range(2):
        piece = code[:, 128 * part : 128 * part + 128]
        turned = pltpu.roll(piece, 64, 1)
        pair = []
        for odd in range(2):
            both = jnp.where(low_half, turned, piece) if odd else jnp.where(low_half, piece, turned)
            wanted = jnp.concatenate([both, both], axis=1)
            per = []
            for comp in range(3):
                lanes = slice(comp * SLOTS, (comp + 1) * SLOTS)
                hit = jnp.where(labels[0] == wanted, halves[0][:, lanes], 0.0)
                hit = hit + jnp.where(labels[1] == wanted, halves[1][:, lanes], 0.0)
                hit = jnp.sum(hit, axis=0, keepdims=True)
                hit = hit[:, :128] + hit[:, 128:]
                per.append(hit + pltpu.roll(hit, 64, 1))
            pair.append(per)
        for comp in range(3):
            found[comp][part] = jnp.where(low_half, pair[0][comp], pair[1][comp])
    return [jnp.concatenate(found[comp], axis=1) for comp in range(3)]


def responses(rows, sampled):
    cr = rows[R_CR : R_CR + 1]
    return [rows[R_REST + c : R_REST + c + 1] + cr * sampled[c] for c in range(3)]


def prepare_kernel(t, *refs):
    static, sent, (wxy_out, wz_out, plane_out, slots, turned) = refs[0], refs[1:-5], refs[-5:]
    turn_static(static, turned, t)
    for j in range(SETS):
        rows = slot_rows(turned, t, j)
        wxy, wz = tables(rows, (None, SX - 1, 0)[j])
        hi, low = split(wz)
        wz_out[j, 0:SZ, :] = hi
        wz_out[j, SZ:, :] = low
        if j == 0:
            wxy_out[...] = wxy
        else:
            plane_out[j - 1] = wxy
        slots[32 * j : 32 * j + HEIGHT[t], :] = rows
        if t == 2:
            code = rows[R_CODE : R_CODE + 1].astype(jnp.int32)
            before = responses(rows, look_up(sent, code & (SLOTS - 1)))
            for c in range(3):
                slots[32 * j + 24 + c : 32 * j + 25 + c, :] = before[c]


def displacements(t, rows, sent):
    first = [rows[R_D0 + c : R_D0 + c + 1] for c in range(3)]
    if t == 0:
        return [first], []
    code = rows[R_CODE : R_CODE + 1].astype(jnp.int32)
    if t == 1:
        before = responses(rows, look_up(sent, code & (SLOTS - 1)))
    else:
        before = [rows[24 + c : 25 + c] for c in range(3)]
    gap = [before[c] - first[c] for c in range(3)]
    second = [first[c] + relaxation * gap[c] for c in range(3)]
    if t == 1:
        return [second], [second, gap]
    latest = responses(rows, look_up(sent, code >> 8))
    change = [latest[c] - before[c] for c in range(3)]
    return [latest, change], [latest, change, gap, [latest[c] - second[c] for c in range(3)], before]


def spread_kernel(t, *refs):
    if t == 0:
        static, velocity = refs[0:2]
        sent = ()
        field, xl, xu, ylo, yhi, *tabled, turned = refs[2:]
        prepare_kernel(0, static, *tabled, turned)
    else:
        velocity, sent, tabled = refs[0], refs[1:3], refs[3:7]
        field, xl, xu, ylo, yhi, aux = refs[7:13]
        aux[...] = jnp.zeros_like(aux)
    wxy, wz, plane, slots = tabled
    for j, out in enumerate((field, xl, xu)):
        rows = slots[32 * j : 32 * j + 32, :]
        bases, kept = displacements(t, rows, sent)
        height = SY if j else XY
        for n, base in enumerate(bases):
            forced = spread(plane[j - 1] if j else wxy[...], wz[j], base)
            for c in range(3):
                part = forced[height * c : height * (c + 1)]
                out[3 * n + c] = part + velocity[c] if n == 0 and j == 0 else part
        if j == 0 and t > 0:
            for n, group in enumerate(kept):
                for c in range(3):
                    aux[3 * n + c : 3 * n + c + 1, :] = group[c]
            aux[16:20, :] = rows[R_REST : R_REST + 4]
    for n in range(3 * len(bases)):
        ylo[n] = field[n, pl.ds(0, SX, stride=SY), :]
        yhi[n] = field[n, pl.ds(SY - 1, SX, stride=SY), :]
    if t == 2:
        lanes = slice(3 * SLOTS, 3 * SLOTS + 128)
        total = jnp.sum(sent[0][:, lanes] + sent[1][:, lanes], axis=0, keepdims=True)
        total = jnp.broadcast_to(total, (8, 128))
        ylo[6] = total
        yhi[6] = total
        refs[13][...] = total


def wake(u, beside_z, xl, xu, yl, yu, viscosity):
    lane = iota((XY, SZ), 1)
    y = iota((XY, SZ), 0) % SY
    upper_core = lax.axis_index("fz") > 0
    speed = jnp.sqrt(1.0 + (u[0] * u[0] + u[1] * u[1] + u[2] * u[2]))
    new = []
    for c in range(3):
        here = u[c]
        near = jnp.concatenate([xl[c], here[: XY - SY]], axis=0)
        near = near + jnp.concatenate([here[SY:], xu[c]], axis=0)
        wide_l = jnp.concatenate([jnp.broadcast_to(yl[c][x : x + 1], (SY, SZ)) for x in range(SX)], axis=0)
        wide_u = jnp.concatenate([jnp.broadcast_to(yu[c][x : x + 1], (SY, SZ)) for x in range(SX)], axis=0)
        near = near + jnp.where(y == 0, wide_l, pltpu.roll(here, 1, 0))
        near = near + jnp.where(y == SY - 1, wide_u, pltpu.roll(here, XY - 1, 0))
        left = jnp.where(upper_core, beside_z[c], 0.0)
        right = jnp.where(upper_core, 0.0, beside_z[c])
        near = near + pltpu.roll(jnp.where(lane == SZ - 1, left, here), 1, 1)
        near = near + pltpu.roll(jnp.where(lane == 0, right, here), SZ - 1, 1)
        new.append(here + viscosity * (near - 6.0 * here) - drag_coeff * here * speed)
    return new


def sample(new, wxy, wz2):
    wz_hi, wz_low = wz2[0:SZ], wz2[SZ:]
    both = jnp.concatenate([wz_hi, wz_hi], axis=0)
    sampled = []
    for c in range(3):
        hi, low = split(new[c])
        along_z = dot(jnp.concatenate([hi, low], axis=1), both, NN) + dot(hi, wz_low, NN)
        sampled.append(jnp.sum(wxy * along_z, axis=0, keepdims=True))
    return sampled


def product(a, b):
    rows = a[0] * b[0] + a[1] * b[1] + a[2] * b[2]
    return rows[:, :128] + rows[:, 128:]


def lane_of(row, n):
    return jnp.sum(jnp.where(iota(row.shape, 1) == n, row, 0.0), axis=1, keepdims=True)


def sample_kernel(t, *refs):
    viscosity, far_l, far_u = refs[0:3]
    refs = refs[2:]
    field, beside_z, xl, xu, yl, yu, wxy, wz = refs[1:9]
    fx = lax.axis_index("fx")
    me = lax.axis_index("cable")
    last = lax.axis_size("cable") - 1

    def whole(ref):
        if t < 2:
            return [ref[c] for c in range(3)]
        return [ref[c] + coef * ref[3 + c] for c in range(3)]

    if t == 2:
        gram = yl[6] + yu[6] + (refs[10][...] + refs[11][...])
        first = iota((1, 128), 1) < 64
        square = jnp.sum(jnp.where(first, gram[0:1], 0.0), axis=1, keepdims=True)
        target = jnp.sum(jnp.where(first, 0.0, gram[0:1]), axis=1, keepdims=True)
        coef = -target / (square + (ridge_share * square + 1e-06))
    u = whole(field)
    below = [jnp.where(me > 0, face, 0.0) for face in whole(yl)]
    above = [jnp.where(me < last, face, 0.0) for face in whole(yu)]
    before = [jnp.where(fx > 0, far_l[c], 0.0) + part for c, part in enumerate(whole(xl))]
    after = [jnp.where(fx < lax.axis_size("fx") - 1, far_u[c], 0.0) + part for c, part in enumerate(whole(xu))]
    faces = [before, after, below, above]
    new = wake(u, whole(beside_z), *faces, viscosity[...])
    sampled = sample(new, wxy[...], wz[0])
    if t == 0:
        keep, got, msg = refs[9:12]
        for c in range(3):
            msg[:, SLOTS * c : SLOTS * (c + 1)] = jnp.broadcast_to(sampled[c], (HALF, SLOTS))
        msg[:, 3 * SLOTS : 3 * SLOTS + LATE] = keep[...]
        msg[:, 3 * SLOTS + LATE :] = got[...]
        return
    aux = refs[9]

    def kept(n):
        return [aux[3 * n + c : 3 * n + c + 1, :] for c in range(3)]

    cr = aux[19:20, :]
    response = [aux[16 + c : 17 + c, :] + cr * sampled[c] for c in range(3)]
    if t == 1:
        msg = refs[10]
        disp, gap0 = kept(0), kept(1)
        gap = [response[c] - disp[c] for c in range(3)]
        v0 = [gap[c] - gap0[c] for c in range(3)]
        for c in range(3):
            msg[:, SLOTS * c : SLOTS * (c + 1)] = jnp.broadcast_to(sampled[c], (HALF, SLOTS))
        square, target = product(v0, v0), product(v0, gap)
        square, target = (part + pltpu.roll(part, 64, 1) for part in (square, target))
        row = jnp.where(iota((1, 128), 1) < 64, square, target)
        msg[:, 3 * SLOTS : 3 * SLOTS + 128] = jnp.broadcast_to(row, (HALF, 128))
        return
    out, msg, turn = refs[12:15]
    for c in range(3):
        out[c] = new[c]
    latest, change, gap0, gap1, before = (kept(n) for n in range(5))
    disp = [latest[c] + coef * change[c] for c in range(3)]
    gap = [response[c] - disp[c] for c in range(3)]
    v0 = [gap[c] - gap0[c] for c in range(3)]
    v1 = [gap[c] - gap1[c] for c in range(3)]
    turn[...] = jnp.zeros_like(turn)
    for n, group in enumerate((response, before, latest)):
        for c in range(3):
            turn[3 * n + c : 3 * n + c + 1, :] = group[c][:, :128]
            turn[32 + 3 * n + c : 33 + 3 * n + c, :] = group[c][:, 128:]
    for n, (a, b) in enumerate(((v0, v0), (v0, v1), (v1, v1), (v0, gap), (v1, gap))):
        turn[64 + n : 65 + n, :] = product(a, b)
    turned = jnp.transpose(turn[...])
    row = jnp.sum(turned, axis=0, keepdims=True)
    block = turned[0:64] + pltpu.roll(turned[64:128], 16, 1)
    block = jnp.where(iota((1, 128), 1) < 64, block, row)
    for c in range(4):
        for f in range(2):
            msg[pl.ds(GROUP * c + f, HALF, stride=2), :] = block[HALF * f : HALF * (f + 1)]


def finish_kernel(sent, place, out):
    row = jnp.sum(sent[...], axis=0, keepdims=True)
    g00, g01, g11, b0, b1 = (lane_of(row, 64 + n) for n in range(5))
    shift = ridge_share * (g00 + g11) / 2 + 1e-06
    first, second = g00 + shift, g11 + shift
    determinant = first * second - g01 * g01
    c0 = -(second * b0 - g01 * b1) / determinant
    c1 = -(first * b1 - g01 * b0) / determinant
    start = pl.multiple_of(lax.axis_index("cable") * GROUP, GROUP)
    mine = sent[pl.ds(start, GROUP), :]
    turned = jnp.transpose(jnp.concatenate([mine, jnp.zeros((128 - GROUP, 128), F32)], axis=0))
    hot = (iota((128, SEG_DEV), 0).astype(F32) == place[0:1, :]).astype(F32).astype(BF16)
    parts = split3(turned[0:64])
    got = dot(parts[0], hot, NN) + (dot(parts[1], hot, NN) + dot(parts[2], hot, NN))
    rank = place[1:2, :]
    rows = jnp.zeros((16, SEG_DEV), F32)
    for k in range(CAP):
        rows = jnp.where(rank == k, got[16 * k : 16 * k + 16], rows)
    response, before, latest = rows[0:3], rows[3:6], rows[6:9]
    out[...] = response + c0 * (response - before) + c1 * (response - latest)


def shape(*dims, kind=F32):
    return jax.ShapeDtypeStruct(dims, kind)


def call(kernel, ins, outs, scratch=(), space=pltpu.VMEM):
    size = sum(a.size * a.dtype.itemsize for a in (*ins, *outs))
    return pl.pallas_call(
        kernel,
        out_shape=outs,
        in_specs=[pl.BlockSpec(memory_space=space)] * len(ins),
        out_specs=[pl.BlockSpec(memory_space=pltpu.VMEM)] * len(outs),
        scratch_shapes=list(scratch),
        compiler_params=pltpu.CompilerParams(vmem_limit_bytes=16 * 1024 * 1024),
        cost_estimate=pl.CostEstimate(flops=0, bytes_accessed=size, transcendentals=0),
    )(*ins)


def shifted(array, axis, by):
    count = lax.axis_size(axis)
    return lax.ppermute(array, axis, [(i, (i + by) % count) for i in range(count)])


def exchange(array, axes):
    return lax.all_to_all(array, axes, 0, 0, tiled=True)


def body(velocity, viscosity, disp_init, rest_shape, compliance, stencil_weights, anchor, owners):
    flow = velocity.reshape(3, XY, SZ)
    thick = viscosity.reshape(XY, SZ)
    ins = (disp_init, rest_shape, compliance.reshape(1, SEG_DEV), stencil_weights, anchor, owners)
    msg, later, _, xlo, xhi = call(
        pack_kernel,
        tuple(pltpu.with_memory_space_constraint(a, pltpu.HBM) for a in (*ins, flow)),
        [shape(GROUP, EARLY), shape(56, SEG_DEV), shape(24, SEG_DEV), shape(3, SY, SZ), shape(3, SY, SZ)],
        [pltpu.VMEM(a.shape, a.dtype) for a in ins]
        + [pltpu.VMEM((EARLY, 128), F32), pltpu.SemaphoreType.DMA((8,))],
        pltpu.HBM,
    )
    static = exchange(msg, ("fx", "fz"))
    far_l = shifted(xhi, "fx", 1)
    far_u = shifted(xlo, "fx", -1)
    keep, give, place = call(
        pack_later_kernel,
        (later,),
        [shape(HALF, LATE), shape(HALF, LATE), shape(8, SEG_DEV)],
        [pltpu.VMEM((LATE, 128), F32)],
    )
    static, *carried = lax.optimization_barrier((static, keep, shifted(give, "fz", 1)))
    table_outs = [
        shape(XY, SLOTS),
        shape(SETS, 2 * SZ, SLOTS, kind=BF16),
        shape(2, SY, SLOTS),
        shape(32 * SETS, SLOTS),
    ]
    turned = [pltpu.VMEM((LATE, 128), F32)]
    sent, tabled = (), ()
    for t in range(3):
        n = 6 if t == 2 else 3
        faced = 7 if t == 2 else 3
        outs = [shape(n, XY, SZ), shape(n, SY, SZ), shape(n, SY, SZ)] + [shape(faced, SX, SZ)] * 2
        kernel = functools.partial(spread_kernel, t)
        if t == 0:
            field, xl, xu, ylo, yhi, *tabled = call(kernel, (static, flow), outs + table_outs, turned)
            extra = []
        else:
            outs.append(shape(24, SLOTS))
            if t == 2:
                outs.append(shape(8, 128))
            field, xl, xu, ylo, yhi, *extra = call(kernel, (flow, *sent, *tabled), outs)
        yl = shifted(yhi, "cable", 1)
        yu = shifted(ylo, "cable", -1)
        beside_z = shifted(field, "fz", 1)
        if t == 2:
            across = shifted(extra[1], "cable", 2)
        ins = [thick, far_l, far_u, field, beside_z, xl, xu, yl, yu, *tabled[0:2], *extra]
        kernel = functools.partial(sample_kernel, t)
        if t < 2:
            if t == 0:
                ins += carried
            (msg,) = call(kernel, ins, [shape(HALF, 3 * SLOTS + (128 if t else 2 * LATE))])
            half = exchange(msg, "fx")
            if t == 0:
                static, before = half, ()
            sent = (half, shifted(half if t else half[:, : 3 * SLOTS], "fz", 1))
            tabled = call(functools.partial(prepare_kernel, t + 1), (static, *before), table_outs, turned)
            before = sent
        else:
            ins.append(across)
            out, msg = call(kernel, ins, [shape(3, XY, SZ), shape(4 * GROUP, 128)], [pltpu.VMEM((128, 128), F32)])
    last = exchange(msg, ("cable", "fx", "fz"))
    (disp_next,) = call(finish_kernel, (last, place), [shape(3, SEG_DEV)])
    return disp_next, out.reshape(velocity.shape)


def solution(mesh):
    segments = ("cable", "fx", "fz")
    placed = (
        P(None, "fx", "cable", "fz"),
        P("fx", "cable", "fz"),
        P(None, segments),
        P(None, segments),
        P(segments),
        P(None, None, segments),
        P(None, segments),
        P(None, segments),
    )
    return jax.shard_map(
        body,
        mesh=mesh,
        in_specs=placed,
        out_specs=(P(None, segments), P(None, "fx", "cable", "fz")),
        check_vma=False,
    )
```

```python
import functools

import jax
import jax.numpy as jnp
from jax import lax
from jax.experimental import pallas as pl
from jax.experimental.pallas import tpu as pltpu
from jax.sharding import PartitionSpec as P


F32 = jnp.float32
BF16 = jnp.bfloat16
NT = (((1,), (1,)), ((), ()))
NN = (((1,), (0,)), ((), ()))

spread_gain = 16.0
drag_coeff = 0.05
relaxation = 0.5
ridge_share = 0.01

SEG_DEV = 64
GROUP = 64
CAP = 4
HALF = GROUP // 2
SLOTS = GROUP * CAP
SX, SY, SZ = 8, 16, 128
XY = SX * SY

R_W, R_CELL, R_D0, R_REST, R_CR, R_CODE = 0, 12, 13, 16, 19, 20
HEIGHT = (16, 24, 24)
SETS = 3
BASE = (0, 0, 288)
EARLY, LATE = 256, 640


def split(x):
    hi = x.astype(BF16)
    return hi, (x - hi.astype(F32)).astype(BF16)


def dot(a, b, dims):
    return lax.dot_general(a, b, dims, preferred_element_type=F32)


def iota(shape, dim):
    return lax.broadcasted_iota(jnp.int32, shape, dim)


def split3(x):
    hi, low = split(x)
    return hi, low, (x - hi.astype(F32) - low.astype(F32)).astype(BF16)


def rank_of(own):
    hot = (iota((GROUP, SEG_DEV), 0) == own).astype(F32)
    earlier = (iota((SEG_DEV, SEG_DEV), 0) < iota((SEG_DEV, SEG_DEV), 1)).astype(F32)
    return jnp.sum(hot * dot(hot, earlier, NN), axis=0, keepdims=True)


def put_slots(fields, rank, rows, turn, base):
    height = fields.shape[0]
    parts = split3(jnp.concatenate([jnp.where(rank == k, fields, 0.0) for k in range(CAP)], axis=0))
    dest = iota((GROUP, SEG_DEV), 0)
    hots = jnp.concatenate([(dest == row).astype(F32).astype(BF16) for row in rows], axis=0)
    got = dot(parts[0], hots, NT) + (dot(parts[1], hots, NT) + dot(parts[2], hots, NT))
    for j in range(SETS):
        start = base + CAP * height * j
        turn[start : start + CAP * height, 0:GROUP] = got[:, GROUP * j : GROUP * (j + 1)]


def pack_kernel(*refs):
    far, (msg, later, firsts, xlo, xhi), near, (turn, sems) = refs[0:7], refs[7:12], refs[12:18], refs[18:20]
    copies = [pltpu.make_async_copy(far[n], near[n], sems.at[n]) for n in (5, 4, 3, 0, 1, 2)]
    copies.append(pltpu.make_async_copy(far[6].at[:, 0:SY, :], xlo, sems.at[6]))
    copies.append(pltpu.make_async_copy(far[6].at[:, XY - SY : XY, :], xhi, sems.at[7]))
    for copy in copies:
        copy.start()
    disp, rest, comp, weights, anchor, owner = near
    fz_n, fx_n, cable_n = lax.axis_size("fz"), lax.axis_size("fx"), lax.axis_size("cable")
    device = (lax.axis_index("cable") * fx_n + lax.axis_index("fx")) * fz_n + lax.axis_index("fz")
    position = (device * SEG_DEV + iota((1, SEG_DEV), 1)).astype(F32)
    ramp = 1.0 + 2.0 * position / (SEG_DEV * fz_n * fx_n * cable_n)
    later[...] = jnp.zeros_like(later)
    firsts[...] = jnp.zeros_like(firsts)
    turn[...] = jnp.zeros_like(turn)
    for copy in copies:
        copy.wait()
    own = owner[0:1, :]
    rank = rank_of(own)
    firsts[0:12, :] = weights[0]
    firsts[R_CELL : R_CELL + 1, :] = anchor[0:1, :].astype(F32)
    firsts[R_D0 : R_D0 + 3, :] = disp[...]
    put_slots(firsts[0 : HEIGHT[0], :], rank, (own, own + fz_n, own - fz_n), turn, BASE[0])
    for n in range(EARLY // 128):
        msg[:, 128 * n : 128 * n + 128] = jnp.transpose(turn[128 * n : 128 * n + 128, :])[0:GROUP]
    for t in (1, 2):
        at = 24 * (t - 1)
        later[at : at + 12, :] = weights[t]
        later[at + R_CELL : at + R_CELL + 1, :] = anchor[t : t + 1, :].astype(F32)
        later[at + R_D0 : at + R_D0 + 3, :] = disp[...]
        later[at + R_REST : at + R_REST + 3, :] = rest[...]
        later[at + R_CR : at + R_CR + 1, :] = comp[...] * ramp
    later[48:51, :] = owner[...].astype(F32)
    later[51:52, :] = rank


def pack_later_kernel(later, keep, give, place, turn):
    mine = lax.axis_index("fz")
    turn[...] = jnp.zeros_like(turn)
    owners = [later[48 + t : 49 + t, :].astype(jnp.int32) for t in range(3)]
    ranks = [later[51:52, :], rank_of(owners[1]), rank_of(owners[2])]
    codes = [owners[t].astype(F32) * CAP + ranks[t] for t in range(2)]
    code = codes[0] + SLOTS * codes[1]
    for t in (1, 2):
        side, fx = (owners[t] & 1) ^ mine, owners[t] >> 1
        at = side * HALF + fx
        rows = (at, jnp.where(fx < HALF - 1, at + 1, -1), jnp.where(fx > 0, at - 1, -1))
        fields = later[24 * (t - 1) : 24 * t, :]
        fields = jnp.where(iota((24, SEG_DEV), 0) == R_CODE, code, fields)
        put_slots(fields, ranks[t], rows, turn, BASE[t])
    for n in range(LATE // 128):
        lanes = slice(128 * n, 128 * n + 128)
        block = jnp.transpose(turn[lanes, :])
        keep[:, lanes] = block[0:HALF]
        give[:, lanes] = block[HALF:GROUP]
    place[...] = jnp.zeros_like(place)
    place[0:1, :] = later[50:51, :]
    place[1:2, :] = ranks[2]


def turn_static(static, turned, t):
    first = BASE[t] // 128
    last = (BASE[t] + SETS * CAP * HEIGHT[t] + 127) // 128
    low = lax.axis_index("fz") == 0
    for n in range(first, last):
        if t == 0:
            spare = LATE - GROUP
            turned[spare:LATE, :] = static[:, 128 * n : 128 * n + 128]
            homes = [turned[pl.ds(spare + f, HALF, stride=2), :] for f in range(2)]
        else:
            at = 3 * SLOTS + 128 * n
            same, other = static[:, at : at + 128], static[:, at + LATE : at + LATE + 128]
            homes = [jnp.where(low, same, other), jnp.where(low, other, same)]
        wide = jnp.concatenate([*homes, jnp.zeros((128 - GROUP, 128), F32)], axis=0)
        turned[128 * n : 128 * n + 128, :] = jnp.transpose(wide)


def slot_rows(turned, t, j):
    height = HEIGHT[t]
    start = BASE[t] + CAP * height * j
    part = [turned[start + height * k : start + height * (k + 1), :] for k in range(CAP)]
    halves = [part[2 * n] + pltpu.roll(part[2 * n + 1], 64, 1) for n in range(2)]
    return jnp.concatenate(halves, axis=1)


def along(rows, first, at):
    total = jnp.zeros(at.shape, F32)
    for i in range(4):
        total = jnp.where(at == i, rows[first + i : first + i + 1], total)
    return total


def tables(rows, plane=None):
    cell = rows[R_CELL : R_CELL + 1].astype(jnp.int32)
    wy = along(rows, R_W + 4, iota((SY, SLOTS), 0) - ((cell >> 7) & (SY - 1)))
    wz = along(rows, R_W + 8, iota((SZ, SLOTS), 0) - (cell & (SZ - 1)))
    if plane is not None:
        return along(rows, R_W, plane - (cell >> 11)) * wy, wz
    wx = along(rows, R_W, iota((SX, SLOTS), 0) - (cell >> 11))
    return jnp.concatenate([wx[x : x + 1] * wy for x in range(SX)], axis=0), wz


def spread(wxy, wz2, base):
    hi, low = split(jnp.concatenate([wxy * (spread_gain * base[c]) for c in range(3)], axis=0))
    both = dot(hi, wz2, NT)
    return both[:, :SZ] + (both[:, SZ:] + dot(low, wz2[0:SZ], NT))


def look_up(halves, code):
    low_half = iota((1, 128), 1) < 64
    mine = lax.axis_index("fz")
    height = HALF
    label = (iota((height, SLOTS), 0) * 2 + mine) * CAP + iota((height, SLOTS), 1) // 64
    labels = (label, label + CAP * (1 - 2 * mine))
    found = [[None] * 2 for _ in range(3)]
    for part in range(2):
        piece = code[:, 128 * part : 128 * part + 128]
        turned = pltpu.roll(piece, 64, 1)
        pair = []
        for odd in range(2):
            both = jnp.where(low_half, turned, piece) if odd else jnp.where(low_half, piece, turned)
            wanted = jnp.concatenate([both, both], axis=1)
            per = []
            for comp in range(3):
                lanes = slice(comp * SLOTS, (comp + 1) * SLOTS)
                hit = jnp.where(labels[0] == wanted, halves[0][:, lanes], 0.0)
                hit = hit + jnp.where(labels[1] == wanted, halves[1][:, lanes], 0.0)
                hit = jnp.sum(hit, axis=0, keepdims=True)
                hit = hit[:, :128] + hit[:, 128:]
                per.append(hit + pltpu.roll(hit, 64, 1))
            pair.append(per)
        for comp in range(3):
            found[comp][part] = jnp.where(low_half, pair[0][comp], pair[1][comp])
    return [jnp.concatenate(found[comp], axis=1) for comp in range(3)]


def responses(rows, sampled):
    cr = rows[R_CR : R_CR + 1]
    return [rows[R_REST + c : R_REST + c + 1] + cr * sampled[c] for c in range(3)]


def prepare_kernel(t, sets, *refs):
    static, sent, (wxy_out, wz_out, plane_out, slots, turned) = refs[0], refs[1:-5], refs[-5:]
    turn_static(static, turned, t)
    for j in sets:
        rows = slot_rows(turned, t, j)
        wxy, wz = tables(rows, (None, SX - 1, 0)[j])
        hi, low = split(wz)
        wz_out[j, 0:SZ, :] = hi
        wz_out[j, SZ:, :] = low
        if j == 0:
            wxy_out[...] = wxy
        else:
            plane_out[j - 1] = wxy
        slots[32 * j : 32 * j + HEIGHT[t], :] = rows
        if t == 2:
            code = rows[R_CODE : R_CODE + 1].astype(jnp.int32)
            before = responses(rows, look_up(sent, code & (SLOTS - 1)))
            for c in range(3):
                slots[32 * j + 24 + c : 32 * j + 25 + c, :] = before[c]


def displacements(t, rows, sent):
    first = [rows[R_D0 + c : R_D0 + c + 1] for c in range(3)]
    if t == 0:
        return [first], []
    code = rows[R_CODE : R_CODE + 1].astype(jnp.int32)
    if t == 1:
        before = responses(rows, look_up(sent, code & (SLOTS - 1)))
    else:
        before = [rows[24 + c : 25 + c] for c in range(3)]
    gap = [before[c] - first[c] for c in range(3)]
    second = [first[c] + relaxation * gap[c] for c in range(3)]
    if t == 1:
        return [second], [second, gap]
    latest = responses(rows, look_up(sent, code >> 8))
    change = [latest[c] - before[c] for c in range(3)]
    return [latest, change], [latest, change, gap, [latest[c] - second[c] for c in range(3)], before]


def spread_kernel(t, *refs):
    if t == 0:
        static, velocity = refs[0:2]
        sent = ()
        field, ylo, yhi, *tabled, turned = refs[2:]
        prepare_kernel(0, (0,), static, *tabled, turned)
    else:
        velocity, sent, tabled = refs[0], refs[1:3], refs[3:7]
        field, ylo, yhi, aux = refs[7:11]
        aux[...] = jnp.zeros_like(aux)
    wxy, wz, _, slots = tabled
    rows = slots[0:32, :]
    bases, kept = displacements(t, rows, sent)
    for n, base in enumerate(bases):
        forced = spread(wxy[...], wz[0], base)
        for c in range(3):
            part = forced[XY * c : XY * (c + 1)]
            field[3 * n + c] = part + velocity[c] if n == 0 else part
    if t > 0:
        for n, group in enumerate(kept):
            for c in range(3):
                aux[3 * n + c : 3 * n + c + 1, :] = group[c]
        aux[16:20, :] = rows[R_REST : R_REST + 4]
    for n in range(3 * len(bases)):
        ylo[n] = field[n, pl.ds(0, SX, stride=SY), :]
        yhi[n] = field[n, pl.ds(SY - 1, SX, stride=SY), :]
    if t == 2:
        lanes = slice(3 * SLOTS, 3 * SLOTS + 128)
        total = jnp.sum(sent[0][:, lanes] + sent[1][:, lanes], axis=0, keepdims=True)
        total = jnp.broadcast_to(total, (8, 128))
        ylo[6] = total
        yhi[6] = total
        refs[11][...] = total


def sides_kernel(t, *refs):
    if t == 0:
        (static, *outs), tabled, turned = refs[0:3], refs[3:7], refs[7]
        sent = ()
        prepare_kernel(0, (1, 2), static, *tabled, turned)
    else:
        sent, tabled, outs = refs[0:2], refs[2:6], refs[6:8]
    _, wz, plane, slots = tabled
    for j, out in enumerate(outs):
        bases, _ = displacements(t, slots[32 * j + 32 : 32 * j + 64, :], sent)
        for n, base in enumerate(bases):
            forced = spread(plane[j], wz[j + 1], base)
            for c in range(3):
                out[3 * n + c] = forced[SY * c : SY * (c + 1)]


def wake(u, beside_z, xl, xu, yl, yu, viscosity):
    lane = iota((XY, SZ), 1)
    y = iota((XY, SZ), 0) % SY
    upper_core = lax.axis_index("fz") > 0
    speed = jnp.sqrt(1.0 + (u[0] * u[0] + u[1] * u[1] + u[2] * u[2]))
    new = []
    for c in range(3):
        here = u[c]
        near = jnp.concatenate([xl[c], here[: XY - SY]], axis=0)
        near = near + jnp.concatenate([here[SY:], xu[c]], axis=0)
        wide_l = jnp.concatenate([jnp.broadcast_to(yl[c][x : x + 1], (SY, SZ)) for x in range(SX)], axis=0)
        wide_u = jnp.concatenate([jnp.broadcast_to(yu[c][x : x + 1], (SY, SZ)) for x in range(SX)], axis=0)
        near = near + jnp.where(y == 0, wide_l, pltpu.roll(here, 1, 0))
        near = near + jnp.where(y == SY - 1, wide_u, pltpu.roll(here, XY - 1, 0))
        left = jnp.where(upper_core, beside_z[c], 0.0)
        right = jnp.where(upper_core, 0.0, beside_z[c])
        near = near + pltpu.roll(jnp.where(lane == SZ - 1, left, here), 1, 1)
        near = near + pltpu.roll(jnp.where(lane == 0, right, here), SZ - 1, 1)
        new.append(here + viscosity * (near - 6.0 * here) - drag_coeff * here * speed)
    return new


def sample(new, wxy, wz2):
    wz_hi, wz_low = wz2[0:SZ], wz2[SZ:]
    both = jnp.concatenate([wz_hi, wz_hi], axis=0)
    sampled = []
    for c in range(3):
        hi, low = split(new[c])
        along_z = dot(jnp.concatenate([hi, low], axis=1), both, NN) + dot(hi, wz_low, NN)
        sampled.append(jnp.sum(wxy * along_z, axis=0, keepdims=True))
    return sampled


def product(a, b):
    rows = a[0] * b[0] + a[1] * b[1] + a[2] * b[2]
    return rows[:, :128] + rows[:, 128:]


def lane_of(row, n):
    return jnp.sum(jnp.where(iota(row.shape, 1) == n, row, 0.0), axis=1, keepdims=True)


def sample_kernel(t, *refs):
    viscosity, far_l, far_u = refs[0:3]
    refs = refs[2:]
    field, beside_z, xl, xu, yl, yu, wxy, wz = refs[1:9]
    fx = lax.axis_index("fx")
    me = lax.axis_index("cable")
    last = lax.axis_size("cable") - 1

    def whole(ref):
        if t < 2:
            return [ref[c] for c in range(3)]
        return [ref[c] + coef * ref[3 + c] for c in range(3)]

    if t == 2:
        gram = yl[6] + yu[6] + (refs[10][...] + refs[11][...])
        first = iota((1, 128), 1) < 64
        square = jnp.sum(jnp.where(first, gram[0:1], 0.0), axis=1, keepdims=True)
        target = jnp.sum(jnp.where(first, 0.0, gram[0:1]), axis=1, keepdims=True)
        coef = -target / (square + (ridge_share * square + 1e-06))
    u = whole(field)
    below = [jnp.where(me > 0, face, 0.0) for face in whole(yl)]
    above = [jnp.where(me < last, face, 0.0) for face in whole(yu)]
    before = [jnp.where(fx > 0, far_l[c], 0.0) + part for c, part in enumerate(whole(xl))]
    after = [jnp.where(fx < lax.axis_size("fx") - 1, far_u[c], 0.0) + part for c, part in enumerate(whole(xu))]
    faces = [before, after, below, above]
    new = wake(u, whole(beside_z), *faces, viscosity[...])
    sampled = sample(new, wxy[...], wz[0])
    if t == 0:
        keep, got, msg = refs[9:12]
        for c in range(3):
            msg[:, SLOTS * c : SLOTS * (c + 1)] = jnp.broadcast_to(sampled[c], (HALF, SLOTS))
        msg[:, 3 * SLOTS : 3 * SLOTS + LATE] = keep[...]
        msg[:, 3 * SLOTS + LATE :] = got[...]
        return
    aux = refs[9]

    def kept(n):
        return [aux[3 * n + c : 3 * n + c + 1, :] for c in range(3)]

    cr = aux[19:20, :]
    response = [aux[16 + c : 17 + c, :] + cr * sampled[c] for c in range(3)]
    if t == 1:
        msg = refs[10]
        disp, gap0 = kept(0), kept(1)
        gap = [response[c] - disp[c] for c in range(3)]
        v0 = [gap[c] - gap0[c] for c in range(3)]
        for c in range(3):
            msg[:, SLOTS * c : SLOTS * (c + 1)] = jnp.broadcast_to(sampled[c], (HALF, SLOTS))
        square, target = product(v0, v0), product(v0, gap)
        square, target = (part + pltpu.roll(part, 64, 1) for part in (square, target))
        row = jnp.where(iota((1, 128), 1) < 64, square, target)
        msg[:, 3 * SLOTS : 3 * SLOTS + 128] = jnp.broadcast_to(row, (HALF, 128))
        return
    out, msg, turn = refs[12:15]
    for c in range(3):
        out[c] = new[c]
    latest, change, gap0, gap1, before = (kept(n) for n in range(5))
    disp = [latest[c] + coef * change[c] for c in range(3)]
    gap = [response[c] - disp[c] for c in range(3)]
    v0 = [gap[c] - gap0[c] for c in range(3)]
    v1 = [gap[c] - gap1[c] for c in range(3)]
    turn[...] = jnp.zeros_like(turn)
    for n, group in enumerate((response, before, latest)):
        for c in range(3):
            turn[3 * n + c : 3 * n + c + 1, :] = group[c][:, :128]
            turn[32 + 3 * n + c : 33 + 3 * n + c, :] = group[c][:, 128:]
    for n, (a, b) in enumerate(((v0, v0), (v0, v1), (v1, v1), (v0, gap), (v1, gap))):
        turn[64 + n : 65 + n, :] = product(a, b)
    turned = jnp.transpose(turn[...])
    row = jnp.sum(turned, axis=0, keepdims=True)
    block = turned[0:64] + pltpu.roll(turned[64:128], 16, 1)
    block = jnp.where(iota((1, 128), 1) < 64, block, row)
    for c in range(4):
        for f in range(2):
            msg[pl.ds(GROUP * c + f, HALF, stride=2), :] = block[HALF * f : HALF * (f + 1)]


def finish_kernel(sent, place, out):
    row = jnp.sum(sent[...], axis=0, keepdims=True)
    g00, g01, g11, b0, b1 = (lane_of(row, 64 + n) for n in range(5))
    shift = ridge_share * (g00 + g11) / 2 + 1e-06
    first, second = g00 + shift, g11 + shift
    determinant = first * second - g01 * g01
    c0 = -(second * b0 - g01 * b1) / determinant
    c1 = -(first * b1 - g01 * b0) / determinant
    start = pl.multiple_of(lax.axis_index("cable") * GROUP, GROUP)
    mine = sent[pl.ds(start, GROUP), :]
    turned = jnp.transpose(jnp.concatenate([mine, jnp.zeros((128 - GROUP, 128), F32)], axis=0))
    hot = (iota((128, SEG_DEV), 0).astype(F32) == place[0:1, :]).astype(F32).astype(BF16)
    parts = split3(turned[0:64])
    got = dot(parts[0], hot, NN) + (dot(parts[1], hot, NN) + dot(parts[2], hot, NN))
    rank = place[1:2, :]
    rows = jnp.zeros((16, SEG_DEV), F32)
    for k in range(CAP):
        rows = jnp.where(rank == k, got[16 * k : 16 * k + 16], rows)
    response, before, latest = rows[0:3], rows[3:6], rows[6:9]
    out[...] = response + c0 * (response - before) + c1 * (response - latest)


def shape(*dims, kind=F32):
    return jax.ShapeDtypeStruct(dims, kind)


def call(kernel, ins, outs, scratch=(), space=pltpu.VMEM):
    size = sum(a.size * a.dtype.itemsize for a in (*ins, *outs))
    return pl.pallas_call(
        kernel,
        out_shape=outs,
        in_specs=[pl.BlockSpec(memory_space=space)] * len(ins),
        out_specs=[pl.BlockSpec(memory_space=pltpu.VMEM)] * len(outs),
        scratch_shapes=list(scratch),
        compiler_params=pltpu.CompilerParams(vmem_limit_bytes=16 * 1024 * 1024),
        cost_estimate=pl.CostEstimate(flops=0, bytes_accessed=size, transcendentals=0),
    )(*ins)


def shifted(array, axis, by):
    count = lax.axis_size(axis)
    return lax.ppermute(array, axis, [(i, (i + by) % count) for i in range(count)])


def exchange(array, axes):
    return lax.all_to_all(array, axes, 0, 0, tiled=True)


def body(velocity, viscosity, disp_init, rest_shape, compliance, stencil_weights, anchor, owners):
    flow = velocity.reshape(3, XY, SZ)
    thick = viscosity.reshape(XY, SZ)
    ins = (disp_init, rest_shape, compliance.reshape(1, SEG_DEV), stencil_weights, anchor, owners)
    msg, later, _, xlo, xhi = call(
        pack_kernel,
        tuple(pltpu.with_memory_space_constraint(a, pltpu.HBM) for a in (*ins, flow)),
        [shape(GROUP, EARLY), shape(56, SEG_DEV), shape(24, SEG_DEV), shape(3, SY, SZ), shape(3, SY, SZ)],
        [pltpu.VMEM(a.shape, a.dtype) for a in ins]
        + [pltpu.VMEM((EARLY, 128), F32), pltpu.SemaphoreType.DMA((8,))],
        pltpu.HBM,
    )
    static = exchange(msg, ("fx", "fz"))
    far_l = shifted(xhi, "fx", 1)
    far_u = shifted(xlo, "fx", -1)
    keep, give, place = call(
        pack_later_kernel,
        (later,),
        [shape(HALF, LATE), shape(HALF, LATE), shape(8, SEG_DEV)],
        [pltpu.VMEM((LATE, 128), F32)],
    )
    carried = (keep, shifted(give, "fz", 1))
    table_outs = [
        shape(XY, SLOTS),
        shape(SETS, 2 * SZ, SLOTS, kind=BF16),
        shape(2, SY, SLOTS),
        shape(32 * SETS, SLOTS),
    ]
    turned = [pltpu.VMEM((LATE, 128), F32)]
    sent, tabled = (), ()
    for t in range(3):
        n = 6 if t == 2 else 3
        faced = 7 if t == 2 else 3
        outs = [shape(n, XY, SZ), shape(faced, SX, SZ), shape(faced, SX, SZ)]
        planes = [shape(n, SY, SZ)] * 2
        kernel = functools.partial(spread_kernel, t)
        beside = functools.partial(sides_kernel, t)
        if t == 0:
            field, ylo, yhi, *tabled = call(kernel, (static, flow), outs + table_outs, turned)
            extra = []
            spare = [pltpu.VMEM(a.shape, a.dtype) for a in table_outs]
            wait_for, ins = (static,), ()
        else:
            outs.append(shape(24, SLOTS))
            if t == 2:
                outs.append(shape(8, 128))
            field, ylo, yhi, *extra = call(kernel, (flow, *sent, *tabled), outs)
            spare = []
            wait_for, ins = sent, tabled
        xl, xu = call(beside, (*wait_for, *ins), planes, [*spare, *turned] if t == 0 else ())
        yl = shifted(yhi, "cable", 1)
        yu = shifted(ylo, "cable", -1)
        beside_z = shifted(field, "fz", 1)
        if t == 2:
            across = shifted(extra[1], "cable", 2)
        ins = [thick, far_l, far_u, field, beside_z, xl, xu, yl, yu, *tabled[0:2], *extra]
        kernel = functools.partial(sample_kernel, t)
        if t < 2:
            if t == 0:
                ins += carried
            (msg,) = call(kernel, ins, [shape(HALF, 3 * SLOTS + (128 if t else 2 * LATE))])
            half = exchange(msg, "fx")
            if t == 0:
                static, before = half, ()
            sent = (half, shifted(half if t else half[:, : 3 * SLOTS], "fz", 1))
            tabled = call(functools.partial(prepare_kernel, t + 1, range(SETS)), (static, *before), table_outs, turned)
            before = sent
        else:
            ins.append(across)
            out, msg = call(kernel, ins, [shape(3, XY, SZ), shape(4 * GROUP, 128)], [pltpu.VMEM((128, 128), F32)])
    last = exchange(msg, ("cable", "fx", "fz"))
    (disp_next,) = call(finish_kernel, (last, place), [shape(3, SEG_DEV)])
    return disp_next, out.reshape(velocity.shape)


def solution(mesh):
    segments = ("cable", "fx", "fz")
    placed = (
        P(None, "fx", "cable", "fz"),
        P("fx", "cable", "fz"),
        P(None, segments),
        P(None, segments),
        P(segments),
        P(None, None, segments),
        P(None, segments),
        P(None, segments),
    )
    return jax.shard_map(
        body,
        mesh=mesh,
        in_specs=placed,
        out_specs=(P(None, segments), P(None, "fx", "cable", "fz")),
        check_vma=False,
    )
```

```python
import functools

import jax
import jax.numpy as jnp
from jax import lax
from jax.experimental import pallas as pl
from jax.experimental.pallas import tpu as pltpu
from jax.sharding import PartitionSpec as P


F32 = jnp.float32
BF16 = jnp.bfloat16
NT = (((1,), (1,)), ((), ()))
NN = (((1,), (0,)), ((), ()))

spread_gain = 16.0
drag_coeff = 0.05
relaxation = 0.5
ridge_share = 0.01

SEG_DEV = 64
GROUP = 64
CAP = 4
HALF = GROUP // 2
SLOTS = GROUP * CAP
SX, SY, SZ = 8, 16, 128
XY = SX * SY

R_W, R_CELL, R_D0, R_REST, R_CR, R_CODE = 0, 12, 13, 16, 19, 20
HEIGHT = (16, 24, 24)
SETS = 3
BASE = (0, 0, 288)
EARLY, LATE = 256, 640


def split(x):
    hi = x.astype(BF16)
    return hi, (x - hi.astype(F32)).astype(BF16)


def dot(a, b, dims):
    return lax.dot_general(a, b, dims, preferred_element_type=F32)


def iota(shape, dim):
    return lax.broadcasted_iota(jnp.int32, shape, dim)


def split3(x):
    hi, low = split(x)
    return hi, low, (x - hi.astype(F32) - low.astype(F32)).astype(BF16)


def rank_of(own):
    hot = (iota((GROUP, SEG_DEV), 0) == own).astype(F32)
    earlier = (iota((SEG_DEV, SEG_DEV), 0) < iota((SEG_DEV, SEG_DEV), 1)).astype(F32)
    return jnp.sum(hot * dot(hot, earlier, NN), axis=0, keepdims=True)


def put_slots(fields, rank, rows, turn, base):
    height = fields.shape[0]
    parts = split3(jnp.concatenate([jnp.where(rank == k, fields, 0.0) for k in range(CAP)], axis=0))
    dest = iota((GROUP, SEG_DEV), 0)
    hots = jnp.concatenate([(dest == row).astype(F32).astype(BF16) for row in rows], axis=0)
    got = dot(parts[0], hots, NT) + (dot(parts[1], hots, NT) + dot(parts[2], hots, NT))
    for j in range(SETS):
        start = base + CAP * height * j
        turn[start : start + CAP * height, 0:GROUP] = got[:, GROUP * j : GROUP * (j + 1)]


def pack_kernel(*refs):
    far, (msg, later, firsts, stay, leave), near, (turn, sems) = refs[0:7], refs[7:12], refs[12:18], refs[18:20]
    copies = [pltpu.make_async_copy(far[n], near[n], sems.at[n]) for n in (5, 4, 3, 0, 1, 2)]
    for n, face in enumerate((stay, leave)):
        start = pl.multiple_of((lax.axis_index("fz") ^ (1 - n)) * (XY - SY), SY)
        copies.append(pltpu.make_async_copy(far[6].at[:, pl.ds(start, SY), :], face, sems.at[6 + n]))
    for copy in copies:
        copy.start()
    disp, rest, comp, weights, anchor, owner = near
    fz_n, fx_n, cable_n = lax.axis_size("fz"), lax.axis_size("fx"), lax.axis_size("cable")
    device = (lax.axis_index("cable") * fx_n + lax.axis_index("fx")) * fz_n + lax.axis_index("fz")
    position = (device * SEG_DEV + iota((1, SEG_DEV), 1)).astype(F32)
    ramp = 1.0 + 2.0 * position / (SEG_DEV * fz_n * fx_n * cable_n)
    later[...] = jnp.zeros_like(later)
    firsts[...] = jnp.zeros_like(firsts)
    turn[...] = jnp.zeros_like(turn)
    for copy in copies:
        copy.wait()
    own = owner[0:1, :]
    rank = rank_of(own)
    firsts[0:12, :] = weights[0]
    firsts[R_CELL : R_CELL + 1, :] = anchor[0:1, :].astype(F32)
    firsts[R_D0 : R_D0 + 3, :] = disp[...]
    put_slots(firsts[0 : HEIGHT[0], :], rank, (own, own + fz_n, own - fz_n), turn, BASE[0])
    for n in range(EARLY // 128):
        msg[:, 128 * n : 128 * n + 128] = jnp.transpose(turn[128 * n : 128 * n + 128, :])[0:GROUP]
    for t in (1, 2):
        at = 24 * (t - 1)
        later[at : at + 12, :] = weights[t]
        later[at + R_CELL : at + R_CELL + 1, :] = anchor[t : t + 1, :].astype(F32)
        later[at + R_D0 : at + R_D0 + 3, :] = disp[...]
        later[at + R_REST : at + R_REST + 3, :] = rest[...]
        later[at + R_CR : at + R_CR + 1, :] = comp[...] * ramp
    later[48:51, :] = owner[...].astype(F32)
    later[51:52, :] = rank


def pack_later_kernel(later, keep, give, place, turn):
    mine = lax.axis_index("fz")
    turn[...] = jnp.zeros_like(turn)
    owners = [later[48 + t : 49 + t, :].astype(jnp.int32) for t in range(3)]
    ranks = [later[51:52, :], rank_of(owners[1]), rank_of(owners[2])]
    codes = [owners[t].astype(F32) * CAP + ranks[t] for t in range(2)]
    code = codes[0] + SLOTS * codes[1]
    for t in (1, 2):
        side, fx = (owners[t] & 1) ^ mine, owners[t] >> 1
        at = side * HALF + fx
        rows = (at, jnp.where(fx < HALF - 1, at + 1, -1), jnp.where(fx > 0, at - 1, -1))
        fields = later[24 * (t - 1) : 24 * t, :]
        fields = jnp.where(iota((24, SEG_DEV), 0) == R_CODE, code, fields)
        put_slots(fields, ranks[t], rows, turn, BASE[t])
    for n in range(LATE // 128):
        lanes = slice(128 * n, 128 * n + 128)
        block = jnp.transpose(turn[lanes, :])
        keep[:, lanes] = block[0:HALF]
        give[:, lanes] = block[HALF:GROUP]
    place[...] = jnp.zeros_like(place)
    place[0:1, :] = later[50:51, :]
    place[1:2, :] = ranks[2]


def turn_static(static, turned, t):
    first = BASE[t] // 128
    last = (BASE[t] + SETS * CAP * HEIGHT[t] + 127) // 128
    low = lax.axis_index("fz") == 0
    for n in range(first, last):
        if t == 0:
            spare = LATE - GROUP
            turned[spare:LATE, :] = static[:, 128 * n : 128 * n + 128]
            homes = [turned[pl.ds(spare + f, HALF, stride=2), :] for f in range(2)]
        else:
            at = 3 * SLOTS + 128 * n
            same, other = static[:, at : at + 128], static[:, at + LATE : at + LATE + 128]
            homes = [jnp.where(low, same, other), jnp.where(low, other, same)]
        wide = jnp.concatenate([*homes, jnp.zeros((128 - GROUP, 128), F32)], axis=0)
        turned[128 * n : 128 * n + 128, :] = jnp.transpose(wide)


def slot_rows(turned, t, j):
    height = HEIGHT[t]
    start = BASE[t] + CAP * height * j
    part = [turned[start + height * k : start + height * (k + 1), :] for k in range(CAP)]
    halves = [part[2 * n] + pltpu.roll(part[2 * n + 1], 64, 1) for n in range(2)]
    return jnp.concatenate(halves, axis=1)


def along(rows, first, at):
    total = jnp.zeros(at.shape, F32)
    for i in range(4):
        total = jnp.where(at == i, rows[first + i : first + i + 1], total)
    return total


def tables(rows, plane=None):
    cell = rows[R_CELL : R_CELL + 1].astype(jnp.int32)
    wy = along(rows, R_W + 4, iota((SY, SLOTS), 0) - ((cell >> 7) & (SY - 1)))
    wz = along(rows, R_W + 8, iota((SZ, SLOTS), 0) - (cell & (SZ - 1)))
    if plane is not None:
        return along(rows, R_W, plane - (cell >> 11)) * wy, wz
    wx = along(rows, R_W, iota((SX, SLOTS), 0) - (cell >> 11))
    return jnp.concatenate([wx[x : x + 1] * wy for x in range(SX)], axis=0), wz


def spread(wxy, wz2, base):
    hi, low = split(jnp.concatenate([wxy * (spread_gain * base[c]) for c in range(3)], axis=0))
    both = dot(hi, wz2, NT)
    return both[:, :SZ] + (both[:, SZ:] + dot(low, wz2[0:SZ], NT))


def look_up(halves, code):
    low_half = iota((1, 128), 1) < 64
    mine = lax.axis_index("fz")
    height = HALF
    label = (iota((height, SLOTS), 0) * 2 + mine) * CAP + iota((height, SLOTS), 1) // 64
    labels = (label, label + CAP * (1 - 2 * mine))
    found = [[None] * 2 for _ in range(3)]
    for part in range(2):
        piece = code[:, 128 * part : 128 * part + 128]
        turned = pltpu.roll(piece, 64, 1)
        pair = []
        for odd in range(2):
            both = jnp.where(low_half, turned, piece) if odd else jnp.where(low_half, piece, turned)
            wanted = jnp.concatenate([both, both], axis=1)
            per = []
            for comp in range(3):
                lanes = slice(comp * SLOTS, (comp + 1) * SLOTS)
                hit = jnp.where(labels[0] == wanted, halves[0][:, lanes], 0.0)
                hit = hit + jnp.where(labels[1] == wanted, halves[1][:, lanes], 0.0)
                hit = jnp.sum(hit, axis=0, keepdims=True)
                hit = hit[:, :128] + hit[:, 128:]
                per.append(hit + pltpu.roll(hit, 64, 1))
            pair.append(per)
        for comp in range(3):
            found[comp][part] = jnp.where(low_half, pair[0][comp], pair[1][comp])
    return [jnp.concatenate(found[comp], axis=1) for comp in range(3)]


def responses(rows, sampled):
    cr = rows[R_CR : R_CR + 1]
    return [rows[R_REST + c : R_REST + c + 1] + cr * sampled[c] for c in range(3)]


def prepare_kernel(t, sets, *refs):
    static, sent, (wxy_out, wz_out, plane_out, slots, turned) = refs[0], refs[1:-5], refs[-5:]
    turn_static(static, turned, t)
    for j in sets:
        rows = slot_rows(turned, t, j)
        wxy, wz = tables(rows, (None, SX - 1, 0)[j])
        hi, low = split(wz)
        wz_out[j, 0:SZ, :] = hi
        wz_out[j, SZ:, :] = low
        if j == 0:
            wxy_out[...] = wxy
        else:
            plane_out[j - 1] = wxy
        slots[32 * j : 32 * j + HEIGHT[t], :] = rows
        if t == 2:
            code = rows[R_CODE : R_CODE + 1].astype(jnp.int32)
            before = responses(rows, look_up(sent, code & (SLOTS - 1)))
            for c in range(3):
                slots[32 * j + 24 + c : 32 * j + 25 + c, :] = before[c]


def displacements(t, rows, sent):
    first = [rows[R_D0 + c : R_D0 + c + 1] for c in range(3)]
    if t == 0:
        return [first], []
    code = rows[R_CODE : R_CODE + 1].astype(jnp.int32)
    if t == 1:
        before = responses(rows, look_up(sent, code & (SLOTS - 1)))
    else:
        before = [rows[24 + c : 25 + c] for c in range(3)]
    gap = [before[c] - first[c] for c in range(3)]
    second = [first[c] + relaxation * gap[c] for c in range(3)]
    if t == 1:
        return [second], [second, gap]
    latest = responses(rows, look_up(sent, code >> 8))
    change = [latest[c] - before[c] for c in range(3)]
    return [latest, change], [latest, change, gap, [latest[c] - second[c] for c in range(3)], before]


def spread_kernel(t, *refs):
    if t == 0:
        static, velocity = refs[0:2]
        sent = ()
        field, ylo, yhi, *tabled, turned = refs[2:]
        prepare_kernel(0, (0,), static, *tabled, turned)
    else:
        velocity, sent, tabled = refs[0], refs[1:3], refs[3:7]
        field, ylo, yhi, aux = refs[7:11]
        aux[...] = jnp.zeros_like(aux)
    wxy, wz, _, slots = tabled
    rows = slots[0:32, :]
    bases, kept = displacements(t, rows, sent)
    for n, base in enumerate(bases):
        forced = spread(wxy[...], wz[0], base)
        for c in range(3):
            part = forced[XY * c : XY * (c + 1)]
            field[3 * n + c] = part + velocity[c] if n == 0 else part
    if t > 0:
        for n, group in enumerate(kept):
            for c in range(3):
                aux[3 * n + c : 3 * n + c + 1, :] = group[c]
        aux[16:20, :] = rows[R_REST : R_REST + 4]
    for n in range(3 * len(bases)):
        ylo[n] = field[n, pl.ds(0, SX, stride=SY), :]
        yhi[n] = field[n, pl.ds(SY - 1, SX, stride=SY), :]
    if t == 2:
        lanes = slice(3 * SLOTS, 3 * SLOTS + 128)
        total = jnp.sum(sent[0][:, lanes] + sent[1][:, lanes], axis=0, keepdims=True)
        total = jnp.broadcast_to(total, (8, 128))
        ylo[6] = total
        yhi[6] = total
        refs[11][...] = total


def sides_kernel(t, *refs):
    if t == 0:
        (static, *outs), tabled, turned = refs[0:3], refs[3:7], refs[7]
        sent = ()
        prepare_kernel(0, (1, 2), static, *tabled, turned)
    else:
        sent, tabled, outs = refs[0:2], refs[2:6], refs[6:8]
    _, wz, plane, slots = tabled
    for j, out in enumerate(outs):
        bases, _ = displacements(t, slots[32 * j + 32 : 32 * j + 64, :], sent)
        for n, base in enumerate(bases):
            forced = spread(plane[j], wz[j + 1], base)
            for c in range(3):
                out[3 * n + c] = forced[SY * c : SY * (c + 1)]


def wake(u, beside_z, xl, xu, yl, yu, viscosity):
    lane = iota((XY, SZ), 1)
    y = iota((XY, SZ), 0) % SY
    upper_core = lax.axis_index("fz") > 0
    speed = jnp.sqrt(1.0 + (u[0] * u[0] + u[1] * u[1] + u[2] * u[2]))
    new = []
    for c in range(3):
        here = u[c]
        near = jnp.concatenate([xl[c], here[: XY - SY]], axis=0)
        near = near + jnp.concatenate([here[SY:], xu[c]], axis=0)
        wide_l = jnp.concatenate([jnp.broadcast_to(yl[c][x : x + 1], (SY, SZ)) for x in range(SX)], axis=0)
        wide_u = jnp.concatenate([jnp.broadcast_to(yu[c][x : x + 1], (SY, SZ)) for x in range(SX)], axis=0)
        near = near + jnp.where(y == 0, wide_l, pltpu.roll(here, 1, 0))
        near = near + jnp.where(y == SY - 1, wide_u, pltpu.roll(here, XY - 1, 0))
        left = jnp.where(upper_core, beside_z[c], 0.0)
        right = jnp.where(upper_core, 0.0, beside_z[c])
        near = near + pltpu.roll(jnp.where(lane == SZ - 1, left, here), 1, 1)
        near = near + pltpu.roll(jnp.where(lane == 0, right, here), SZ - 1, 1)
        new.append(here + viscosity * (near - 6.0 * here) - drag_coeff * here * speed)
    return new


def sample(new, wxy, wz2):
    wz_hi, wz_low = wz2[0:SZ], wz2[SZ:]
    both = jnp.concatenate([wz_hi, wz_hi], axis=0)
    sampled = []
    for c in range(3):
        hi, low = split(new[c])
        along_z = dot(jnp.concatenate([hi, low], axis=1), both, NN) + dot(hi, wz_low, NN)
        sampled.append(jnp.sum(wxy * along_z, axis=0, keepdims=True))
    return sampled


def product(a, b):
    rows = a[0] * b[0] + a[1] * b[1] + a[2] * b[2]
    return rows[:, :128] + rows[:, 128:]


def lane_of(row, n):
    return jnp.sum(jnp.where(iota(row.shape, 1) == n, row, 0.0), axis=1, keepdims=True)


def sample_kernel(t, *refs):
    viscosity, moved, other = refs[0:3]
    refs = refs[2:]
    field, beside_z, xl, xu, yl, yu, wxy, wz = refs[1:9]
    fx = lax.axis_index("fx")
    me = lax.axis_index("cable")
    last = lax.axis_size("cable") - 1

    def whole(ref):
        if t < 2:
            return [ref[c] for c in range(3)]
        return [ref[c] + coef * ref[3 + c] for c in range(3)]

    if t == 2:
        gram = yl[6] + yu[6] + (refs[10][...] + refs[11][...])
        first = iota((1, 128), 1) < 64
        square = jnp.sum(jnp.where(first, gram[0:1], 0.0), axis=1, keepdims=True)
        target = jnp.sum(jnp.where(first, 0.0, gram[0:1]), axis=1, keepdims=True)
        coef = -target / (square + (ridge_share * square + 1e-06))
    u = whole(field)
    below = [jnp.where(me > 0, face, 0.0) for face in whole(yl)]
    above = [jnp.where(me < last, face, 0.0) for face in whole(yu)]
    first = lax.axis_index("fz") == 0
    before, after = whole(xl), whole(xu)
    for c in range(3):
        far_l, far_u = jnp.where(first, moved[c], other[c]), jnp.where(first, other[c], moved[c])
        before[c] = before[c] + jnp.where(fx > 0, far_l, 0.0)
        after[c] = after[c] + jnp.where(fx < lax.axis_size("fx") - 1, far_u, 0.0)
    faces = [before, after, below, above]
    new = wake(u, whole(beside_z), *faces, viscosity[...])
    sampled = sample(new, wxy[...], wz[0])
    if t == 0:
        keep, got, msg = refs[9:12]
        for c in range(3):
            msg[:, SLOTS * c : SLOTS * (c + 1)] = jnp.broadcast_to(sampled[c], (HALF, SLOTS))
        msg[:, 3 * SLOTS : 3 * SLOTS + LATE] = keep[...]
        msg[:, 3 * SLOTS + LATE :] = got[...]
        return
    aux = refs[9]

    def kept(n):
        return [aux[3 * n + c : 3 * n + c + 1, :] for c in range(3)]

    cr = aux[19:20, :]
    response = [aux[16 + c : 17 + c, :] + cr * sampled[c] for c in range(3)]
    if t == 1:
        msg = refs[10]
        disp, gap0 = kept(0), kept(1)
        gap = [response[c] - disp[c] for c in range(3)]
        v0 = [gap[c] - gap0[c] for c in range(3)]
        for c in range(3):
            msg[:, SLOTS * c : SLOTS * (c + 1)] = jnp.broadcast_to(sampled[c], (HALF, SLOTS))
        square, target = product(v0, v0), product(v0, gap)
        square, target = (part + pltpu.roll(part, 64, 1) for part in (square, target))
        row = jnp.where(iota((1, 128), 1) < 64, square, target)
        msg[:, 3 * SLOTS : 3 * SLOTS + 128] = jnp.broadcast_to(row, (HALF, 128))
        return
    out, msg, turn = refs[12:15]
    for c in range(3):
        out[c] = new[c]
    latest, change, gap0, gap1, before = (kept(n) for n in range(5))
    disp = [latest[c] + coef * change[c] for c in range(3)]
    gap = [response[c] - disp[c] for c in range(3)]
    v0 = [gap[c] - gap0[c] for c in range(3)]
    v1 = [gap[c] - gap1[c] for c in range(3)]
    turn[...] = jnp.zeros_like(turn)
    for n, group in enumerate((response, before, latest)):
        for c in range(3):
            turn[3 * n + c : 3 * n + c + 1, :] = group[c][:, :128]
            turn[32 + 3 * n + c : 33 + 3 * n + c, :] = group[c][:, 128:]
    for n, (a, b) in enumerate(((v0, v0), (v0, v1), (v1, v1), (v0, gap), (v1, gap))):
        turn[64 + n : 65 + n, :] = product(a, b)
    turned = jnp.transpose(turn[...])
    row = jnp.sum(turned, axis=0, keepdims=True)
    block = turned[0:64] + pltpu.roll(turned[64:128], 16, 1)
    block = jnp.where(iota((1, 128), 1) < 64, block, row)
    for c in range(4):
        for f in range(2):
            msg[pl.ds(GROUP * c + f, HALF, stride=2), :] = block[HALF * f : HALF * (f + 1)]


def finish_kernel(sent, place, out):
    row = jnp.sum(sent[...], axis=0, keepdims=True)
    g00, g01, g11, b0, b1 = (lane_of(row, 64 + n) for n in range(5))
    shift = ridge_share * (g00 + g11) / 2 + 1e-06
    first, second = g00 + shift, g11 + shift
    determinant = first * second - g01 * g01
    c0 = -(second * b0 - g01 * b1) / determinant
    c1 = -(first * b1 - g01 * b0) / determinant
    start = pl.multiple_of(lax.axis_index("cable") * GROUP, GROUP)
    mine = sent[pl.ds(start, GROUP), :]
    turned = jnp.transpose(jnp.concatenate([mine, jnp.zeros((128 - GROUP, 128), F32)], axis=0))
    hot = (iota((128, SEG_DEV), 0).astype(F32) == place[0:1, :]).astype(F32).astype(BF16)
    parts = split3(turned[0:64])
    got = dot(parts[0], hot, NN) + (dot(parts[1], hot, NN) + dot(parts[2], hot, NN))
    rank = place[1:2, :]
    rows = jnp.zeros((16, SEG_DEV), F32)
    for k in range(CAP):
        rows = jnp.where(rank == k, got[16 * k : 16 * k + 16], rows)
    response, before, latest = rows[0:3], rows[3:6], rows[6:9]
    out[...] = response + c0 * (response - before) + c1 * (response - latest)


def shape(*dims, kind=F32):
    return jax.ShapeDtypeStruct(dims, kind)


def call(kernel, ins, outs, scratch=(), space=pltpu.VMEM):
    size = sum(a.size * a.dtype.itemsize for a in (*ins, *outs))
    return pl.pallas_call(
        kernel,
        out_shape=outs,
        in_specs=[pl.BlockSpec(memory_space=space)] * len(ins),
        out_specs=[pl.BlockSpec(memory_space=pltpu.VMEM)] * len(outs),
        scratch_shapes=list(scratch),
        compiler_params=pltpu.CompilerParams(vmem_limit_bytes=16 * 1024 * 1024),
        cost_estimate=pl.CostEstimate(flops=0, bytes_accessed=size, transcendentals=0),
    )(*ins)


def shifted(array, axis, by):
    count = lax.axis_size(axis)
    return lax.ppermute(array, axis, [(i, (i + by) % count) for i in range(count)])


def exchange(array, axes):
    return lax.all_to_all(array, axes, 0, 0, tiled=True)


def body(velocity, viscosity, disp_init, rest_shape, compliance, stencil_weights, anchor, owners):
    flow = velocity.reshape(3, XY, SZ)
    thick = viscosity.reshape(XY, SZ)
    ins = (disp_init, rest_shape, compliance.reshape(1, SEG_DEV), stencil_weights, anchor, owners)
    msg, later, _, stay, leave = call(
        pack_kernel,
        tuple(pltpu.with_memory_space_constraint(a, pltpu.HBM) for a in (*ins, flow)),
        [shape(GROUP, EARLY), shape(56, SEG_DEV), shape(24, SEG_DEV), shape(3, SY, SZ), shape(3, SY, SZ)],
        [pltpu.VMEM(a.shape, a.dtype) for a in ins]
        + [pltpu.VMEM((EARLY, 128), F32), pltpu.SemaphoreType.DMA((8,))],
        pltpu.HBM,
    )
    static = exchange(msg, ("fx", "fz"))
    both = jnp.concatenate([stay, shifted(leave, "fz", 1)], axis=0)
    fx_n = lax.axis_size("fx")
    moves = [(2 * i + f, 2 * ((i + 1 - 2 * f) % fx_n) + f) for i in range(fx_n) for f in range(2)]
    moved = lax.ppermute(both, ("fx", "fz"), moves)
    other = shifted(moved[3:6], "fz", 1)
    keep, give, place = call(
        pack_later_kernel,
        (later,),
        [shape(HALF, LATE), shape(HALF, LATE), shape(8, SEG_DEV)],
        [pltpu.VMEM((LATE, 128), F32)],
    )
    carried = (keep, shifted(give, "fz", 1))
    table_outs = [
        shape(XY, SLOTS),
        shape(SETS, 2 * SZ, SLOTS, kind=BF16),
        shape(2, SY, SLOTS),
        shape(32 * SETS, SLOTS),
    ]
    turned = [pltpu.VMEM((LATE, 128), F32)]
    sent, tabled = (), ()
    for t in range(3):
        n = 6 if t == 2 else 3
        faced = 7 if t == 2 else 3
        outs = [shape(n, XY, SZ), shape(faced, SX, SZ), shape(faced, SX, SZ)]
        planes = [shape(n, SY, SZ)] * 2
        kernel = functools.partial(spread_kernel, t)
        beside = functools.partial(sides_kernel, t)
        if t == 0:
            field, ylo, yhi, *tabled = call(kernel, (static, flow), outs + table_outs, turned)
            extra = []
            spare = [pltpu.VMEM(a.shape, a.dtype) for a in table_outs]
            wait_for, ins = (static,), ()
        else:
            outs.append(shape(24, SLOTS))
            if t == 2:
                outs.append(shape(8, 128))
            field, ylo, yhi, *extra = call(kernel, (flow, *sent, *tabled), outs)
            spare = []
            wait_for, ins = sent, tabled
        xl, xu = call(beside, (*wait_for, *ins), planes, [*spare, *turned] if t == 0 else ())
        yl = shifted(yhi, "cable", 1)
        yu = shifted(ylo, "cable", -1)
        beside_z = shifted(field, "fz", 1)
        if t == 2:
            across = shifted(extra[1], "cable", 2)
        ins = [thick, moved, other, field, beside_z, xl, xu, yl, yu, *tabled[0:2], *extra]
        kernel = functools.partial(sample_kernel, t)
        if t < 2:
            if t == 0:
                ins += carried
            (msg,) = call(kernel, ins, [shape(HALF, 3 * SLOTS + (128 if t else 2 * LATE))])
            half = exchange(msg, "fx")
            if t == 0:
                static, before = half, ()
            sent = (half, shifted(half if t else half[:, : 3 * SLOTS], "fz", 1))
            tabled = call(functools.partial(prepare_kernel, t + 1, range(SETS)), (static, *before), table_outs, turned)
            before = sent
        else:
            ins.append(across)
            out, msg = call(kernel, ins, [shape(3, XY, SZ), shape(4 * GROUP, 128)], [pltpu.VMEM((128, 128), F32)])
    last = exchange(msg, ("cable", "fx", "fz"))
    (disp_next,) = call(finish_kernel, (last, place), [shape(3, SEG_DEV)])
    return disp_next, out.reshape(velocity.shape)


def solution(mesh):
    segments = ("cable", "fx", "fz")
    placed = (
        P(None, "fx", "cable", "fz"),
        P("fx", "cable", "fz"),
        P(None, segments),
        P(None, segments),
        P(segments),
        P(None, None, segments),
        P(None, segments),
        P(None, segments),
    )
    return jax.shard_map(
        body,
        mesh=mesh,
        in_specs=placed,
        out_specs=(P(None, segments), P(None, "fx", "cable", "fz")),
        check_vma=False,
    )
```
